32 devices in a mesh: dp: 8 (over z, y), tensor: 4 (over x, core).
Axes of the slice: x: 2, y: 2, z: 4, core: 2. Of those that a mesh axis runs over, the one named last changes fastest.
Arguments:
- tokens: bfloat16 [16, 1024, 768], P('dp', 'tensor'), may hold values from -6 to 6
- lengths: int32 [16], P('dp'), may hold values from 256 to 1024, as said below
- mem_mask: int32 [16, 2, 2], P('dp'), may hold values 0 or 1
- cotangent: bfloat16 [16, 1024, 768], P('dp', 'tensor'), may hold values from -6 to 6
- w_qkv: bfloat16 [3, 768, 768], P(None, 'dp', 'tensor'), may hold values from -0.21875 to 0.21875
- w_gauss: bfloat16 [2, 12, 64], P(None, 'tensor', 'dp'), may hold values from -0.75 to 0.75
- w_out: bfloat16 [768, 768], P('tensor', 'dp'), may hold values from -0.625 to 0.625
- ln_gain: float32 [768], P(('dp', 'tensor')), may hold values from 0.5 to 1.5
- ln_bias: float32 [768], P(('dp', 'tensor')), may hold values from -1.5 to 1.5
- w_up: bfloat16 [768, 3072], P('dp', 'tensor'), may hold values from -0.21875 to 0.21875
- w_down: bfloat16 [3072, 768], P('tensor', 'dp'), may hold values from -0.109375 to 0.109375
Outputs:
- output: float32 [16, 1024, 768], P('dp', 'tensor')
- grad_tokens: float32 [16, 1024, 768], P('dp', 'tensor')
- grad_qkv: float32 [3, 768, 768], P(None, 'dp', 'tensor')
- grad_gauss: float32 [2, 12, 64], P(None, 'tensor', 'dp')
- grad_out: float32 [768, 768], P('tensor', 'dp')
- grad_gain: float32 [768], P(('dp', 'tensor'))
- grad_bias: float32 [768], P(('dp', 'tensor'))
- grad_up: float32 [768, 3072], P('dp', 'tensor')
- grad_down: float32 [3072, 768], P('tensor', 'dp')
The draws below stay inside these ranges and needn't reach their ends.
Inputs may be any that keep to these rules, and one draw needn't show every extreme that they name: `lengths`: sequence 0 uses all 1024 slots.
All inputs are finite; a program needn't handle non-finite values. No bound on the sum of `mem_mask` on one device may be relied on, other than what follows from the above.
Results may differ from the reference program's by a relative error of at most 0.014.
The reference program's roundings to bfloat16 on the way count: a program that leaves them out, or rounds other values in their place, can miss the bound.
Values may be sent and summed in bfloat16 or wider, within the bound.
No kernel may reach another device: no remote copies, remote signals or barrier semaphores. Data moves between devices by JAX's collectives and lax.ppermute only.
A program may use at most 192 MiB of HBM per device.

```python
import jax
import jax.numpy as jnp
from jax import lax

D = 768
H = 12
DH = 64
FF = 3072
NB = 256
SEGL = 512
SEQ = 1024
SEGS = 2
SEQS = 16


def draw_lengths(key, part):
    drawn = jax.random.randint(key, (SEQS,), SEQ // 4, SEQ + 1)
    return drawn.at[0].set(SEQ)


def draw_tokens(key, part):
    drawn = jnp.clip(jax.random.normal(key, (SEQS, SEQ, D), jnp.float32), -6.0, 6.0)
    return drawn.astype(jnp.bfloat16)


def plant(entries, own_key, least, largest):
    spot = [jax.random.randint(jax.random.fold_in(own_key, axis), (), 0, length) for axis, length in enumerate(entries.shape)]
    widest = entries.shape.index(max(entries.shape))
    beside = spot[:widest] + [(spot[widest] + 1) % entries.shape[widest]] + spot[widest + 1:]
    return entries.at[tuple(spot)].set(least).at[tuple(beside)].set(largest)


def shard_levels(key, shape, shards, low, high):
    level, own = 1.0, jax.random.fold_in(key, 6)
    for axis_at, blocks in shards:
        steps = jnp.exp(jax.random.uniform(jax.random.fold_in(own, axis_at), (blocks,), jnp.float32, low / len(shards), high / len(shards)))
        level = level * jnp.repeat(steps, shape[axis_at] // blocks).reshape([-1 if axis == axis_at else 1 for axis in range(len(shape))])
    return level


def bell_draw(own_key, shape, spread, limit, pieces=(), kind=jnp.bfloat16):
    loudness = shard_levels(own_key, shape, pieces, -0.22, 0.18) if pieces else 1.0
    values = jax.random.normal(own_key, shape, jnp.float32) * spread * loudness
    return jnp.minimum(jnp.maximum(values, -limit), limit).astype(kind)


def setup_inputs(seed: int = 0) -> dict:
    splits = jax.random.split(jax.random.key(seed), 12)
    return {
        "tokens": draw_tokens(jax.random.fold_in(splits[11], 71), 0),
        "lengths": draw_lengths(jax.random.fold_in(splits[11], 71), 0),
        "mem_mask": plant((jax.random.randint(splits[2], (SEQS, SEGS, SEGS), 0, 4) < 3).astype(jnp.int32), jax.random.fold_in(splits[2], 1), 0, 1),
        "cotangent": bell_draw(splits[3], (SEQS, SEQ, D), 1.0, 6.0, ((0, 8), (1, 4))),
        "w_qkv": bell_draw(splits[4], (3, D, D), D ** -0.5, 0.21875, ((1, 8), (2, 4))),
        "w_gauss": bell_draw(splits[5], (2, H, DH), DH ** -0.5, 0.75, ((1, 4), (2, 8))),
        "w_out": bell_draw(splits[6], (D, D), (D // 8) ** -0.5, 0.625, ((0, 4), (1, 8))),
        "ln_gain": jnp.clip(1.0 + 0.1 * jax.random.normal(splits[7], (D,), jnp.float32), 0.5, 1.5),
        "ln_bias": bell_draw(splits[8], (D,), 0.3, 1.5, ((0, 32),), jnp.float32),
        "w_up": bell_draw(splits[9], (D, FF), D ** -0.5, 0.21875, ((0, 8), (1, 4))),
        "w_down": bell_draw(splits[10], (FF, D), FF ** -0.5, 0.109375, ((0, 4), (1, 8))),
    }


highest = lax.Precision.HIGHEST

@jax.custom_vjp
def low(v):
    return lax.optimization_barrier(v.astype(jnp.bfloat16)).astype(jnp.float32)

@jax.custom_vjp
def low_back(v):
    return v

def low_keep(v):
    return (low(v), None)

def low_pass(kept, grad):
    return (grad,)

def back_keep(v):
    return (v, None)

def back_low(kept, grad):
    return (low(grad),)
low.defvjp(low_keep, low_pass)
low_back.defvjp(back_keep, back_low)

def round_both(value):
    return low_back(low(value))

def ridge_matrix(basis_count, sample_count):
    centres = (jnp.arange(basis_count, dtype=jnp.float32) + 0.5) / basis_count
    samples = (jnp.arange(sample_count, dtype=jnp.float32) + 0.5) / sample_count
    spacing = 1.0 / basis_count
    basis_rows = jnp.exp(-0.5 * ((samples[None, :] - centres[:, None]) / spacing) ** 2)
    gram_matrix = jnp.dot(basis_rows, basis_rows.T, precision=highest) + 0.5 * jnp.eye(basis_count, dtype=jnp.float32)
    factor = jnp.linalg.cholesky(gram_matrix)
    forward_solve = lax.linalg.triangular_solve(factor, basis_rows, left_side=True, lower=True)
    return lax.linalg.triangular_solve(factor, forward_solve, left_side=True, lower=True, transpose_a=True)

def memory_pairs(visible):
    segment_ids = jnp.arange(visible.shape[0])
    return jnp.where(segment_ids[None, :] < segment_ids[:, None], visible.astype(jnp.float32), 0.0)

def mixer(inputs, validity, pairing, w_query, w_key, w_value, gaussian, ridge_fit):
    point_count = inputs.shape[0]
    blocks = point_count // SEGL
    head_count = w_query.shape[1] // DH
    basis_count = ridge_fit.shape[0]
    queries = round_both(jnp.dot(inputs, w_query, precision=highest))
    key_proj = round_both(jnp.dot(inputs, w_key, precision=highest))
    values = round_both(jnp.dot(inputs, w_value, precision=highest))
    query_heads = queries.reshape(blocks, SEGL, head_count, DH)
    key_heads = key_proj.reshape(blocks, SEGL, head_count, DH)
    value_heads = values.reshape(blocks, SEGL, head_count, DH)
    live_keys = validity.reshape(blocks, SEGL)
    scores = low_back(jnp.einsum('bqhd,bkhd->bhqk', query_heads, key_heads, precision=highest) * DH ** (-0.5))
    positions = jnp.arange(SEGL)
    causal = positions[None, :] <= positions[:, None]
    diagonal = positions[None, :] == positions[:, None]
    allowed = causal[None, None] & ((live_keys[:, None, None, :] > 0.5) | diagonal[None, None])
    scores = jnp.where(allowed, scores, -1e+30)
    row_max = lax.optimization_barrier(jnp.max(scores, axis=-1, keepdims=True))
    exponent = jnp.exp(scores - row_max)
    softmax_out = low(exponent / lax.optimization_barrier(jnp.sum(exponent, axis=-1, keepdims=True)))
    attended = jnp.einsum('bhqk,bkhd->bqhd', softmax_out, value_heads, precision=highest)
    mean_logit = jnp.einsum('bqhd,hd->bqh', query_heads, gaussian[0], precision=highest)
    var_logit = jnp.einsum('bqhd,hd->bqh', query_heads, gaussian[1], precision=highest)
    basis_var = (1.0 / basis_count) ** 2
    centre_pos = jax.nn.sigmoid(mean_logit)
    spread_sq = 0.05 * jax.nn.softplus(var_logit) + basis_var
    centres = (jnp.arange(basis_count, dtype=jnp.float32) + 0.5) / basis_count
    density = low(jnp.sqrt(basis_var / spread_sq)[..., None] * jnp.exp(-0.5 * (centre_pos[..., None] - centres) ** 2 / spread_sq[..., None]))
    masked = (values * validity[:, None]).reshape(blocks, SEGL, head_count * DH)
    counts = jnp.maximum(lax.optimization_barrier(jnp.sum(pairing, axis=1)), 1.0)
    pooled = low(jnp.einsum('sj,jpc->spc', pairing, masked, precision=highest) / counts[:, None, None])
    memory_coef = round_both(jnp.einsum('np,spc->snc', ridge_fit, pooled, precision=highest)).reshape(blocks, basis_count, head_count, DH)
    recalled = jnp.einsum('bqhn,bnhd->bqhd', density, memory_coef, precision=highest)
    return round_both((attended + recalled).reshape(point_count, head_count * DH))

def layer_norm(residual, norm_gain, norm_bias):
    centred = residual - lax.optimization_barrier(jnp.mean(residual, axis=-1, keepdims=True))
    return centred * lax.rsqrt(lax.optimization_barrier(jnp.mean(centred * centred, axis=-1, keepdims=True)) + 1e-05) * norm_gain + norm_bias

def feed_forward(normed, weight_up, weight_down):
    pre = low_back(jnp.dot(normed, weight_up, precision=highest))
    hidden = round_both(jax.nn.gelu(pre, approximate=True))
    return jnp.dot(hidden, weight_down, precision=highest)

def reference(tokens, lengths, mem_mask, cotangent, w_qkv, w_gauss, w_out, ln_gain, ln_bias, w_up, w_down):
    positions = jnp.arange(SEQ)
    validity = (positions[None, :] < lengths[:, None]).astype(jnp.float32)
    pairings = jax.vmap(memory_pairs)(mem_mask)

    def forward(inputs_all, weight_qkv, gaussian, weight_out, norm_gain, norm_bias, weight_up, weight_down):
        ridge_fit = low(ridge_matrix(NB, SEGL))

        def sequence_fn(inputs, valid_row, pairing):
            heads_out = mixer(inputs, valid_row, pairing, weight_qkv[0], weight_qkv[1], weight_qkv[2], gaussian, ridge_fit)
            residual = inputs + low_back(jnp.dot(heads_out, weight_out, precision=highest))
            normed = round_both(layer_norm(residual, norm_gain, norm_bias))
            return residual + feed_forward(normed, weight_up, weight_down)
        checked = jax.checkpoint(sequence_fn)
        return lax.map(lambda entry: checked(entry[0], entry[1], entry[2]), (inputs_all, validity, pairings))
    floats = tuple((array.astype(jnp.float32) for array in (tokens, w_qkv, w_gauss, w_out, ln_gain, ln_bias, w_up, w_down)))
    output, pullback = jax.vjp(forward, *floats)
    gradients = pullback(cotangent.astype(jnp.float32) * validity[:, :, None])
    return (output, gradients[0], gradients[1], gradients[2], gradients[3], gradients[4], gradients[5], gradients[6], gradients[7])
```

```python
import jax
import jax.numpy as jnp
import numpy as np
from jax import lax
from jax.sharding import PartitionSpec as P

D = 768
H = 12
DH = 64
NB = 256
SEGL = 512
AXES = ("dp", "tensor")
F32 = jnp.float32
BF16 = jnp.bfloat16


def ridge_matrix():
    centres = (np.arange(NB) + 0.5) / NB
    samples = (np.arange(SEGL) + 0.5) / SEGL
    rows = np.exp(-0.5 * ((samples[None, :] - centres[:, None]) * NB) ** 2)
    gram = rows @ rows.T + 0.5 * np.eye(NB)
    return np.linalg.solve(gram, rows).astype(np.float32).astype(jnp.bfloat16)


def xor_permute(value, dp_mask, tensor_mask):
    dp_count, rank_count = lax.axis_size("dp"), lax.axis_size("tensor")
    pairs = [
        (d * rank_count + t, (d ^ dp_mask) * rank_count + (t ^ tensor_mask))
        for d in range(dp_count)
        for t in range(rank_count)
    ]
    return lax.ppermute(value, AXES, pairs)


MASKS = {"c": (0, 1), "x": (0, 2), "y": (1, 0)}


def gather_pieces(piece, order):
    arrays = {(): piece[None]}
    value = piece
    stacked = value
    keys = [dict(c=0, x=0, y=0, z=0)]
    for letter in order:
        if letter == "z":
            parts = [stacked] + [xor_permute(stacked, 2 * k, 0) for k in (1, 2, 3)]
        else:
            parts = [stacked, xor_permute(stacked, *MASKS[letter])]
        keys = [dict(key, **{letter: k}) for k in range(len(parts)) for key in keys]
        stacked = jnp.stack(parts).reshape((-1,) + piece.shape)
    return stacked, [(k["z"] * 2 + k["y"]) * 4 + k["x"] * 2 + k["c"] for k in keys]


def gather_all(piece, order):
    if lax.axis_size("dp") != 8:
        return lax.all_gather(piece, AXES, axis=0)
    stacked, flat = gather_pieces(piece, order)
    me = lax.axis_index("dp") * 4 + lax.axis_index("tensor")
    position = np.argsort(np.array(flat))
    return jnp.take(stacked, jnp.asarray(position)[jnp.arange(32) ^ me], axis=0)


def scatter_all(parts, order):
    if lax.axis_size("dp") != 8:
        return lax.psum_scatter(parts, AXES, scatter_dimension=0)
    me = lax.axis_index("dp") * 4 + lax.axis_index("tensor")
    value = jnp.take(parts.astype(BF16), jnp.arange(32) ^ me, axis=0)
    value = value.reshape((4, 2, 2, 2) + parts.shape[1:])
    axes = "zyxc"
    for letter in order:
        at = axes.index(letter)
        own = lax.index_in_dim(value, 0, at, keepdims=False).astype(F32)
        if letter == "z":
            for k in (1, 2, 3):
                own = own + xor_permute(
                    lax.index_in_dim(value, k, at, keepdims=False), 2 * k, 0
                ).astype(F32)
        else:
            own = own + xor_permute(
                lax.index_in_dim(value, 1, at, keepdims=False), *MASKS[letter]
            ).astype(F32)
        axes = axes.replace(letter, "")
        value = own.astype(BF16) if axes else own
    return value


def swap(value):
    rank_count = lax.axis_size("tensor")
    return lax.ppermute(value, "tensor", [(t, t ^ 1) for t in range(rank_count)])


def to_segment(local):
    core = lax.axis_index("tensor") % 2
    own = lax.dynamic_index_in_dim(local, core, 0, keepdims=False)
    other = swap(lax.dynamic_index_in_dim(local, 1 - core, 0, keepdims=False))
    return jnp.where(core == 0, jnp.concatenate([own, other]), jnp.concatenate([other, own]))


def from_segment(segment):
    core = lax.axis_index("tensor") % 2
    halves = segment.reshape((2, -1) + segment.shape[1:])
    own = lax.dynamic_index_in_dim(halves, core, 0, keepdims=False)
    other = swap(lax.dynamic_index_in_dim(halves, 1 - core, 0, keepdims=False))
    return jnp.where(core == 0, jnp.stack([own, other]), jnp.stack([other, own]))


def dot(left, right, left_dim, right_dim):
    return lax.dot_general(
        left, right, (((left_dim,), (right_dim,)), ((), ())), preferred_element_type=F32
    )


def density_of(mean_logit, var_logit):
    basis_var = (1.0 / NB) ** 2
    centre_pos = jax.nn.sigmoid(mean_logit)
    spread_sq = 0.05 * jax.nn.softplus(var_logit) + basis_var
    centres = (jnp.arange(NB, dtype=F32) + 0.5) / NB
    return jnp.sqrt(basis_var / spread_sq)[..., None] * jnp.exp(
        -0.5 * (centre_pos[..., None] - centres) ** 2 / spread_sq[..., None]
    )


def layer_norm(residual, norm_gain, norm_bias):
    centred = residual - jnp.mean(residual, axis=-1, keepdims=True)
    return (
        centred * lax.rsqrt(jnp.mean(centred * centred, axis=-1, keepdims=True) + 1e-05) * norm_gain
        + norm_bias
    )


def gelu_tanh(value):
    return jax.nn.gelu(value, approximate=True)


def local(
    tokens, lengths, mem_mask, cotangent, w_qkv, w_gauss, w_out, ln_gain, ln_bias, w_up, w_down
):
    dp_count = lax.axis_size("dp")
    rank = lax.axis_index("tensor")
    core, segment = rank % 2, rank // 2
    ridge = jnp.asarray(ridge_matrix())
    rows = D // dp_count

    qkv_parts = gather_all(w_qkv, "zyxc")
    small = jnp.concatenate([w_gauss.astype(F32).reshape(-1), ln_gain, ln_bias])
    small_parts = gather_all(small, "zyxc")
    out_parts = gather_all(w_out.T, "zyxc")
    up_parts = gather_all(w_up, "zyxc")
    down_parts = gather_all(w_down.T, "xzyc")
    parts_of = lambda parts: parts.reshape((dp_count, 4) + parts.shape[1:])
    weight_qkv = parts_of(qkv_parts).transpose(2, 0, 3, 1, 4).reshape(3, D, D)
    weight_out_t = parts_of(out_parts).transpose(0, 2, 1, 3).reshape(D, D)
    weight_up = parts_of(up_parts).transpose(0, 2, 1, 3).reshape(D, 4 * D)
    weight_down_t = parts_of(down_parts).transpose(0, 2, 1, 3).reshape(D, 4 * D)
    gauss_size = w_gauss.size
    gauss = parts_of(small_parts[:, :gauss_size]).reshape(dp_count, 4, 2, 3, -1)
    gauss = gauss.transpose(2, 1, 3, 0, 4).reshape(2, H, DH)
    norm_gain = small_parts[:, gauss_size : gauss_size + ln_gain.size].reshape(D)
    norm_bias = small_parts[:, gauss_size + ln_gain.size :].reshape(D)

    x = to_segment(tokens)
    valid = (
        segment * SEGL + jnp.arange(SEGL) < lax.dynamic_index_in_dim(lengths, core, 0, False)
    ).astype(F32)
    pair = lax.dynamic_index_in_dim(mem_mask, core, 0, False)[1, 0].astype(F32)
    pair_scale = pair / jnp.maximum(pair, 1.0)
    seed = (to_segment(cotangent).astype(F32) * valid[:, None]).astype(BF16)

    q, k, v = (dot(x, weight_qkv[i], 1, 0).astype(BF16) for i in range(3))
    pooled = (v.astype(F32) * (valid * pair_scale)[:, None]).astype(BF16)
    coef_next = dot(ridge, pooled, 1, 0).astype(BF16)
    coef = lax.ppermute(coef_next, "tensor", [(0, 2), (1, 3)])
    heads = lambda value: value.reshape(value.shape[0], H, DH)
    positions = jnp.arange(SEGL)
    allowed = (positions[None, :] < positions[:, None]) & (valid[None, :] > 0.5)
    allowed = allowed | (positions[None, :] == positions[:, None])
    qh, kh, vh = heads(q), heads(k), heads(v)
    scores = jnp.einsum("qhd,khd->hqk", qh, kh, preferred_element_type=F32) * DH**-0.5
    scores = jnp.where(allowed[None], scores, -1e30)
    exponent = jnp.exp(scores - jnp.max(scores, axis=-1, keepdims=True))
    attn = (exponent / jnp.sum(exponent, axis=-1, keepdims=True)).astype(BF16)
    attended = jnp.einsum("hqk,khd->qhd", attn, vh, preferred_element_type=F32)
    logits = [jnp.einsum("qhd,hd->qh", qh.astype(F32), gauss[i]) for i in range(2)]
    density = density_of(*logits).astype(BF16)
    coef_heads = heads(coef)
    recalled = jnp.einsum("qhn,nhd->qhd", density, coef_heads, preferred_element_type=F32)
    heads_out = (attended + recalled).reshape(SEGL, D).astype(BF16)
    residual = x.astype(F32) + dot(heads_out, weight_out_t, 1, 1)
    normed = layer_norm(residual, norm_gain, norm_bias).astype(BF16)

    pre = dot(normed, weight_up, 1, 0)
    hidden = gelu_tanh(pre).astype(BF16)
    output = residual + dot(hidden, weight_down_t, 1, 1)

    grad_down_t = dot(seed, hidden, 0, 0)
    hidden_grad = dot(seed, weight_down_t, 1, 0).astype(BF16).astype(F32)
    _, gelu_back = jax.vjp(gelu_tanh, pre)
    pre_grad = gelu_back(hidden_grad)[0].astype(BF16)
    grad_up = dot(normed, pre_grad, 0, 0)
    normed_grad = dot(pre_grad, weight_up, 1, 1).astype(BF16).astype(F32)
    _, norm_back = jax.vjp(layer_norm, residual, norm_gain, norm_bias)
    resid_from_norm, gain_part, bias_part = norm_back(normed_grad)
    resid_grad = seed.astype(F32) + resid_from_norm
    mix_grad = resid_grad.astype(BF16)

    grad_out_t = dot(mix_grad, heads_out, 0, 0)
    head_grad = heads(dot(mix_grad, weight_out_t, 1, 0).astype(BF16))
    coef_grad = jnp.einsum("qhn,qhd->nhd", density, head_grad, preferred_element_type=F32)
    coef_grad = lax.ppermute(coef_grad.reshape(NB, D).astype(BF16), "tensor", [(2, 0), (3, 1)])
    masked_grad = dot(ridge, coef_grad, 0, 0) * (valid * pair_scale)[:, None]
    density_grad = jnp.einsum("qhd,nhd->qhn", head_grad, coef_heads, preferred_element_type=F32)
    _, density_back = jax.vjp(density_of, *logits)
    logit_grads = density_back(density_grad)
    value_grad = jnp.einsum("hqk,qhd->khd", attn, head_grad, preferred_element_type=F32)
    prob_grad = jnp.einsum("qhd,khd->hqk", head_grad, vh, preferred_element_type=F32)
    probs = attn.astype(F32)
    score_grad = (
        probs * (prob_grad - jnp.sum(prob_grad * probs, axis=-1, keepdims=True))
    ).astype(BF16)
    query_grad = jnp.einsum("hqk,khd->qhd", score_grad, kh, preferred_element_type=F32) * DH**-0.5
    for i in range(2):
        query_grad = query_grad + logit_grads[i][..., None] * gauss[i]
    key_grad = jnp.einsum("hqk,qhd->khd", score_grad, qh, preferred_element_type=F32) * DH**-0.5
    value_grad = value_grad.reshape(SEGL, D) + masked_grad
    qkv_grad = [
        query_grad.reshape(SEGL, D).astype(BF16),
        key_grad.reshape(SEGL, D).astype(BF16),
        value_grad.astype(BF16),
    ]
    gauss_grad = jnp.stack([jnp.einsum("qhd,qh->hd", qh.astype(F32), g) for g in logit_grads])
    grad_qkv = jnp.stack([dot(x, g, 0, 0) for g in qkv_grad])
    whole_grad = sum(dot(g, weight_qkv[i], 1, 1) for i, g in enumerate(qkv_grad))
    grad_tokens = whole_grad + resid_grad

    split = lambda grad: grad.reshape(dp_count, rows, 4, -1).transpose(0, 2, 1, 3).reshape(
        dp_count * 4, rows, -1
    )
    own_down = scatter_all(split(grad_down_t), "cyzx").T
    own_up = scatter_all(split(grad_up), "cxyz")
    own_out = scatter_all(split(grad_out_t), "cxyz").T
    own_qkv = scatter_all(jnp.stack([split(g) for g in grad_qkv], axis=1), "cxyz")
    gauss_parts = gauss_grad.reshape(2, 4, 3, dp_count, -1).transpose(3, 1, 0, 2, 4)
    small_grads = jnp.concatenate(
        [
            gauss_parts.reshape(dp_count * 4, -1),
            gain_part.reshape(dp_count * 4, -1),
            bias_part.reshape(dp_count * 4, -1),
        ],
        axis=1,
    )
    own_small = scatter_all(small_grads, "cxyz")
    own_gauss = own_small[:gauss_size].reshape(w_gauss.shape)
    own_gain = own_small[gauss_size : gauss_size + ln_gain.size]
    own_bias = own_small[gauss_size + ln_gain.size :]
    return (
        from_segment(output),
        from_segment(grad_tokens),
        own_qkv,
        own_gauss,
        own_out,
        own_gain,
        own_bias,
        own_up,
        own_down,
    )


def solution(mesh):
    return jax.shard_map(
        local,
        mesh=mesh,
        in_specs=(
            P("dp", "tensor", None),
            P("dp"),
            P("dp", None, None),
            P("dp", "tensor", None),
            P(None, "dp", "tensor"),
            P(None, "tensor", "dp"),
            P("tensor", "dp"),
            P(("dp", "tensor")),
            P(("dp", "tensor")),
            P("dp", "tensor"),
            P("tensor", "dp"),
        ),
        out_specs=(
            P("dp", "tensor", None),
            P("dp", "tensor", None),
            P(None, "dp", "tensor"),
            P(None, "tensor", "dp"),
            P("tensor", "dp"),
            P(("dp", "tensor")),
            P(("dp", "tensor")),
            P("dp", "tensor"),
            P("tensor", "dp"),
        ),
        check_vma=False,
    )
```

```python
import functools

import jax
import jax.numpy as jnp
import numpy as np
from jax import lax
from jax.experimental import pallas as pl
from jax.experimental.pallas import tpu as pltpu
from jax.sharding import PartitionSpec as P

D = 768
H = 12
DH = 64
NB = 256
SEGL = 512
FF = 3072
PAIRS = H // 2
AXES = ("dp", "tensor")
F32 = jnp.float32
BF16 = jnp.bfloat16
BASIS_VAR = (1.0 / NB) ** 2
VMEM = pltpu.VMEM
SMEM = pltpu.SMEM


def ridge_matrix():
    centres = (np.arange(NB) + 0.5) / NB
    samples = (np.arange(SEGL) + 0.5) / SEGL
    rows = np.exp(-0.5 * ((samples[None, :] - centres[:, None]) * NB) ** 2)
    gram = rows @ rows.T + 0.5 * np.eye(NB)
    return np.linalg.solve(gram, rows).astype(np.float32).astype(jnp.bfloat16)


SIZES = {"z": 4, "y": 2, "x": 2, "c": 2}


def xor_permute(value, letter, k):
    dp_mask, tensor_mask = {"z": (2 * k, 0), "y": (k, 0), "x": (0, 2 * k), "c": (0, k)}[letter]
    dp_count, rank_count = lax.axis_size("dp"), lax.axis_size("tensor")
    pairs = [
        (d * rank_count + t, (d ^ dp_mask) * rank_count + (t ^ tensor_mask))
        for d in range(dp_count)
        for t in range(rank_count)
    ]
    return lax.ppermute(value, AXES, pairs)


def swap(value):
    return xor_permute(value, "c", 1)


def piece_table(order):
    first, second, third = order
    table = []
    for at, (k3, kc) in enumerate([(0, 0), (1, 0), (0, 1), (1, 1)]):
        for i2 in range(SIZES[second]):
            for i1 in range(SIZES[first]):
                k = {first: i1, second: i2, third: k3}
                table.append((at, (i2, i1), k["z"] * 2 + k["y"], k["x"], kc))
    return table


def gather(piece, order):
    first, second, third = order
    for letter in (first, second):
        piece = jnp.stack(
            [piece] + [xor_permute(piece, letter, k) for k in range(1, SIZES[letter])]
        )
    other = xor_permute(piece, third, 1)
    return [piece, other, swap(piece), swap(other)]


def as_gathered(whole, order):
    first, second, third = order
    whole = whole.reshape((4, 2) + whole.shape[1:])
    at = {"z": 0, "y": 1, "x": 2, "c": 3}
    rest = list(range(4, whole.ndim))
    whole = whole.transpose([at["c"], at[third], at[second], at[first]] + rest)
    return [whole[0, 0], whole[0, 1], whole[1, 0], whole[1, 1]]


def scatter(keep, send, order):
    received = swap(send)
    total = lambda k: keep[k].astype(F32) + received[k].astype(F32)
    for letter in order:
        own = total(0)
        arrived = [
            xor_permute(total(k).astype(BF16), letter, k) for k in range(1, SIZES[letter])
        ]
        total = lambda k, own=own, arrived=arrived: sum(
            (a[k].astype(F32) for a in arrived), own[k]
        )
        last = (own, arrived)
    own, arrived = last
    return sum((a.astype(F32) for a in arrived), own)


def whole_from(keep, send, order):
    first, second, third = order
    whole = jnp.stack([keep, send])
    at = {"c": 0, first: 1, second: 2, third: 3}
    rest = list(range(4, whole.ndim))
    whole = whole.transpose([at["z"], at["y"], at["x"], at["c"]] + rest)
    return whole.reshape((8,) + whole.shape[2:])


def to_segment_parts(local):
    core = lax.axis_index("tensor") % 2
    own = lax.dynamic_index_in_dim(local, core, 0, keepdims=False)
    return own, swap(lax.dynamic_index_in_dim(local, 1 - core, 0, keepdims=False))


def from_segment(segment):
    core = lax.axis_index("tensor") % 2
    half = segment.shape[0] // 2
    own = lax.dynamic_slice_in_dim(segment, core * half, half)
    other = swap(lax.dynamic_slice_in_dim(segment, (1 - core) * half, half))
    return jnp.where(core == 0, jnp.stack([own, other]), jnp.stack([other, own]))


def exact_triple(value):
    high = lax.reduce_precision(value, 8, 7)
    middle = lax.reduce_precision(value - high, 8, 7)
    return [part.astype(BF16) for part in (high, middle, value - high - middle)]


def dot(left, right, left_dim=1, right_dim=0):
    return lax.dot_general(
        left, right, (((left_dim,), (right_dim,)), ((), ())), preferred_element_type=F32
    )


def flip(value):
    return jnp.transpose(value.astype(F32))


def aligned(value, step):
    return pl.multiple_of(value * step, step)


def wide_copies(info, table, arrays, target, sems):
    for at, index, r, kx, kc in table:
        rows = pl.ds(aligned(info[0] ^ r, 96), 96)
        j = kx * 2 + kc
        yield pltpu.make_async_copy(
            arrays[at].at[index], target.at[rows, pl.ds(j * D, D)], sems.at[j]
        )


def wait_wide(target, sems, j):
    block = target.at[:, pl.ds(j * D, D)]
    pltpu.make_async_copy(block, block, sems.at[j]).wait()


def narrow_copies(info, table, arrays, spots, sem):
    for at, index, r, kx, kc in table:
        rows = pl.ds(pl.multiple_of((info[0] ^ r) * 96 + (info[2] ^ kc) * 48, 48), 48)
        columns = pl.ds(aligned(info[1] ^ kx, 384), 384)
        for first, target in spots:
            yield pltpu.make_async_copy(
                arrays[at].at[index + (pl.ds(first, 48),)], target.at[rows, columns], sem
            )


def wait_whole(target, sem):
    pltpu.make_async_copy(target, target, sem).wait()


def out_narrow(info, order, keep, send, spots, sem):
    for at, index, r, kx, kc in scatter_table(order):
        rows = pl.ds(pl.multiple_of((info[0] ^ r) * 96 + (info[2] ^ kc) * 48, 48), 48)
        columns = pl.ds(aligned(info[1] ^ kx, 384), 384)
        for first, source in spots:
            yield pltpu.make_async_copy(
                source.at[rows, columns], (keep, send)[kc].at[index + (pl.ds(first, 48),)], sem
            )


def scatter_table(order):
    a, b, c = order
    table = []
    for kc in range(2):
        for i in range(SIZES[a]):
            for j in range(SIZES[b]):
                for l in range(SIZES[c]):
                    k = {a: i, b: j, c: l}
                    table.append((kc, (i, j, l), k["z"] * 2 + k["y"], k["x"], kc))
    return table


def column_validity(info):
    return (lax.broadcasted_iota(jnp.int32, (SEGL, 1), 0) < info[3]).astype(F32)


def qkv_kernel(table_qk, table_v, info, own, other, ridge, *refs):
    qk, v_parts = refs[0:4], refs[4:8]
    x_out, q_out, k_out, v_out, coef_out = refs[8:13]
    wq, wk, wv, sems = refs[13:]
    copies = list(narrow_copies(info, table_qk, qk, [(0, wq), (48, wk)], sems.at[0]))
    copies += list(narrow_copies(info, table_v, v_parts, [(0, wv)], sems.at[1]))
    for copy in copies:
        copy.start()
    core = info[5]
    x_out[pl.ds(aligned(core, 256), 256), :] = own[...]
    x_out[pl.ds(aligned(1 - core, 256), 256), :] = other[...]
    scale = column_validity(info) * info[4].astype(F32)
    pair_wait = pltpu.make_async_copy(wq, wq, sems.at[0])
    pair_wait.wait()
    pair_wait.wait()

    def project(w, out):
        @pl.loop(0, 3)
        def _(step):
            at = pl.ds(aligned(step, 256), 256)
            out[:, at] = dot(x_out[...], w[:, at]).astype(BF16)

    project(wq, q_out)
    project(wk, k_out)
    wait_whole(wv, sems.at[1])

    @pl.loop(0, 3)
    def _(step):
        at = pl.ds(aligned(step, 256), 256)
        values = dot(x_out[...], wv[:, at]).astype(BF16)
        v_out[:, at] = values
        pooled = (values.astype(F32) * scale).astype(BF16)
        coef_out[:, at] = dot(ridge[...], pooled).astype(BF16)


def density_rows(logits, h):
    mean_logit, var_logit = logits[h : h + 1], logits[2 + h : 3 + h]
    mu = jax.nn.sigmoid(mean_logit)
    softplus = jnp.maximum(var_logit, 0.0) + jnp.log1p(jnp.exp(-jnp.abs(var_logit)))
    return mu, 0.05 * softplus + BASIS_VAR, var_logit


def centre_column():
    return (lax.broadcasted_iota(jnp.int32, (NB, 1), 0).astype(F32) + 0.5) / NB


def half_lanes(h):
    lane = lax.broadcasted_iota(jnp.int32, (1, 128), 1)
    return (lane < DH) if h == 0 else (lane >= DH)


def attend_kernel(info, q, k, v, gauss, attn_t, local_t, dens_t, bias):
    @pl.when(pl.program_id(0) == 0)
    def _():
        key = lax.broadcasted_iota(jnp.int32, (SEGL, SEGL), 0)
        query = lax.broadcasted_iota(jnp.int32, (SEGL, SEGL), 1)
        allowed = ((key < query) & (key < info[3])) | (key == query)
        bias[...] = jnp.where(allowed, 0.0, -1e30)

    values_t = flip(v[...]).astype(BF16)
    logits = dot(gauss[0], q[...], 1, 1)
    centres = centre_column()
    for h in range(2):
        rows = slice(h * DH, (h + 1) * DH)
        keys = jnp.where(half_lanes(h), k[...].astype(F32) * DH**-0.5, 0.0).astype(BF16)
        for block in range(2):
            n = 256 * (block + 1)
            at = slice(256 * block, n)
            scores = dot(keys[:n], q[at], 1, 1) + bias[:n, at]
            exponent = jnp.exp(scores - jnp.max(scores, axis=0, keepdims=True))
            total = jnp.sum(exponent, axis=0, keepdims=True)
            probs = (exponent * (1.0 / total)).astype(BF16)
            attn_t[h, :n, at] = probs
            local_t[rows, at] = dot(values_t[rows, :n], probs)
        mu, spread, _ = density_rows(logits, h)
        offset = mu - centres
        dens_t[h] = (
            jnp.sqrt(BASIS_VAR / spread) * jnp.exp(offset * offset * (-0.5 / spread))
        ).astype(BF16)


def layer_stats(residual):
    mean = jnp.mean(residual, axis=-1, keepdims=True)
    centred = residual - mean
    return centred, lax.rsqrt(jnp.mean(centred * centred, axis=-1, keepdims=True) + 1e-05)


def recall_kernel(table, info, dens_t, coef, local_t, x, gain, bias, *refs):
    parts = refs[0:4]
    heads_out, residual, normed, normed_t = refs[4:8]
    w_out, sem = refs[8:]
    step = pl.program_id(0)

    @pl.when(step == 0)
    def _():
        for copy in narrow_copies(info, table, parts, [(48, w_out)], sem):
            copy.start()

    coef_t = flip(coef[...]).astype(BF16)
    recalled = [dot(coef_t[h * DH : (h + 1) * DH], dens_t[h]) for h in range(2)]
    both = local_t[...] + jnp.concatenate(recalled, axis=0)
    heads_out[:, pl.ds(aligned(step, 128), 128)] = flip(both).astype(BF16)

    @pl.when(step == PAIRS - 1)
    def _():
        wait_whole(w_out, sem)

        @pl.loop(0, 3)
        def _(chunk):
            at = pl.ds(aligned(chunk, 256), 256)
            residual[:, at] = x[:, at].astype(F32) + dot(heads_out[...], w_out[at, :], 1, 1)

        centred, scale = layer_stats(residual[...])
        value = (centred * scale * gain[...] + bias[...]).astype(BF16)
        normed[...] = value
        normed_t[...] = flip(value).astype(BF16)


def gelu_parts(pre):
    c0, c1 = 0.7978845608028654, 0.044715
    square = pre * pre
    inner = jnp.tanh(c0 * pre * (1.0 + c1 * square))
    half = 0.5 * (1.0 + inner)
    slope = half + 0.5 * pre * (1.0 - inner * inner) * (c0 * (1.0 + 3.0 * c1 * square))
    return pre * half, slope


def wide_out(info, order, keep, send, source, sems):
    for at, index, r, kx, kc in scatter_table(order):
        rows = pl.ds(aligned(info[0] ^ r, 96), 96)
        j = kx * 2 + kc
        yield j, pltpu.make_async_copy(
            source.at[rows, pl.ds(j * D, D)], (keep, send)[kc].at[index], sems.at[j]
        )


def wait_out(source, sems):
    for j in range(4):
        wait_wide(source, sems, j)


def up_kernel(table, order, info, normed, seed_t, *refs):
    parts = refs[0:4]
    hidden, slope, keep, send = refs[4:8]
    w_up, grad, sems, out_sems = refs[8:]
    for copy in wide_copies(info, table, parts, w_up, sems):
        copy.start()
    outs = list(wide_out(info, order, keep, send, grad, out_sems))
    for j in (0, 2, 1, 3):
        wait_wide(w_up, sems, j)

        @pl.loop(0, 3)
        def _(chunk):
            at = pl.ds(pl.multiple_of(j * D + chunk * 256, 256), 256)
            value, derivative = gelu_parts(dot(normed[...], w_up[:, at]))
            value = value.astype(BF16)
            hidden[:, at] = value
            slope[:, at] = derivative.astype(BF16)
            grad[:, at] = dot(seed_t[...], value).astype(BF16)

        for owner, copy in outs:
            if owner == j:
                copy.start()
    wait_out(grad, out_sems)


def down_kernel(tables, order, info, seed, normed_t, slope, residual, gain, *refs):
    down_parts, up_parts = refs[0:4], refs[4:8]
    keep, send, resid_grad, gain_grad, bias_grad = refs[8:13]
    w_down, w_up, grad, total, down_sems, up_sems, out_sems = refs[13:]
    for copy in wide_copies(info, tables[0], down_parts, w_down, down_sems):
        copy.start()
    for copy in wide_copies(info, tables[1], up_parts, w_up, up_sems):
        copy.start()
    outs = list(wide_out(info, order, keep, send, grad, out_sems))
    total[...] = jnp.zeros_like(total)
    for j in (0, 2, 1, 3):
        wait_wide(w_down, down_sems, j)
        wait_wide(w_up, up_sems, j)

        @pl.loop(0, 3)
        def _(chunk):
            at = pl.ds(pl.multiple_of(j * D + chunk * 256, 256), 256)
            back = dot(seed[...], w_down[:, at]).astype(BF16).astype(F32)
            back = (back * slope[:, at].astype(F32)).astype(BF16)
            grad[:, at] = dot(normed_t[...], back).astype(BF16)
            total[...] += dot(back, w_up[:, at], 1, 1)

        for owner, copy in outs:
            if owner == j:
                copy.start()
    normed_grad = total[...].astype(BF16).astype(F32)
    centred, scale = layer_stats(residual[...])
    unit = centred * scale
    gain_grad[...] = jnp.sum(normed_grad * unit, axis=0, keepdims=True)
    bias_grad[...] = jnp.sum(normed_grad, axis=0, keepdims=True)
    back = normed_grad * gain[...]
    back = back - jnp.mean(back, axis=-1, keepdims=True) - unit * jnp.mean(
        back * unit, axis=-1, keepdims=True
    )
    resid_grad[...] = seed[...].astype(F32) + scale * back
    wait_out(grad, out_sems)


def mix_back_kernel(table, order, info, resid_grad, heads_out, dens_t, *refs):
    parts = refs[0:4]
    head_grad, coef_grad, keep, send = refs[4:8]
    w_out, grad, mix_t, sem, out_sem = refs[8:]
    step = pl.program_id(0)

    @pl.when(step == 0)
    def _():
        for copy in narrow_copies(info, table, parts, [(48, w_out)], sem):
            copy.start()
        mix = resid_grad[...].astype(BF16)
        mix_t[...] = flip(mix).astype(BF16)
        wait_whole(w_out, sem)

        @pl.loop(0, 3)
        def _(chunk):
            at = pl.ds(aligned(chunk, 256), 256)
            head_grad[:, at] = dot(resid_grad[...].astype(BF16), w_out[:, at]).astype(BF16)
            grad[:, at] = dot(mix_t[...], heads_out[:, at]).astype(BF16)

        for copy in out_narrow(info, order, keep, send, [(0, grad)], out_sem):
            copy.start()

    pair_grad = head_grad[:, pl.ds(aligned(step, 128), 128)].astype(F32)
    sums = [
        dot(dens_t[h], jnp.where(half_lanes(h), pair_grad, 0.0).astype(BF16)) for h in range(2)
    ]
    coef_grad[...] = (sums[0] + sums[1]).astype(BF16)

    @pl.when(step == PAIRS - 1)
    def _():
        wait_whole(grad, out_sem)


def attend_back_kernel(
    attn_t, q, k, v, grad, local_t, dens_t, coef, gauss, gauss_column, *refs
):
    dq_out, dk_out, dv_out, gauss_grad, dq_t, dk_sum, dv_sum, rows_of = refs
    keys_t = flip(k[...]).astype(BF16)
    grad_t = flip(grad[...])
    logits = dot(gauss[0], q[...], 1, 1)
    centres = centre_column()
    dk_sum[...] = jnp.zeros_like(dk_sum)
    dv_sum[...] = jnp.zeros_like(dv_sum)
    rows_of[...] = jnp.zeros_like(rows_of)
    only = lambda h, value: jnp.where(half_lanes(h), value.astype(F32), 0.0).astype(BF16)
    for h in range(2):
        rows = slice(h * DH, (h + 1) * DH)
        values, queries, grads = only(h, v[...]), only(h, q[...]), only(h, grad[...])
        delta = jnp.sum(grad_t[rows] * local_t[rows], axis=0, keepdims=True)
        for block in range(2):
            n = 256 * (block + 1)
            at = slice(256 * block, n)
            probs = attn_t[h, :n, at]
            prob_grad = dot(values[:n], grad[at], 1, 1)
            score_grad = (probs.astype(F32) * (prob_grad - delta[:, at])).astype(BF16)
            dv_sum[:n] += dot(probs, grads[at])
            dk_sum[:n] += dot(score_grad, queries[at])
            dq_t[rows, at] = dot(keys_t[rows, :n], score_grad) * DH**-0.5
        mu, spread, var_logit = density_rows(logits, h)
        inverse = 1.0 / spread
        offset = mu - centres
        weighted = dot(only(h, coef[...]), grad[...], 1, 1) * dens_t[h].astype(F32)
        first = weighted * offset
        sum0 = jnp.sum(weighted, axis=0, keepdims=True)
        sum1 = jnp.sum(first, axis=0, keepdims=True)
        sum2 = jnp.sum(first * offset, axis=0, keepdims=True)
        mean_grad = -sum1 * inverse * mu * (1.0 - mu)
        spread_grad = 0.5 * inverse * (sum2 * inverse - sum0)
        var_grad = spread_grad * 0.05 * jax.nn.sigmoid(var_logit)
        rows_of[h : h + 1] = mean_grad
        rows_of[2 + h : 3 + h] = var_grad
        column = gauss_column[0, rows]
        dq_t[rows] += column[:, 0:1] * mean_grad + column[:, 1:2] * var_grad
    dq_out[...] = jnp.transpose(dq_t[...]).astype(BF16)
    dk_out[...] = (dk_sum[...] * DH**-0.5).astype(BF16)
    dv_out[...] = dv_sum[...]
    high = rows_of[...].astype(BF16)
    gauss_grad[0] = dot(high, q[...]) + dot((rows_of[...] - high.astype(F32)).astype(BF16), q[...])


def qkv_grad_kernel(orders, info, x, dq, dk, dv, coef_grad, ridge_t, *refs):
    keep_qk, send_qk, keep_v, send_v, dv_out, x_t, gq, gk, gv, sems = refs
    x_t[...] = flip(x[...]).astype(BF16)
    scale = column_validity(info) * info[4].astype(F32)

    def weight(source, out):
        @pl.loop(0, 3)
        def _(chunk):
            at = pl.ds(aligned(chunk, 256), 256)
            out[:, at] = dot(x_t[...], source[:, at]).astype(BF16)

    weight(dq, gq)
    weight(dk, gk)
    for copy in out_narrow(info, orders[0], keep_qk, send_qk, [(0, gq), (48, gk)], sems.at[0]):
        copy.start()

    @pl.loop(0, 3)
    def _(chunk):
        at = pl.ds(aligned(chunk, 256), 256)
        pooled_grad = dot(ridge_t[...], coef_grad[:, at])
        dv_out[:, at] = (dv[:, at] + pooled_grad * scale).astype(BF16)
        gv[:, at] = dot(x_t[...], dv_out[:, at]).astype(BF16)

    for copy in out_narrow(info, orders[1], keep_v, send_v, [(0, gv)], sems.at[1]):
        copy.start()
    both = pltpu.make_async_copy(gq, gq, sems.at[0])
    both.wait()
    both.wait()
    wait_whole(gv, sems.at[1])


def input_grad_kernel(table_qk, table_v, info, dq, dk, dv, resid_grad, *refs):
    qk, v_parts = refs[0:4], refs[4:8]
    out, wq, wk, wv, sems = refs[8:]
    for copy in narrow_copies(info, table_qk, qk, [(0, wq), (48, wk)], sems.at[0]):
        copy.start()
    for copy in narrow_copies(info, table_v, v_parts, [(0, wv)], sems.at[1]):
        copy.start()
    pair_wait = pltpu.make_async_copy(wq, wq, sems.at[0])
    pair_wait.wait()
    pair_wait.wait()
    wait_whole(wv, sems.at[1])

    @pl.loop(0, 3)
    def _(chunk):
        at = pl.ds(aligned(chunk, 256), 256)
        part = dot(dq[...], wq[at, :], 1, 1) + dot(dk[...], wk[at, :], 1, 1)
        out[:, at] = resid_grad[:, at] + part + dot(dv[...], wv[at, :], 1, 1)


def output_kernel(table, info, hidden, residual, *refs):
    parts = refs[0:4]
    out, w_down, sems = refs[4:]
    for copy in wide_copies(info, table, parts, w_down, sems):
        copy.start()
    wait_out(w_down, sems)

    @pl.loop(0, 3)
    def _(chunk):
        at = pl.ds(aligned(chunk, 256), 256)
        out[:, at] = residual[:, at] + dot(hidden[...], w_down[at, :], 1, 1)


FULL = pl.BlockSpec(memory_space=VMEM)
ANY = pl.BlockSpec(memory_space=pl.ANY)
SCALARS = pl.BlockSpec(memory_space=SMEM)
MATRIX = (D, D)
WIDE = (D, FF)
DMA = pltpu.SemaphoreType.DMA


def shape(dims, dtype=BF16):
    return jax.ShapeDtypeStruct(dims, dtype)


def run(body, name, args, in_specs, outs, out_specs, scratch=(), grid=None, cost=5.0):
    kwargs = {} if grid is None else {"grid": grid}
    return pl.pallas_call(
        body,
        name=name,
        out_shape=tuple(outs),
        in_specs=list(in_specs),
        out_specs=tuple(out_specs),
        scratch_shapes=list(scratch),
        cost_estimate=pl.CostEstimate(
            flops=int(cost * 9e8), bytes_accessed=int(1e6), transcendentals=0
        ),
        compiler_params=pltpu.CompilerParams(vmem_limit_bytes=48 * 1024 * 1024),
        **kwargs,
    )(*args)


PAIR_COLUMNS = pl.BlockSpec((SEGL, 128), lambda p: (0, p))
PAIR_ROWS = pl.BlockSpec((128, SEGL), lambda p: (p, 0))
PAIR_COEF = pl.BlockSpec((NB, 128), lambda p: (0, p))
PAIR_ATTN = pl.BlockSpec((2, SEGL, SEGL), lambda p: (p, 0, 0))
PAIR_DENS = pl.BlockSpec((2, NB, SEGL), lambda p: (p, 0, 0))


def pair_block(*dims):
    return pl.BlockSpec((1,) + dims, lambda p: (p, 0, 0))


ORDER_QK, ORDER_V, ORDER_UP, ORDER_DOWN = "zyx", "zxy", "zyx", "xzy"
BACK_QK, BACK_V, BACK_UP, BACK_DOWN = "xyz", "yxz", "xyz", "yzx"


def local(
    tokens, lengths, mem_mask, cotangent, w_qkv, w_gauss, w_out, ln_gain, ln_bias, w_up, w_down
):
    dp_count = lax.axis_size("dp")
    dp, rank = lax.axis_index("dp"), lax.axis_index("tensor")
    core, segment = rank % 2, rank // 2
    near = dp_count == 8
    gauss_size, gain_size = w_gauss.size, ln_gain.size
    ridge = ridge_matrix()

    used = lax.dynamic_index_in_dim(lengths, core, 0, False)
    valid_count = jnp.clip(used - segment * SEGL, 0, SEGL)
    pair = lax.dynamic_index_in_dim(mem_mask, core, 0, False)[1, 0]
    where = (dp, segment, core) if near else (0, 0, 0)
    info = jnp.stack(
        [jnp.asarray(value, jnp.int32) for value in where + (valid_count, pair, core)]
    )

    projections = jnp.concatenate([w_qkv, w_out.T[None]])
    if near:
        mine = lax.dynamic_slice_in_dim(projections, core * 48, 48, axis=1)
        partner = swap(lax.dynamic_slice_in_dim(projections, (1 - core) * 48, 48, axis=1))
        projections = jnp.where(
            core == 0,
            jnp.concatenate([mine, partner], axis=2),
            jnp.concatenate([partner, mine], axis=2),
        )
        small = jnp.concatenate(
            [w_gauss.reshape(-1)] + exact_triple(jnp.concatenate([ln_gain, ln_bias]))
        )
        small_rows = jnp.pad(small[None], ((0, 15), (0, 384 - small.size)))
        qk_parts = gather(projections[:2].reshape(96, 384), ORDER_QK)
        v_parts = gather(
            jnp.concatenate([projections[2], projections[3], small_rows]), ORDER_V
        )
        up_parts = gather(w_up, ORDER_UP)
        down_parts = gather(w_down.T, ORDER_DOWN)
        rows = jnp.concatenate(
            [part[:, :, 96, : small.size].reshape(-1, small.size) for part in v_parts]
        )
        flat = [r * 4 + kx * 2 + kc for _, _, r, kx, kc in piece_table(ORDER_V)]
        position = jnp.asarray(np.argsort(np.array(flat)))
        rows = rows[position[jnp.arange(32) ^ (dp * 4 + rank)]]
        triple = rows[:, gauss_size:].astype(F32).reshape(32, 3, 2, gain_size)
        scales = triple[:, 0] + triple[:, 1] + triple[:, 2]
        gauss_parts = rows[:, :gauss_size]
    else:
        every = lambda value: lax.all_gather(value, AXES, axis=0)
        cut = lambda value: value.reshape((8, dp_count // 8) + value.shape[1:])
        both = cut(every(projections).reshape(dp_count, 4, 4, -1, 192))
        both = both.transpose(0, 3, 1, 4, 2, 5).reshape(8, 4, 2, 48, 2, 384)
        both = both.transpose(0, 4, 2, 1, 3, 5)
        qk_parts = as_gathered(both[:, :, :, :2].reshape(8, 2, 2, 96, 384), ORDER_QK)
        v_parts = as_gathered(
            jnp.pad(both[:, :, :, 2:].reshape(8, 2, 2, 96, 384), ((0, 0),) * 3 + ((0, 16), (0, 0))),
            ORDER_V,
        )
        wide = lambda value: cut(every(value).reshape(dp_count, 4, -1, D)).transpose(
            0, 2, 1, 3, 4
        ).reshape(8, 2, 2, 96, D)
        up_parts = as_gathered(wide(w_up), ORDER_UP)
        down_parts = as_gathered(wide(w_down.T), ORDER_DOWN)
        scales = every(jnp.stack([ln_gain, ln_bias]))
        gauss_parts = every(w_gauss.reshape(-1))
    norm_gain, norm_bias = scales[:, 0].reshape(1, D), scales[:, 1].reshape(1, D)
    gauss = gauss_parts.reshape(dp_count, 4, 2, 3, -1).transpose(2, 1, 3, 0, 4)
    gauss = gauss.reshape(2, PAIRS, 2, DH)
    spread_rows = jnp.eye(2, dtype=BF16)[None, None, :, :, None] * gauss[:, :, :, None, :]
    gauss_rows = spread_rows.transpose(1, 0, 2, 3, 4).reshape(PAIRS, 4, 128)
    gauss_rows = jnp.pad(gauss_rows, ((0, 0), (0, 12), (0, 0)))
    gauss_column = gauss.astype(F32).reshape(2, PAIRS, 128).transpose(1, 2, 0)
    gauss_column = jnp.pad(gauss_column, ((0, 0), (0, 0), (0, 126)))
    table_qk, table_v = piece_table(ORDER_QK), piece_table(ORDER_V)
    table_up, table_down = piece_table(ORDER_UP), piece_table(ORDER_DOWN)

    own, other = to_segment_parts(tokens)
    seed_own, seed_other = to_segment_parts(cotangent)
    seed = jnp.where(
        core == 0,
        jnp.concatenate([seed_own, seed_other]),
        jnp.concatenate([seed_other, seed_own]),
    )
    seed = jnp.where(jnp.arange(SEGL)[:, None] < valid_count, seed, 0.0).astype(BF16)
    seed_t = seed.T

    tall = shape((SEGL, D))
    x, q, k, v, coef = run(
        functools.partial(qkv_kernel, table_qk, table_v),
        "qkv",
        [info, own, other, jnp.asarray(ridge)] + qk_parts + v_parts,
        [SCALARS, FULL, FULL, FULL] + [ANY] * 8,
        [tall] * 4 + [shape((NB, D))],
        [FULL] * 5,
        [VMEM(MATRIX, BF16)] * 3 + [DMA((2,))],
        cost=6.0,
    )
    coef = lax.ppermute(coef, "tensor", [(0, 2), (1, 3)])
    attn_t, local_t, dens_t = run(
        attend_kernel,
        "attend",
        [info, q, k, v, gauss_rows],
        [SCALARS] + [PAIR_COLUMNS] * 3 + [pair_block(16, 128)],
        [shape((H, SEGL, SEGL)), shape((D, SEGL), F32), shape((H, NB, SEGL))],
        [PAIR_ATTN, PAIR_ROWS, PAIR_DENS],
        [VMEM((SEGL, SEGL), F32)],
        grid=(PAIRS,),
        cost=12.0,
    )
    whole = lambda *dims: pl.BlockSpec(dims, lambda p: (0,) * len(dims))
    heads_out, residual, normed, normed_t = run(
        functools.partial(recall_kernel, table_v),
        "recall",
        [info, dens_t, coef, local_t, x, norm_gain, norm_bias] + v_parts,
        [SCALARS, PAIR_DENS, PAIR_COEF, PAIR_ROWS, whole(SEGL, D), whole(1, D), whole(1, D)]
        + [ANY] * 4,
        [tall, shape((SEGL, D), F32), tall, shape((D, SEGL))],
        [whole(SEGL, D)] * 3 + [whole(D, SEGL)],
        [VMEM(MATRIX, BF16), DMA(())],
        grid=(PAIRS,),
        cost=7.0,
    )
    piece_dims = lambda order: tuple(SIZES[letter] for letter in order)
    wide_grad = [shape(piece_dims(BACK_DOWN) + (96, D))] * 2
    hidden, slope, keep_down, send_down = run(
        functools.partial(up_kernel, table_up, BACK_DOWN),
        "up",
        [info, normed, seed_t] + up_parts,
        [SCALARS, FULL, FULL] + [ANY] * 4,
        [shape((SEGL, FF))] * 2 + wide_grad,
        [FULL] * 2 + [ANY] * 2,
        [VMEM(WIDE, BF16)] * 2 + [DMA((4,))] * 2,
        cost=12.0,
    )
    own_down = collect(keep_down, send_down, BACK_DOWN, dp_count, D).T
    wide_grad = [shape(piece_dims(BACK_UP) + (96, D))] * 2
    row = shape((1, D), F32)
    keep_up, send_up, resid_grad, gain_part, bias_part = run(
        functools.partial(down_kernel, (table_down, table_up), BACK_UP),
        "down",
        [info, seed, normed_t, slope, residual, norm_gain] + down_parts + up_parts,
        [SCALARS] + [FULL] * 5 + [ANY] * 8,
        wide_grad + [shape((SEGL, D), F32), row, row],
        [ANY] * 2 + [FULL] * 3,
        [VMEM(WIDE, BF16)] * 3 + [VMEM((SEGL, D), F32)] + [DMA((4,))] * 3,
        cost=15.0,
    )
    own_up = collect(keep_up, send_up, BACK_UP, dp_count, D)
    narrow_grad = [shape(piece_dims(BACK_V) + (48, 384))] * 2
    head_grad, coef_grad, keep_out, send_out = run(
        functools.partial(mix_back_kernel, table_v, BACK_V),
        "mix_back",
        [info, resid_grad, heads_out, dens_t] + v_parts,
        [SCALARS, whole(SEGL, D), whole(SEGL, D), PAIR_DENS] + [ANY] * 4,
        [tall, shape((NB, D))] + narrow_grad,
        [whole(SEGL, D), PAIR_COEF] + [ANY] * 2,
        [VMEM(MATRIX, BF16)] * 2 + [VMEM((D, SEGL), BF16)] + [DMA(())] * 2,
        grid=(PAIRS,),
        cost=6.0,
    )
    coef_grad = lax.ppermute(coef_grad, "tensor", [(2, 0), (3, 1)])
    dq, dk, dv, gauss_grad = run(
        attend_back_kernel,
        "attend_back",
        [attn_t, q, k, v, head_grad, local_t, dens_t, coef, gauss_rows, gauss_column],
        [PAIR_ATTN]
        + [PAIR_COLUMNS] * 4
        + [PAIR_ROWS, PAIR_DENS, PAIR_COEF, pair_block(16, 128), pair_block(128, 128)],
        [tall, tall, shape((SEGL, D), F32), shape((PAIRS, 16, 128), F32)],
        [PAIR_COLUMNS] * 3 + [pair_block(16, 128)],
        [
            VMEM((128, SEGL), F32),
            VMEM((SEGL, 128), F32),
            VMEM((SEGL, 128), F32),
            VMEM((16, SEGL), F32),
        ],
        grid=(PAIRS,),
        cost=16.0,
    )
    keep_qk, send_qk, keep_v, send_v, dv = run(
        functools.partial(qkv_grad_kernel, (BACK_QK, BACK_V)),
        "qkv_grad",
        [info, x, dq, dk, dv, coef_grad, jnp.asarray(ridge.T)],
        [SCALARS] + [FULL] * 6,
        [shape(piece_dims(BACK_QK) + (96, 384))] * 2 + narrow_grad + [tall],
        [ANY] * 4 + [FULL],
        [VMEM((D, SEGL), BF16)] + [VMEM(MATRIX, BF16)] * 3 + [DMA((2,))],
        cost=6.0,
    )

    gauss_grad = gauss_grad[:, :4].reshape(PAIRS, 2, 2, 2, DH)
    gauss_grad = jnp.stack([gauss_grad[:, :, h, h] for h in range(2)], axis=2)
    gauss_grad = gauss_grad.transpose(1, 0, 2, 3).reshape(2, 4, 3, dp_count, -1)
    small_grads = jnp.concatenate(
        [
            gauss_grad.transpose(3, 1, 0, 2, 4).reshape(dp_count * 4, -1),
            gain_part.reshape(dp_count * 4, -1),
            bias_part.reshape(dp_count * 4, -1),
        ],
        axis=1,
    )
    count = small_grads.shape[1]
    if near:
        small_grads = small_grads[jnp.arange(32) ^ (dp * 4 + rank)]
        at = {"z": 0, "y": 1, "x": 2, "c": 3}
        small_grads = small_grads.reshape(4, 2, 2, 2, count).transpose(
            [at["c"]] + [at[letter] for letter in BACK_V] + [4]
        )
        small_grads = jnp.pad(small_grads[..., None, :], ((0, 0),) * 4 + ((0, 15), (0, 384 - count)))
        small_grads = small_grads.astype(BF16)
        joined = [
            jnp.concatenate(parts, axis=3)
            for parts in ((keep_v, keep_out, small_grads[0]), (send_v, send_out, small_grads[1]))
        ]
        own_v = scatter(*joined, BACK_V)
        own_small = own_v[96, :count]
        own_qk = scatter(keep_qk, send_qk, BACK_QK)
        narrow = jnp.concatenate([own_qk, own_v[:96]]).reshape(4, 48, 384)
        mine = lax.dynamic_slice_in_dim(narrow, core * 192, 192, axis=2)
        partner = swap(lax.dynamic_slice_in_dim(narrow, (1 - core) * 192, 192, axis=2))
        narrow = jnp.where(
            core == 0,
            jnp.concatenate([mine, partner], axis=1),
            jnp.concatenate([partner, mine], axis=1),
        )
    else:
        own_small = lax.psum_scatter(small_grads, AXES, scatter_dimension=0)
        pieces = [
            whole_from(keep_qk, send_qk, BACK_QK).reshape(8, 2, 2, 2, 48, 384),
            whole_from(keep_v, send_v, BACK_V)[:, :, :, None],
            whole_from(keep_out, send_out, BACK_V)[:, :, :, None],
        ]
        pieces = jnp.concatenate(pieces, axis=3).transpose(0, 2, 4, 3, 1, 5)
        pieces = pieces.reshape(dp_count, D // dp_count, 4, 4, 192).transpose(0, 3, 2, 1, 4)
        narrow = lax.psum_scatter(
            pieces.reshape((-1,) + pieces.shape[2:]).astype(F32), AXES, scatter_dimension=0
        )
    own_qkv, own_out = narrow[:3], narrow[3].T
    own_gauss = own_small[:gauss_size].reshape(w_gauss.shape)
    own_gain = own_small[gauss_size : gauss_size + gain_size]
    own_bias = own_small[gauss_size + gain_size :]

    (grad_tokens,) = run(
        functools.partial(input_grad_kernel, table_qk, table_v),
        "input_grad",
        [info, dq, dk, dv, resid_grad] + qk_parts + v_parts,
        [SCALARS] + [FULL] * 4 + [ANY] * 8,
        [shape((SEGL, D), F32)],
        [FULL],
        [VMEM(MATRIX, BF16)] * 3 + [DMA((2,))],
        cost=5.0,
    )
    (output,) = run(
        functools.partial(output_kernel, table_down),
        "output",
        [info, hidden, residual] + down_parts,
        [SCALARS] + [FULL] * 2 + [ANY] * 4,
        [shape((SEGL, D), F32)],
        [FULL],
        [VMEM(WIDE, BF16), DMA((4,))],
        cost=6.0,
    )
    return (
        from_segment(output),
        from_segment(grad_tokens),
        own_qkv,
        own_gauss,
        own_out,
        own_gain,
        own_bias,
        own_up,
        own_down,
    )


def collect(keep, send, order, dp_count, columns):
    if dp_count == 8:
        return scatter(keep, send, order)
    whole = whole_from(keep, send, order).transpose(0, 3, 1, 2, 4)
    whole = whole.reshape(dp_count, D // dp_count, 4, columns).transpose(0, 2, 1, 3)
    return lax.psum_scatter(
        whole.reshape((-1,) + whole.shape[2:]).astype(F32), AXES, scatter_dimension=0
    )


def solution(mesh):
    return jax.shard_map(
        local,
        mesh=mesh,
        in_specs=(
            P("dp", "tensor", None),
            P("dp"),
            P("dp", None, None),
            P("dp", "tensor", None),
            P(None, "dp", "tensor"),
            P(None, "tensor", "dp"),
            P("tensor", "dp"),
            P(("dp", "tensor")),
            P(("dp", "tensor")),
            P("dp", "tensor"),
            P("tensor", "dp"),
        ),
        out_specs=(
            P("dp", "tensor", None),
            P("dp", "tensor", None),
            P(None, "dp", "tensor"),
            P(None, "tensor", "dp"),
            P("tensor", "dp"),
            P(("dp", "tensor")),
            P(("dp", "tensor")),
            P("dp", "tensor"),
            P("tensor", "dp"),
        ),
        check_vma=False,
    )
```

```python
import functools

import jax
import jax.numpy as jnp
import numpy as np
from jax import lax
from jax.experimental import pallas as pl
from jax.experimental.pallas import tpu as pltpu
from jax.sharding import PartitionSpec as P

D = 768
H = 12
DH = 64
NB = 256
SEGL = 512
FF = 3072
PAIRS = H // 2
AXES = ("dp", "tensor")
F32 = jnp.float32
BF16 = jnp.bfloat16
BASIS_VAR = (1.0 / NB) ** 2
VMEM = pltpu.VMEM
SMEM = pltpu.SMEM


def ridge_matrix():
    centres = (np.arange(NB) + 0.5) / NB
    samples = (np.arange(SEGL) + 0.5) / SEGL
    rows = np.exp(-0.5 * ((samples[None, :] - centres[:, None]) * NB) ** 2)
    gram = rows @ rows.T + 0.5 * np.eye(NB)
    return np.linalg.solve(gram, rows).astype(np.float32).astype(jnp.bfloat16)


SIZES = {"z": 4, "y": 2, "x": 2, "c": 2}


def xor_permute(value, letter, k):
    dp_mask, tensor_mask = {"z": (2 * k, 0), "y": (k, 0), "x": (0, 2 * k), "c": (0, k)}[letter]
    dp_count, rank_count = lax.axis_size("dp"), lax.axis_size("tensor")
    pairs = [
        (d * rank_count + t, (d ^ dp_mask) * rank_count + (t ^ tensor_mask))
        for d in range(dp_count)
        for t in range(rank_count)
    ]
    return lax.ppermute(value, AXES, pairs)


def swap(value):
    return xor_permute(value, "c", 1)


def after(value, *others):
    return lax.optimization_barrier((value,) + others)[0]


def piece_table(order, cores=2):
    first, second, third = order
    table = []
    for at, (kc, k3) in enumerate([(0, 0), (0, 1), (1, 0), (1, 1)][: 2 * cores]):
        for i2 in range(SIZES[second]):
            for i1 in range(SIZES[first]):
                k = {first: i1, second: i2, third: k3}
                table.append((at, (i2, i1), k["z"] * 2 + k["y"], k["x"], kc))
    return table


def spread(piece, letter):
    return [piece] + [xor_permute(piece, letter, k) for k in range(1, SIZES[letter])]


def as_gathered(whole, order):
    first, second, third = order
    whole = whole.reshape((4, 2) + whole.shape[1:])
    at = {"z": 0, "y": 1, "x": 2, "c": 3}
    rest = list(range(4, whole.ndim))
    whole = whole.transpose([at["c"], at[third], at[second], at[first]] + rest)
    return [whole[0, 0], whole[0, 1], whole[1, 0], whole[1, 1]]


def stage(total, letter):
    own = total(0)
    arrived = [xor_permute(total(k).astype(BF16), letter, k) for k in range(1, SIZES[letter])]
    return own, arrived


def combined(own, arrived):
    return lambda k: sum((a[k].astype(F32) for a in arrived), own[k])


def final_sum(own, arrived):
    return sum((a.astype(F32) for a in arrived), own)


def whole_from(parts, order):
    first, second, third = order
    whole = jnp.stack(parts)
    at = {"c": 0, first: 1, second: 2, third: 3}
    rest = list(range(4, whole.ndim))
    whole = whole.transpose([at["z"], at["y"], at["x"], at["c"]] + rest)
    return whole.reshape((8,) + whole.shape[2:])


def to_segment_parts(local):
    core = lax.axis_index("tensor") % 2
    own = lax.dynamic_index_in_dim(local, core, 0, keepdims=False)
    return own, swap(lax.dynamic_index_in_dim(local, 1 - core, 0, keepdims=False))


def from_segment(segment):
    core = lax.axis_index("tensor") % 2
    half = segment.shape[0] // 2
    own = lax.dynamic_slice_in_dim(segment, core * half, half)
    other = swap(lax.dynamic_slice_in_dim(segment, (1 - core) * half, half))
    return jnp.where(core == 0, jnp.stack([own, other]), jnp.stack([other, own]))


def exact_triple(value):
    high = lax.reduce_precision(value, 8, 7)
    middle = lax.reduce_precision(value - high, 8, 7)
    return [part.astype(BF16) for part in (high, middle, value - high - middle)]


def dot(left, right, left_dim=1, right_dim=0):
    return lax.dot_general(
        left, right, (((left_dim,), (right_dim,)), ((), ())), preferred_element_type=F32
    )


def flip(value):
    return jnp.transpose(value.astype(F32))


def aligned(value, step):
    return pl.multiple_of(value * step, step)


def wide_copies(info, table, arrays, target, sems):
    for at, index, r, kx, _ in table:
        rows = pl.ds(aligned(info[0] ^ r, 96), 96)
        yield pltpu.make_async_copy(
            arrays[at].at[index], target.at[rows, pl.ds(kx * D, D)], sems.at[kx]
        )


def wait_wide(target, sems, j):
    block = target.at[:, pl.ds(j * D, D)]
    pltpu.make_async_copy(block, block, sems.at[j]).wait()


def narrow_copies(info, table, arrays, spots, sem):
    for at, index, r, kx, kc in table:
        rows = pl.ds(pl.multiple_of((info[0] ^ r) * 96 + (info[2] ^ kc) * 48, 48), 48)
        columns = pl.ds(aligned(info[1] ^ kx, 384), 384)
        for first, target in spots:
            yield pltpu.make_async_copy(
                arrays[at].at[index + (pl.ds(first, 48),)], target.at[rows, columns], sem
            )


def wait_whole(target, sem):
    pltpu.make_async_copy(target, target, sem).wait()


def out_narrow(info, order, keep, send, spots, sem):
    for index, r, kx, kc in scatter_table(order):
        rows = pl.ds(pl.multiple_of((info[0] ^ r) * 96 + (info[2] ^ kc) * 48, 48), 48)
        columns = pl.ds(aligned(info[1] ^ kx, 384), 384)
        for first, source in spots:
            yield pltpu.make_async_copy(
                source.at[rows, columns], (keep, send)[kc].at[index + (pl.ds(first, 48),)], sem
            )


def scatter_table(order, cores=2):
    a, b, c = order
    table = []
    for kc in range(cores):
        for i in range(SIZES[a]):
            for j in range(SIZES[b]):
                for l in range(SIZES[c]):
                    k = {a: i, b: j, c: l}
                    table.append(((i, j, l), k["z"] * 2 + k["y"], k["x"], kc))
    return table


def column_validity(info):
    return (lax.broadcasted_iota(jnp.int32, (SEGL, 1), 0) < info[3]).astype(F32)


def qkv_kernel(table_qk, table_v, info, own, other, ridge, *refs):
    qk, v_parts = refs[0:4], refs[4:8]
    x_out, q_out, k_out, v_out, coef_out = refs[8:13]
    wq, wk, wv, sems = refs[13:]
    copies = list(narrow_copies(info, table_qk, qk, [(0, wq), (48, wk)], sems.at[0]))
    copies += list(narrow_copies(info, table_v, v_parts, [(0, wv)], sems.at[1]))
    for copy in copies:
        copy.start()
    core = info[5]
    x_out[pl.ds(aligned(core, 256), 256), :] = own[...]
    x_out[pl.ds(aligned(1 - core, 256), 256), :] = other[...]
    scale = column_validity(info) * info[4].astype(F32)
    pair_wait = pltpu.make_async_copy(wq, wq, sems.at[0])
    pair_wait.wait()
    pair_wait.wait()

    def project(w, out):
        @pl.loop(0, 3)
        def _(step):
            at = pl.ds(aligned(step, 256), 256)
            out[:, at] = dot(x_out[...], w[:, at]).astype(BF16)

    project(wq, q_out)
    project(wk, k_out)
    wait_whole(wv, sems.at[1])

    @pl.loop(0, 3)
    def _(step):
        at = pl.ds(aligned(step, 256), 256)
        values = dot(x_out[...], wv[:, at]).astype(BF16)
        v_out[:, at] = values
        pooled = (values.astype(F32) * scale).astype(BF16)
        coef_out[:, at] = dot(ridge[...], pooled).astype(BF16)


def density_rows(logits, h):
    mean_logit, var_logit = logits[h : h + 1], logits[2 + h : 3 + h]
    mu = jax.nn.sigmoid(mean_logit)
    softplus = jnp.maximum(var_logit, 0.0) + jnp.log1p(jnp.exp(-jnp.abs(var_logit)))
    return mu, 0.05 * softplus + BASIS_VAR, var_logit


def centre_column():
    return (lax.broadcasted_iota(jnp.int32, (NB, 1), 0).astype(F32) + 0.5) / NB


def half_lanes(h):
    lane = lax.broadcasted_iota(jnp.int32, (1, 128), 1)
    return (lane < DH) if h == 0 else (lane >= DH)


def attend_kernel(info, q, k, v, gauss, attn_t, local_t, dens_t, bias):
    @pl.when(pl.program_id(0) == 0)
    def _():
        key = lax.broadcasted_iota(jnp.int32, (SEGL, SEGL), 0)
        query = lax.broadcasted_iota(jnp.int32, (SEGL, SEGL), 1)
        allowed = ((key < query) & (key < info[3])) | (key == query)
        bias[...] = jnp.where(allowed, 0.0, -1e30)

    values_t = flip(v[...]).astype(BF16)
    logits = dot(gauss[0], q[...], 1, 1)
    centres = centre_column()
    for h in range(2):
        rows = slice(h * DH, (h + 1) * DH)
        keys = jnp.where(half_lanes(h), k[...].astype(F32) * DH**-0.5, 0.0).astype(BF16)
        for block in range(2):
            n = 256 * (block + 1)
            at = slice(256 * block, n)
            scores = dot(keys[:n], q[at], 1, 1) + bias[:n, at]
            exponent = jnp.exp(scores - jnp.max(scores, axis=0, keepdims=True))
            total = jnp.sum(exponent, axis=0, keepdims=True)
            probs = (exponent * (1.0 / total)).astype(BF16)
            attn_t[h, :n, at] = probs
            local_t[rows, at] = dot(values_t[rows, :n], probs)
        mu, spread, _ = density_rows(logits, h)
        offset = mu - centres
        dens_t[h] = (
            jnp.sqrt(BASIS_VAR / spread) * jnp.exp(offset * offset * (-0.5 / spread))
        ).astype(BF16)


def layer_stats(residual):
    mean = jnp.mean(residual, axis=-1, keepdims=True)
    centred = residual - mean
    return centred, lax.rsqrt(jnp.mean(centred * centred, axis=-1, keepdims=True) + 1e-05)


def recall_kernel(table, info, dens_t, coef, local_t, x, gain, bias, *refs):
    parts = refs[0:4]
    heads_out, residual, normed = refs[4:7]
    w_out, sem = refs[7:]
    step = pl.program_id(0)

    @pl.when(step == 0)
    def _():
        for copy in narrow_copies(info, table, parts, [(48, w_out)], sem):
            copy.start()

    coef_t = flip(coef[...]).astype(BF16)
    recalled = [dot(coef_t[h * DH : (h + 1) * DH], dens_t[h]) for h in range(2)]
    both = local_t[...] + jnp.concatenate(recalled, axis=0)
    heads_out[:, pl.ds(aligned(step, 128), 128)] = flip(both).astype(BF16)

    @pl.when(step == PAIRS - 1)
    def _():
        wait_whole(w_out, sem)

        @pl.loop(0, 3)
        def _(chunk):
            at = pl.ds(aligned(chunk, 256), 256)
            residual[:, at] = x[:, at].astype(F32) + dot(heads_out[...], w_out[at, :], 1, 1)

        centred, scale = layer_stats(residual[...])
        normed[...] = (centred * scale * gain[...] + bias[...]).astype(BF16)


def gelu_parts(pre):
    c0, c1 = 0.7978845608028654, 0.044715
    square = pre * pre
    inner = jnp.tanh(c0 * pre * (1.0 + c1 * square))
    half = 0.5 * (1.0 + inner)
    slope = half + 0.5 * pre * (1.0 - inner * inner) * (c0 * (1.0 + 3.0 * c1 * square))
    return pre * half, slope


def wide_out(info, order, keep, source, sems):
    for index, r, kx, _ in scatter_table(order, 1):
        rows = pl.ds(aligned(info[0] ^ r, 96), 96)
        yield kx, pltpu.make_async_copy(
            source.at[rows, pl.ds(kx * D, D)], keep.at[index], sems.at[kx]
        )


def wait_out(source, sems):
    for j in range(2):
        wait_wide(source, sems, j)


def up_kernel(table, order, info, own, other, seed_t, *refs):
    parts = refs[0:2]
    hidden, slope, keep = refs[2:5]
    w_up, grad, sems, out_sems = refs[5:]
    for copy in wide_copies(info, table, parts, w_up, sems):
        copy.start()
    outs = list(wide_out(info, order, keep, grad, out_sems))
    for j in range(2):
        wait_wide(w_up, sems, j)

        @pl.loop(0, 3)
        def _(chunk):
            at = pl.ds(pl.multiple_of(j * D + chunk * 256, 256), 256)
            sums = []
            for half, source in enumerate((own, other)):
                value, derivative = gelu_parts(dot(source[...], w_up[:, at]))
                value = value.astype(BF16)
                hidden[half, :, at] = value
                slope[half, :, at] = derivative.astype(BF16)
                sums.append(dot(seed_t[:, half * SEGL : (half + 1) * SEGL], value))
            grad[:, at] = (sums[0] + sums[1]).astype(BF16)

        for owner, copy in outs:
            if owner == j:
                copy.start()
    wait_out(grad, out_sems)


def down_kernel(tables, order, info, seed, own, other, slope, *refs):
    down_parts, up_parts = refs[0:2], refs[2:4]
    keep, own_grad, other_grad = refs[4:7]
    w_down, w_up, grad, total, normed_t, down_sems, up_sems, out_sems = refs[7:]
    for copy in wide_copies(info, tables[0], down_parts, w_down, down_sems):
        copy.start()
    for copy in wide_copies(info, tables[1], up_parts, w_up, up_sems):
        copy.start()
    outs = list(wide_out(info, order, keep, grad, out_sems))
    total[...] = jnp.zeros_like(total)
    normed_t[:, :SEGL] = flip(own[...]).astype(BF16)
    normed_t[:, SEGL:] = flip(other[...]).astype(BF16)
    for j in range(2):
        wait_wide(w_down, down_sems, j)
        wait_wide(w_up, up_sems, j)

        @pl.loop(0, 3)
        def _(chunk):
            at = pl.ds(pl.multiple_of(j * D + chunk * 256, 256), 256)
            sums = []
            for half in range(2):
                back = dot(seed[half], w_down[:, at]).astype(BF16).astype(F32)
                back = (back * slope[half, :, at].astype(F32)).astype(BF16)
                sums.append(dot(normed_t[:, half * SEGL : (half + 1) * SEGL], back))
                total[half] += dot(back, w_up[:, at], 1, 1)
            grad[:, at] = (sums[0] + sums[1]).astype(BF16)

        for owner, copy in outs:
            if owner == j:
                copy.start()
    own_grad[...] = total[0]
    other_grad[...] = total[1].astype(BF16)
    wait_out(grad, out_sems)


def mix_back_kernel(table, order, info, own, other, seed, residual, gain, heads_out, dens_t, *refs):
    parts = refs[0:4]
    resid_grad, head_grad, coef_grad, gain_grad, bias_grad, keep, send = refs[4:11]
    w_out, grad, mix, mix_t, sem, out_sem = refs[11:]
    step = pl.program_id(0)

    @pl.when(step == 0)
    def _():
        for copy in narrow_copies(info, table, parts, [(48, w_out)], sem):
            copy.start()
        normed_grad = (own[...] + other[...].astype(F32)).astype(BF16).astype(F32)
        centred, scale = layer_stats(residual[...])
        unit = centred * scale
        gain_grad[...] = jnp.sum(normed_grad * unit, axis=0, keepdims=True)
        bias_grad[...] = jnp.sum(normed_grad, axis=0, keepdims=True)
        back = normed_grad * gain[...]
        back = back - jnp.mean(back, axis=-1, keepdims=True) - unit * jnp.mean(
            back * unit, axis=-1, keepdims=True
        )
        back = seed[...].astype(F32) + scale * back
        resid_grad[...] = back
        mix[...] = back.astype(BF16)
        mix_t[...] = flip(mix[...]).astype(BF16)
        wait_whole(w_out, sem)

        @pl.loop(0, 3)
        def _(chunk):
            at = pl.ds(aligned(chunk, 256), 256)
            head_grad[:, at] = dot(mix[...], w_out[:, at]).astype(BF16)
            grad[:, at] = dot(mix_t[...], heads_out[:, at]).astype(BF16)

        for copy in out_narrow(info, order, keep, send, [(0, grad)], out_sem):
            copy.start()

    pair_grad = head_grad[:, pl.ds(aligned(step, 128), 128)].astype(F32)
    sums = [
        dot(dens_t[h], jnp.where(half_lanes(h), pair_grad, 0.0).astype(BF16)) for h in range(2)
    ]
    coef_grad[...] = (sums[0] + sums[1]).astype(BF16)

    @pl.when(step == PAIRS - 1)
    def _():
        wait_whole(grad, out_sem)


def attend_back_kernel(
    attn_t, q, k, v, grad, local_t, dens_t, coef, gauss, gauss_column, *refs
):
    dq_out, dk_out, dv_out, gauss_grad, dq_t, dk_sum, dv_sum, rows_of = refs
    keys_t = flip(k[...]).astype(BF16)
    grad_t = flip(grad[...])
    logits = dot(gauss[0], q[...], 1, 1)
    centres = centre_column()
    dk_sum[...] = jnp.zeros_like(dk_sum)
    dv_sum[...] = jnp.zeros_like(dv_sum)
    rows_of[...] = jnp.zeros_like(rows_of)
    only = lambda h, value: jnp.where(half_lanes(h), value.astype(F32), 0.0).astype(BF16)
    for h in range(2):
        rows = slice(h * DH, (h + 1) * DH)
        values, queries, grads = only(h, v[...]), only(h, q[...]), only(h, grad[...])
        delta = jnp.sum(grad_t[rows] * local_t[rows], axis=0, keepdims=True)
        for block in range(2):
            n = 256 * (block + 1)
            at = slice(256 * block, n)
            probs = attn_t[h, :n, at]
            prob_grad = dot(values[:n], grad[at], 1, 1)
            score_grad = (probs.astype(F32) * (prob_grad - delta[:, at])).astype(BF16)
            dv_sum[:n] += dot(probs, grads[at])
            dk_sum[:n] += dot(score_grad, queries[at])
            dq_t[rows, at] = dot(keys_t[rows, :n], score_grad) * DH**-0.5
        mu, spread, var_logit = density_rows(logits, h)
        inverse = 1.0 / spread
        offset = mu - centres
        weighted = dot(only(h, coef[...]), grad[...], 1, 1) * dens_t[h].astype(F32)
        first = weighted * offset
        sum0 = jnp.sum(weighted, axis=0, keepdims=True)
        sum1 = jnp.sum(first, axis=0, keepdims=True)
        sum2 = jnp.sum(first * offset, axis=0, keepdims=True)
        mean_grad = -sum1 * inverse * mu * (1.0 - mu)
        spread_grad = 0.5 * inverse * (sum2 * inverse - sum0)
        var_grad = spread_grad * 0.05 * jax.nn.sigmoid(var_logit)
        rows_of[h : h + 1] = mean_grad
        rows_of[2 + h : 3 + h] = var_grad
        column = gauss_column[0, rows]
        dq_t[rows] += column[:, 0:1] * mean_grad + column[:, 1:2] * var_grad
    dq_out[...] = jnp.transpose(dq_t[...]).astype(BF16)
    dk_out[...] = (dk_sum[...] * DH**-0.5).astype(BF16)
    dv_out[...] = dv_sum[...]
    high = rows_of[...].astype(BF16)
    gauss_grad[0] = dot(high, q[...]) + dot((rows_of[...] - high.astype(F32)).astype(BF16), q[...])


def qkv_grad_kernel(orders, info, x, dq, dk, dv, coef_grad, ridge_t, *refs):
    keep_qk, send_qk, keep_v, send_v, dv_out, x_t, gq, gk, gv, sems = refs
    x_t[...] = flip(x[...]).astype(BF16)
    scale = column_validity(info) * info[4].astype(F32)

    def weight(source, out):
        @pl.loop(0, 3)
        def _(chunk):
            at = pl.ds(aligned(chunk, 256), 256)
            out[:, at] = dot(x_t[...], source[:, at]).astype(BF16)

    weight(dq, gq)
    weight(dk, gk)
    for copy in out_narrow(info, orders[0], keep_qk, send_qk, [(0, gq), (48, gk)], sems.at[0]):
        copy.start()

    @pl.loop(0, 3)
    def _(chunk):
        at = pl.ds(aligned(chunk, 256), 256)
        pooled_grad = dot(ridge_t[...], coef_grad[:, at])
        dv_out[:, at] = (dv[:, at] + pooled_grad * scale).astype(BF16)
        gv[:, at] = dot(x_t[...], dv_out[:, at]).astype(BF16)

    for copy in out_narrow(info, orders[1], keep_v, send_v, [(0, gv)], sems.at[1]):
        copy.start()
    both = pltpu.make_async_copy(gq, gq, sems.at[0])
    both.wait()
    both.wait()
    wait_whole(gv, sems.at[1])


def input_grad_kernel(table_qk, table_v, info, dq, dk, dv, resid_grad, *refs):
    qk, v_parts = refs[0:4], refs[4:8]
    out, wq, wk, wv, sems = refs[8:]
    for copy in narrow_copies(info, table_qk, qk, [(0, wq), (48, wk)], sems.at[0]):
        copy.start()
    for copy in narrow_copies(info, table_v, v_parts, [(0, wv)], sems.at[1]):
        copy.start()
    pair_wait = pltpu.make_async_copy(wq, wq, sems.at[0])
    pair_wait.wait()
    pair_wait.wait()
    wait_whole(wv, sems.at[1])

    @pl.loop(0, 3)
    def _(chunk):
        at = pl.ds(aligned(chunk, 256), 256)
        part = dot(dq[...], wq[at, :], 1, 1) + dot(dk[...], wk[at, :], 1, 1)
        out[:, at] = resid_grad[:, at] + part + dot(dv[...], wv[at, :], 1, 1)


def output_kernel(table, info, hidden, residual, *refs):
    parts = refs[0:2]
    out, other, w_down, sems = refs[2:]
    for copy in wide_copies(info, table, parts, w_down, sems):
        copy.start()
    wait_out(w_down, sems)

    @pl.loop(0, 3)
    def _(chunk):
        at = pl.ds(aligned(chunk, 256), 256)
        out[:, at] = residual[:, at] + dot(hidden[0], w_down[at, :], 1, 1)
        other[:, at] = dot(hidden[1], w_down[at, :], 1, 1)


FULL = pl.BlockSpec()
ANY = pl.BlockSpec(memory_space=pl.ANY)
SCALARS = pl.BlockSpec(memory_space=SMEM)
MATRIX = (D, D)
HALF = FF // 2
WIDE = (D, HALF)
DMA = pltpu.SemaphoreType.DMA


def shape(dims, dtype=BF16):
    return jax.ShapeDtypeStruct(dims, dtype)


def run(body, name, args, in_specs, outs, out_specs, scratch=(), grid=None, cost=5.0, vmem=48):
    kwargs = {} if grid is None else {"grid": grid}
    args = [
        value
        if spec is SCALARS
        else pltpu.with_memory_space_constraint(value, pltpu.HBM)
        for value, spec in zip(args, in_specs)
    ]
    return pl.pallas_call(
        body,
        name=name,
        out_shape=tuple(pltpu.HBM(out.shape, out.dtype) for out in outs),
        in_specs=list(in_specs),
        out_specs=tuple(out_specs),
        scratch_shapes=list(scratch),
        cost_estimate=pl.CostEstimate(
            flops=int(cost * 2e8), bytes_accessed=int(1e6), transcendentals=0
        ),
        compiler_params=pltpu.CompilerParams(vmem_limit_bytes=vmem * 1024 * 1024),
        **kwargs,
    )(*args)


PAIR_COLUMNS = pl.BlockSpec((SEGL, 128), lambda p: (0, p))
PAIR_ROWS = pl.BlockSpec((128, SEGL), lambda p: (p, 0))
PAIR_COEF = pl.BlockSpec((NB, 128), lambda p: (0, p))
PAIR_ATTN = pl.BlockSpec((2, SEGL, SEGL), lambda p: (p, 0, 0))
PAIR_DENS = pl.BlockSpec((2, NB, SEGL), lambda p: (p, 0, 0))


def pair_block(*dims):
    return pl.BlockSpec((1,) + dims, lambda p: (p, 0, 0))


ORDER_QK, ORDER_V, ORDER_UP, ORDER_DOWN = "zyx", "zxy", "zyx", "xzy"
BACK_QK, BACK_V, BACK_UP, BACK_DOWN = "xyz", "yxz", "xyz", "yzx"


def local(
    tokens, lengths, mem_mask, cotangent, w_qkv, w_gauss, w_out, ln_gain, ln_bias, w_up, w_down
):
    dp_count = lax.axis_size("dp")
    dp, rank = lax.axis_index("dp"), lax.axis_index("tensor")
    core, segment = rank % 2, rank // 2
    near = dp_count == 8
    gauss_size, gain_size = w_gauss.size, ln_gain.size
    ridge = ridge_matrix()

    used = [
        jnp.clip(lax.dynamic_index_in_dim(lengths, at, 0, False) - segment * SEGL, 0, SEGL)
        for at in (core, 1 - core)
    ]
    pair = lax.dynamic_index_in_dim(mem_mask, core, 0, False)[1, 0]
    where = (dp, segment, core) if near else (0, 0, 0)
    info = jnp.stack([jnp.asarray(value, jnp.int32) for value in where + (used[0], pair, core)])

    projections = jnp.concatenate([w_qkv, w_out.T[None]])
    if near:
        mine = lax.dynamic_slice_in_dim(projections, core * 48, 48, axis=1)
        partner = swap(lax.dynamic_slice_in_dim(projections, (1 - core) * 48, 48, axis=1))
        projections = jnp.where(
            core == 0,
            jnp.concatenate([mine, partner], axis=2),
            jnp.concatenate([partner, mine], axis=2),
        )
        small = jnp.concatenate(
            [w_gauss.reshape(-1)] + exact_triple(jnp.concatenate([ln_gain, ln_bias]))
        )
        small_rows = jnp.pad(small[None], ((0, 15), (0, 384 - small.size)))
        along_z = spread(jnp.concatenate([projections.reshape(192, 384), small_rows]), "z")
        qk_parts = spread(jnp.stack([part[:96] for part in along_z]), "y")
        v_parts = spread(jnp.stack([part[96:] for part in along_z]), "x")
        qk_parts = spread(jnp.stack(qk_parts), "x")
        v_parts = spread(jnp.stack(v_parts), "y")
        qk_parts = qk_parts + [swap(part) for part in qk_parts]
        v_parts = v_parts + [swap(part) for part in v_parts]
        up_parts = spread(after(w_up, *along_z[1:]), "z")
        up_parts = spread(jnp.stack(up_parts), "y")
        up_parts = spread(jnp.stack(up_parts), "x")
        down_parts = spread(after(w_down.T, *along_z[1:]), "x")
        down_parts = spread(jnp.stack(down_parts), "z")
        down_parts = spread(jnp.stack(down_parts), "y")
    else:
        every = lambda value: lax.all_gather(value, AXES, axis=0)
        cut = lambda value: value.reshape((8, dp_count // 8) + value.shape[1:])
        both = cut(every(projections).reshape(dp_count, 4, 4, -1, 192))
        both = both.transpose(0, 3, 1, 4, 2, 5).reshape(8, 4, 2, 48, 2, 384)
        both = both.transpose(0, 4, 2, 1, 3, 5)
        qk_parts = as_gathered(both[:, :, :, :2].reshape(8, 2, 2, 96, 384), ORDER_QK)
        v_parts = as_gathered(
            jnp.pad(both[:, :, :, 2:].reshape(8, 2, 2, 96, 384), ((0, 0),) * 3 + ((0, 16), (0, 0))),
            ORDER_V,
        )

        def wide(value):
            value = cut(every(value).reshape(dp_count, 4, -1, D)).transpose(0, 2, 1, 3, 4)
            value = value.reshape(8, 2, 2, 96, D)
            return lax.dynamic_slice_in_dim(value, core, 1, axis=2)

        double = lambda value: jnp.concatenate([value, value], axis=2)
        up_parts = as_gathered(double(wide(w_up)), ORDER_UP)[:2]
        down_parts = as_gathered(double(wide(w_down.T)), ORDER_DOWN)[:2]
    table_qk, table_v = piece_table(ORDER_QK), piece_table(ORDER_V)
    table_up, table_down = piece_table(ORDER_UP, 1), piece_table(ORDER_DOWN, 1)

    own, other = to_segment_parts(tokens)
    tall = shape((SEGL, D))
    x, q, k, v, coef = run(
        functools.partial(qkv_kernel, table_qk, table_v),
        "qkv",
        [info, own, other, jnp.asarray(ridge)] + qk_parts + v_parts,
        [SCALARS, FULL, FULL, FULL] + [ANY] * 8,
        [tall] * 4 + [shape((NB, D))],
        [FULL] * 5,
        [VMEM(MATRIX, BF16)] * 3 + [DMA((2,))],
        cost=6.0,
        vmem=14,
    )
    coef = lax.ppermute(coef, "tensor", [(0, 2), (1, 3)])

    if near:
        rows = jnp.concatenate(
            [part[:, :, 96, : small.size].reshape(-1, small.size) for part in v_parts]
        )
        flat = [r * 4 + kx * 2 + kc for _, _, r, kx, kc in table_v]
        position = jnp.asarray(np.argsort(np.array(flat)))
        rows = rows[position[jnp.arange(32) ^ (dp * 4 + rank)]]
        triple = rows[:, gauss_size:].astype(F32).reshape(32, 3, 2, gain_size)
        scales = triple[:, 0] + triple[:, 1] + triple[:, 2]
        gauss_parts = rows[:, :gauss_size]
    else:
        scales = every(jnp.stack([ln_gain, ln_bias]))
        gauss_parts = every(w_gauss.reshape(-1))
    norm_gain, norm_bias = scales[:, 0].reshape(1, D), scales[:, 1].reshape(1, D)
    gauss = gauss_parts.reshape(dp_count, 4, 2, 3, -1).transpose(2, 1, 3, 0, 4)
    gauss = gauss.reshape(2, PAIRS, 2, DH)
    spread_rows = jnp.eye(2, dtype=BF16)[None, None, :, :, None] * gauss[:, :, :, None, :]
    gauss_rows = spread_rows.transpose(1, 0, 2, 3, 4).reshape(PAIRS, 4, 128)
    gauss_rows = jnp.pad(gauss_rows, ((0, 0), (0, 12), (0, 0)))
    gauss_column = gauss.astype(F32).reshape(2, PAIRS, 128).transpose(1, 2, 0)
    gauss_column = jnp.pad(gauss_column, ((0, 0), (0, 0), (0, 126)))

    cotangent = after(cotangent, q)
    theirs = swap(cotangent)
    everything = jnp.where(
        core == 0,
        jnp.concatenate([cotangent, theirs], axis=1),
        jnp.concatenate([theirs, cotangent], axis=1),
    )
    seed = jnp.stack(
        [lax.dynamic_index_in_dim(everything, at, 0, False) for at in (core, 1 - core)]
    )
    seed = jnp.stack(
        [
            jnp.where(jnp.arange(SEGL)[:, None] < count, part, 0.0).astype(BF16)
            for count, part in zip(used, seed)
        ]
    )
    seed_t = seed.reshape(2 * SEGL, D).T

    attn_t, local_t, dens_t = run(
        attend_kernel,
        "attend",
        [info, q, k, v, gauss_rows],
        [SCALARS] + [PAIR_COLUMNS] * 3 + [pair_block(16, 128)],
        [shape((H, SEGL, SEGL)), shape((D, SEGL), F32), shape((H, NB, SEGL))],
        [PAIR_ATTN, PAIR_ROWS, PAIR_DENS],
        [VMEM((SEGL, SEGL), F32)],
        grid=(PAIRS,),
        cost=12.0,
        vmem=14,
    )
    whole = lambda *dims: pl.BlockSpec(dims, lambda p: (0,) * len(dims))
    heads_out, residual, normed = run(
        functools.partial(recall_kernel, table_v),
        "recall",
        [info, dens_t, coef, local_t, x, norm_gain, norm_bias] + v_parts,
        [SCALARS, PAIR_DENS, PAIR_COEF, PAIR_ROWS, whole(SEGL, D), whole(1, D), whole(1, D)]
        + [ANY] * 4,
        [tall, shape((SEGL, D), F32), tall],
        [whole(SEGL, D)] * 3,
        [VMEM(MATRIX, BF16), DMA(())],
        grid=(PAIRS,),
        cost=7.0,
        vmem=18,
    )
    normed_other = swap(normed)
    piece_dims = lambda order: tuple(SIZES[letter] for letter in order)
    hidden, slope, keep_down = run(
        functools.partial(up_kernel, table_up, BACK_DOWN),
        "up",
        [info, normed, normed_other, seed_t] + up_parts,
        [SCALARS, FULL, FULL, FULL] + [ANY] * 2,
        [shape((2, SEGL, HALF))] * 2 + [shape(piece_dims(BACK_DOWN) + (96, D))],
        [FULL] * 2 + [ANY],
        [VMEM(WIDE, BF16)] * 2 + [DMA((2,))] * 2,
        cost=12.0,
        vmem=22,
    )
    if near:
        down_1 = stage(lambda k: keep_down[k].astype(F32), BACK_DOWN[0])
    keep_up, own_grad, other_grad = run(
        functools.partial(down_kernel, (table_down, table_up), BACK_UP),
        "down",
        [info, seed, normed, normed_other, slope] + down_parts + up_parts,
        [SCALARS] + [FULL] * 4 + [ANY] * 4,
        [shape(piece_dims(BACK_UP) + (96, D)), shape((SEGL, D), F32), tall],
        [ANY] + [FULL] * 2,
        [VMEM(WIDE, BF16)] * 3
        + [VMEM((2, SEGL, D), F32), VMEM((D, 2 * SEGL), BF16)]
        + [DMA((2,))] * 3,
        cost=15.0,
        vmem=30,
    )
    if near:
        up_1 = stage(lambda k: keep_up[k].astype(F32), BACK_UP[0])
    other_grad = swap(other_grad)
    narrow_grad = [shape(piece_dims(BACK_V) + (48, 384))] * 2
    row = shape((1, D), F32)
    resid_grad, head_grad, coef_grad, gain_part, bias_part, keep_out, send_out = run(
        functools.partial(mix_back_kernel, table_v, BACK_V),
        "mix_back",
        [info, own_grad, other_grad, seed[0], residual, norm_gain, heads_out, dens_t] + v_parts,
        [SCALARS]
        + [whole(SEGL, D)] * 4
        + [whole(1, D), whole(SEGL, D), PAIR_DENS]
        + [ANY] * 4,
        [shape((SEGL, D), F32), tall, shape((NB, D)), row, row] + narrow_grad,
        [whole(SEGL, D), whole(SEGL, D), PAIR_COEF, whole(1, D), whole(1, D)] + [ANY] * 2,
        [VMEM(MATRIX, BF16)] * 2
        + [VMEM((SEGL, D), BF16), VMEM((D, SEGL), BF16)]
        + [DMA(())] * 2,
        grid=(PAIRS,),
        cost=6.0,
        vmem=26,
    )
    coef_grad = lax.ppermute(coef_grad, "tensor", [(2, 0), (3, 1)])
    if near:
        head_grad = after(head_grad, *down_1[1])
        down_2 = stage(combined(*down_1), BACK_DOWN[1])
    dq, dk, dv, gauss_grad = run(
        attend_back_kernel,
        "attend_back",
        [attn_t, q, k, v, head_grad, local_t, dens_t, coef, gauss_rows, gauss_column],
        [PAIR_ATTN]
        + [PAIR_COLUMNS] * 4
        + [PAIR_ROWS, PAIR_DENS, PAIR_COEF, pair_block(16, 128), pair_block(128, 128)],
        [tall, tall, shape((SEGL, D), F32), shape((PAIRS, 16, 128), F32)],
        [PAIR_COLUMNS] * 3 + [pair_block(16, 128)],
        [
            VMEM((128, SEGL), F32),
            VMEM((SEGL, 128), F32),
            VMEM((SEGL, 128), F32),
            VMEM((16, SEGL), F32),
        ],
        grid=(PAIRS,),
        cost=16.0,
        vmem=16,
    )
    if near:
        dq = after(dq, *up_1[1])
        up_2 = stage(combined(*up_1), BACK_UP[1])
    keep_qk, send_qk, keep_v, send_v, dv = run(
        functools.partial(qkv_grad_kernel, (BACK_QK, BACK_V)),
        "qkv_grad",
        [info, x, dq, dk, dv, coef_grad, jnp.asarray(ridge.T)],
        [SCALARS] + [FULL] * 6,
        [shape(piece_dims(BACK_QK) + (96, 384))] * 2 + narrow_grad + [tall],
        [ANY] * 4 + [FULL],
        [VMEM((D, SEGL), BF16)] + [VMEM(MATRIX, BF16)] * 3 + [DMA((2,))],
        cost=6.0,
        vmem=18,
    )

    gauss_grad = gauss_grad[:, :4].reshape(PAIRS, 2, 2, 2, DH)
    gauss_grad = jnp.stack([gauss_grad[:, :, h, h] for h in range(2)], axis=2)
    gauss_grad = gauss_grad.transpose(1, 0, 2, 3).reshape(2, 4, 3, dp_count, -1)
    small_grads = jnp.concatenate(
        [
            gauss_grad.transpose(3, 1, 0, 2, 4).reshape(dp_count * 4, -1),
            gain_part.reshape(dp_count * 4, -1),
            bias_part.reshape(dp_count * 4, -1),
        ],
        axis=1,
    )
    count = small_grads.shape[1]
    if near:
        small_grads = small_grads[jnp.arange(32) ^ (dp * 4 + rank)]
        at = {"z": 0, "y": 1, "x": 2, "c": 3}
        small_grads = small_grads.reshape(4, 2, 2, 2, count).transpose(
            [at["c"]] + [at[letter] for letter in BACK_V] + [4]
        )
        small_grads = jnp.pad(small_grads[..., None, :], ((0, 0),) * 4 + ((0, 15), (0, 384 - count)))
        small_grads = small_grads.astype(BF16)
        keep_v, send_v = (
            jnp.concatenate(parts, axis=3)
            for parts in ((keep_v, keep_out, small_grads[0]), (send_v, send_out, small_grads[1]))
        )
        got_qk, got_v = swap(send_qk), swap(send_v)
        first_qk = [(keep_qk[k].astype(F32) + got_qk[k].astype(F32)) for k in range(2)]
        first_v = [(keep_v[k].astype(F32) + got_v[k].astype(F32)) for k in range(2)]
        first_qk[1], first_v[1] = first_qk[1].astype(BF16), first_v[1].astype(BF16)
        qk_1 = stage(lambda k: first_qk[k], BACK_QK[0])
        v_1 = stage(lambda k: first_v[k], BACK_V[0])
        dq_late = after(dq, first_qk[1], first_v[1])
    else:
        dq_late = dq

    (grad_tokens,) = run(
        functools.partial(input_grad_kernel, table_qk, table_v),
        "input_grad",
        [info, dq_late, dk, dv, resid_grad] + qk_parts + v_parts,
        [SCALARS] + [FULL] * 4 + [ANY] * 8,
        [shape((SEGL, D), F32)],
        [FULL],
        [VMEM(MATRIX, BF16)] * 3 + [DMA((2,))],
        cost=5.0,
        vmem=16,
    )
    if near:
        down_3 = stage(combined(*down_2), BACK_DOWN[2])
        up_3 = stage(combined(*up_2), BACK_UP[2])
        hidden = after(hidden, grad_tokens, qk_1[1][0], v_1[1][0])
    fed_own, fed_other = run(
        functools.partial(output_kernel, table_down),
        "output",
        [info, hidden, residual] + down_parts,
        [SCALARS] + [FULL] * 2 + [ANY] * 2,
        [shape((SEGL, D), F32)] * 2,
        [FULL] * 2,
        [VMEM(WIDE, BF16), DMA((2,))],
        cost=6.0,
        vmem=18,
    )
    half = SEGL // 2
    part = lambda value, at: lax.dynamic_slice_in_dim(value, at * half, half)
    arrived = swap(jnp.stack([part(fed_own, 1 - core), part(fed_other, 1 - core)]))
    own_rows, their_rows = part(fed_own, core) + arrived[1], part(fed_other, core) + arrived[0]
    output = jnp.where(
        core == 0, jnp.stack([own_rows, their_rows]), jnp.stack([their_rows, own_rows])
    )

    if near:
        qk_2 = stage(combined(*qk_1), BACK_QK[1])
        v_2 = stage(combined(*v_1), BACK_V[1])
        to_qk, to_v = combined(*qk_2), combined(*v_2)
        joined = final_sum(*stage(lambda k: jnp.concatenate([to_qk(k), to_v(k)]), "z"))
        own_small = joined[192, :count]
        narrow = joined[:192].reshape(4, 48, 384)
        mine = lax.dynamic_slice_in_dim(narrow, core * 192, 192, axis=2)
        partner = swap(lax.dynamic_slice_in_dim(narrow, (1 - core) * 192, 192, axis=2))
        narrow = jnp.where(
            core == 0,
            jnp.concatenate([mine, partner], axis=1),
            jnp.concatenate([partner, mine], axis=1),
        )
        own_up, own_down = final_sum(*up_3), final_sum(*down_3).T
    else:
        own_small = lax.psum_scatter(small_grads, AXES, scatter_dimension=0)
        pieces = [
            whole_from([keep_qk, send_qk], BACK_QK).reshape(8, 2, 2, 2, 48, 384),
            whole_from([keep_v, send_v], BACK_V)[:, :, :, None],
            whole_from([keep_out, send_out], BACK_V)[:, :, :, None],
        ]
        pieces = jnp.concatenate(pieces, axis=3).transpose(0, 2, 4, 3, 1, 5)
        pieces = pieces.reshape(dp_count, D // dp_count, 4, 4, 192).transpose(0, 3, 2, 1, 4)
        total = lambda value: lax.psum_scatter(value.astype(F32), AXES, scatter_dimension=0)
        narrow = total(pieces.reshape((-1,) + pieces.shape[2:]))

        def owned(keep, order):
            mine = whole_from([keep], order)
            both = jnp.concatenate(
                [jnp.where(core == at, mine, jnp.zeros_like(mine)) for at in range(2)], axis=2
            )
            both = both.transpose(0, 3, 1, 2, 4).reshape(dp_count, D // dp_count, 4, D)
            both = both.transpose(0, 2, 1, 3)
            return total(both.reshape((-1,) + both.shape[2:]))

        own_up, own_down = owned(keep_up, BACK_UP), owned(keep_down, BACK_DOWN).T
    own_qkv, own_out = narrow[:3], narrow[3].T
    return (
        output,
        from_segment(grad_tokens),
        own_qkv,
        own_small[:gauss_size].reshape(w_gauss.shape),
        own_out,
        own_small[gauss_size : gauss_size + gain_size],
        own_small[gauss_size + gain_size :],
        own_up,
        own_down,
    )


def solution(mesh):
    return jax.shard_map(
        local,
        mesh=mesh,
        in_specs=(
            P("dp", "tensor", None),
            P("dp"),
            P("dp", None, None),
            P("dp", "tensor", None),
            P(None, "dp", "tensor"),
            P(None, "tensor", "dp"),
            P("tensor", "dp"),
            P(("dp", "tensor")),
            P(("dp", "tensor")),
            P("dp", "tensor"),
            P("tensor", "dp"),
        ),
        out_specs=(
            P("dp", "tensor", None),
            P("dp", "tensor", None),
            P(None, "dp", "tensor"),
            P(None, "tensor", "dp"),
            P("tensor", "dp"),
            P(("dp", "tensor")),
            P(("dp", "tensor")),
            P("dp", "tensor"),
            P("tensor", "dp"),
        ),
        check_vma=False,
    )
```

```python
import functools

import jax
import jax.numpy as jnp
import numpy as np
from jax import lax
from jax.experimental import pallas as pl
from jax.experimental.pallas import tpu as pltpu
from jax.sharding import PartitionSpec as P

D = 768
H = 12
DH = 64
NB = 256
SEGL = 512
FF = 3072
PAIRS = H // 2
AXES = ("dp", "tensor")
F32 = jnp.float32
BF16 = jnp.bfloat16
BASIS_VAR = (1.0 / NB) ** 2
VMEM = pltpu.VMEM
SMEM = pltpu.SMEM


def ridge_matrix():
    centres = (np.arange(NB) + 0.5) / NB
    samples = (np.arange(SEGL) + 0.5) / SEGL
    rows = np.exp(-0.5 * ((samples[None, :] - centres[:, None]) * NB) ** 2)
    gram = rows @ rows.T + 0.5 * np.eye(NB)
    return np.linalg.solve(gram, rows).astype(np.float32).astype(jnp.bfloat16)


SIZES = {"z": 4, "y": 2, "x": 2, "c": 2}


def xor_permute(value, letter, k):
    dp_mask, tensor_mask = {"z": (2 * k, 0), "y": (k, 0), "x": (0, 2 * k), "c": (0, k)}[letter]
    dp_count, rank_count = lax.axis_size("dp"), lax.axis_size("tensor")
    pairs = [
        (d * rank_count + t, (d ^ dp_mask) * rank_count + (t ^ tensor_mask))
        for d in range(dp_count)
        for t in range(rank_count)
    ]
    return lax.ppermute(value, AXES, pairs)


def swap(value):
    return xor_permute(value, "c", 1)


def after(value, *others):
    return lax.optimization_barrier((value,) + others)[0]


def piece_table(order, cores=2):
    first, second, third = order
    table = []
    for at, (kc, k3) in enumerate([(0, 0), (0, 1), (1, 0), (1, 1)][: 2 * cores]):
        for i2 in range(SIZES[second]):
            for i1 in range(SIZES[first]):
                k = {first: i1, second: i2, third: k3}
                table.append((at, (i2, i1), k["z"] * 2 + k["y"], k["x"], kc))
    return table


def spread(piece, letter):
    return [piece] + [xor_permute(piece, letter, k) for k in range(1, SIZES[letter])]


def as_gathered(whole, order):
    first, second, third = order
    whole = whole.reshape((4, 2) + whole.shape[1:])
    at = {"z": 0, "y": 1, "x": 2, "c": 3}
    rest = list(range(4, whole.ndim))
    whole = whole.transpose([at["c"], at[third], at[second], at[first]] + rest)
    return [whole[0, 0], whole[0, 1], whole[1, 0], whole[1, 1]]


def stage(total, letter):
    own = total(0)
    arrived = [xor_permute(total(k).astype(BF16), letter, k) for k in range(1, SIZES[letter])]
    return own, arrived


def combined(own, arrived):
    return lambda k: sum((a[k].astype(F32) for a in arrived), own[k].astype(F32))


def final_sum(own, arrived):
    return sum((a.astype(F32) for a in arrived), own)


def whole_from(parts, order):
    first, second, third = order
    whole = jnp.stack(parts)
    at = {"c": 0, first: 1, second: 2, third: 3}
    rest = list(range(4, whole.ndim))
    whole = whole.transpose([at["z"], at["y"], at["x"], at["c"]] + rest)
    return whole.reshape((8,) + whole.shape[2:])


def to_segment_parts(local):
    core = lax.axis_index("tensor") % 2
    own = lax.dynamic_index_in_dim(local, core, 0, keepdims=False)
    return own, swap(lax.dynamic_index_in_dim(local, 1 - core, 0, keepdims=False))


def exact_triple(value):
    high = lax.reduce_precision(value, 8, 7)
    middle = lax.reduce_precision(value - high, 8, 7)
    return [part.astype(BF16) for part in (high, middle, value - high - middle)]


def dot(left, right, left_dim=1, right_dim=0):
    return lax.dot_general(
        left, right, (((left_dim,), (right_dim,)), ((), ())), preferred_element_type=F32
    )


def flip(value):
    return jnp.transpose(value.astype(F32))


def aligned(value, step):
    return pl.multiple_of(value * step, step)


def wide_copies(info, table, arrays, target, sems):
    for at, index, r, kx, _ in table:
        rows = pl.ds(aligned(info[0] ^ r, 96), 96)
        yield pltpu.make_async_copy(
            arrays[at].at[index], target.at[rows, pl.ds(kx * D, D)], sems.at[kx]
        )


def wait_wide(target, sems, j):
    block = target.at[:, pl.ds(j * D, D)]
    pltpu.make_async_copy(block, block, sems.at[j]).wait()


def narrow_copies(info, table, arrays, spots, sem):
    for at, index, r, kx, kc in table:
        rows = pl.ds(pl.multiple_of((info[0] ^ r) * 96 + (info[2] ^ kc) * 48, 48), 48)
        columns = pl.ds(aligned(info[1] ^ kx, 384), 384)
        for first, target in spots:
            yield pltpu.make_async_copy(
                arrays[at].at[index + (pl.ds(first, 48),)], target.at[rows, columns], sem
            )


def wait_whole(target, sem):
    pltpu.make_async_copy(target, target, sem).wait()


def out_narrow(info, order, keep, send, spots, sem):
    for index, r, kx, kc in scatter_table(order):
        rows = pl.ds(pl.multiple_of((info[0] ^ r) * 96 + (info[2] ^ kc) * 48, 48), 48)
        columns = pl.ds(aligned(info[1] ^ kx, 384), 384)
        for first, source in spots:
            yield pltpu.make_async_copy(
                source.at[rows, columns], (keep, send)[kc].at[index + (pl.ds(first, 48),)], sem
            )


def scatter_table(order, cores=2):
    a, b, c = order
    table = []
    for kc in range(cores):
        for i in range(SIZES[a]):
            for j in range(SIZES[b]):
                for l in range(SIZES[c]):
                    k = {a: i, b: j, c: l}
                    table.append(((i, j, l), k["z"] * 2 + k["y"], k["x"], kc))
    return table


def column_validity(info):
    return (lax.broadcasted_iota(jnp.int32, (SEGL, 1), 0) < info[3]).astype(F32)


def small_layout():
    column = np.arange(D)
    owner = [(column % DH // 8) * 4 + column // 192, column // 24]
    place = [column // DH % 3 * 8 + column % 8, 48 + column % 24]
    return np.stack(owner + place + [column] * 4).astype(np.int32)


def small_places(layout, i, count):
    row = lax.broadcasted_iota(jnp.int32, (count, D), 0)
    place = layout[2 + i // 2][None] + 24 * (i % 2)
    hit = row == place
    if i > 1 and count > 128:
        hit = hit | (row == place + 48) | (row == place + 96)
    return hit.astype(F32).astype(BF16)


def small_masks(info, table, owner):
    row = lax.broadcasted_iota(jnp.int32, (512, D), 0)
    device = row * 0 - 1
    me = info[0] * 4 + info[1] * 2 + info[2]
    for n, (_, _, r, kx, kc) in enumerate(table):
        device = jnp.where(row == 16 * n, me ^ (r * 4 + kx * 2 + kc), device)
    return device == owner[0:1], device == owner[1:2]


def qkv_kernel(table_qk, table_v, near, info, own, other, ridge, *refs):
    qk, v_parts = refs[0:4], refs[4:8]
    if near:
        layout = refs[8][...]
        refs = refs[:8] + refs[9:]
    x_out, q_out, k_out, v_out, coef_out = refs[8:13]
    if near:
        gauss_out, gain_out, bias_out = refs[13:16]
        refs = refs[:13] + refs[16:]
    wq, wk, wv, small, sems = refs[13:]
    copies = list(narrow_copies(info, table_qk, qk, [(0, wq), (48, wk)], sems.at[0]))
    copies += list(narrow_copies(info, table_v, v_parts, [(0, wv)], sems.at[1]))
    if near:
        for n, (at, index, _, _, _) in enumerate(table_v):
            copies.append(
                pltpu.make_async_copy(
                    v_parts[at].at[index + (pl.ds(96, 16),)], small.at[pl.ds(16 * n, 16)], sems.at[2]
                )
            )
    for copy in copies:
        copy.start()
    core = info[5]
    x_out[pl.ds(aligned(core, 256), 256), :] = own[...]
    x_out[pl.ds(aligned(1 - core, 256), 256), :] = other[...]
    scale = column_validity(info) * info[4].astype(F32)
    pair_wait = pltpu.make_async_copy(wq, wq, sems.at[0])
    pair_wait.wait()
    pair_wait.wait()

    def project(w, out):
        @pl.loop(0, 3)
        def _(step):
            at = pl.ds(aligned(step, 256), 256)
            out[:, at] = dot(x_out[...], w[:, at]).astype(BF16)

    project(wq, q_out)
    project(wk, k_out)
    wait_whole(wv, sems.at[1])

    @pl.loop(0, 3)
    def _(step):
        at = pl.ds(aligned(step, 256), 256)
        values = dot(x_out[...], wv[:, at]).astype(BF16)
        v_out[:, at] = values
        pooled = (values.astype(F32) * scale).astype(BF16)
        coef_out[:, at] = dot(ridge[...], pooled).astype(BF16)

    if near:
        wait_whole(small, sems.at[2])
        gauss_mask, scale_mask = small_masks(info, table_v, layout)
        rows = small[:, :256]

        def collect(at, mask):
            return jnp.sum(jnp.where(mask, dot(rows, small_places(layout, at, 256)), 0.0), axis=0, keepdims=True)

        means, variances = collect(0, gauss_mask), collect(1, gauss_mask)
        gain_out[...] = collect(2, scale_mask)
        bias_out[...] = collect(3, scale_mask)
        row = lax.broadcasted_iota(jnp.int32, (16, 128), 0)
        for p in range(PAIRS):
            at = slice(128 * p, 128 * (p + 1))
            value = jnp.where(row < 2, means[:, at], variances[:, at])
            for h in range(2):
                value = jnp.where((row % 2 == h) & ~half_lanes(h), 0.0, value)
            gauss_out[p] = jnp.where(row < 4, value, 0.0).astype(BF16)


def density_rows(logits, h):
    mean_logit, var_logit = logits[h : h + 1], logits[2 + h : 3 + h]
    mu = jax.nn.sigmoid(mean_logit)
    softplus = jnp.maximum(var_logit, 0.0) + jnp.log1p(jnp.exp(-jnp.abs(var_logit)))
    return mu, 0.05 * softplus + BASIS_VAR, var_logit


def centre_column():
    return (lax.broadcasted_iota(jnp.int32, (NB, 1), 0).astype(F32) + 0.5) / NB


def half_lanes(h):
    lane = lax.broadcasted_iota(jnp.int32, (1, 128), 1)
    return (lane < DH) if h == 0 else (lane >= DH)


def attend_kernel(info, q, k, v, gauss, attn_t, local_t, dens_t, bias):
    @pl.when(pl.program_id(0) == 0)
    def _():
        key = lax.broadcasted_iota(jnp.int32, (SEGL, SEGL), 0)
        query = lax.broadcasted_iota(jnp.int32, (SEGL, SEGL), 1)
        allowed = ((key < query) & (key < info[3])) | (key == query)
        bias[...] = jnp.where(allowed, 0.0, -1e30)

    values_t = flip(v[...]).astype(BF16)
    logits = dot(gauss[0], q[...], 1, 1)
    centres = centre_column()
    for h in range(2):
        rows = slice(h * DH, (h + 1) * DH)
        keys = jnp.where(half_lanes(h), k[...].astype(F32) * DH**-0.5, 0.0).astype(BF16)
        for block in range(2):
            n = 256 * (block + 1)
            at = slice(256 * block, n)
            scores = dot(keys[:n], q[at], 1, 1) + bias[:n, at]
            exponent = jnp.exp(scores - jnp.max(scores, axis=0, keepdims=True))
            total = jnp.sum(exponent, axis=0, keepdims=True)
            probs = (exponent * (1.0 / total)).astype(BF16)
            attn_t[h, :n, at] = probs
            local_t[rows, at] = dot(values_t[rows, :n], probs)
        mu, spread, _ = density_rows(logits, h)
        offset = mu - centres
        dens_t[h] = (
            jnp.sqrt(BASIS_VAR / spread) * jnp.exp(offset * offset * (-0.5 / spread))
        ).astype(BF16)


def layer_stats(residual):
    mean = jnp.mean(residual, axis=-1, keepdims=True)
    centred = residual - mean
    return centred, lax.rsqrt(jnp.mean(centred * centred, axis=-1, keepdims=True) + 1e-05)


def recall_kernel(table, info, dens_t, coef, local_t, x, gain, bias, *refs):
    parts = refs[0:4]
    heads_out, residual, normed = refs[4:7]
    w_out, sem = refs[7:]
    step = pl.program_id(0)

    @pl.when(step == 0)
    def _():
        for copy in narrow_copies(info, table, parts, [(48, w_out)], sem):
            copy.start()

    coef_t = flip(coef[...]).astype(BF16)
    recalled = [dot(coef_t[h * DH : (h + 1) * DH], dens_t[h]) for h in range(2)]
    both = local_t[...] + jnp.concatenate(recalled, axis=0)
    heads_out[:, pl.ds(aligned(step, 128), 128)] = flip(both).astype(BF16)

    @pl.when(step == PAIRS - 1)
    def _():
        wait_whole(w_out, sem)

        @pl.loop(0, 3)
        def _(chunk):
            at = pl.ds(aligned(chunk, 256), 256)
            residual[:, at] = x[:, at].astype(F32) + dot(heads_out[...], w_out[at, :], 1, 1)

        centred, scale = layer_stats(residual[...])
        normed[...] = (centred * scale * gain[...] + bias[...]).astype(BF16)


def gelu_parts(pre):
    c0, c1 = 0.7978845608028654, 0.044715
    square = pre * pre
    inner = jnp.tanh(c0 * pre * (1.0 + c1 * square))
    half = 0.5 * (1.0 + inner)
    slope = half + 0.5 * pre * (1.0 - inner * inner) * (c0 * (1.0 + 3.0 * c1 * square))
    return pre * half, slope


def wide_out(info, order, keep, source, sems):
    for index, r, kx, _ in scatter_table(order, 1):
        rows = pl.ds(aligned(info[0] ^ r, 96), 96)
        yield kx, pltpu.make_async_copy(
            source.at[rows, pl.ds(kx * D, D)], keep[index[0]].at[index[1:]], sems.at[kx]
        )


def wait_out(source, sems):
    for j in range(2):
        wait_wide(source, sems, j)


def up_kernel(table, order, info, own, other, seed_t, *refs):
    parts = refs[0:2]
    hidden_out, slope_out = refs[2:4]
    keep = refs[4:6]
    w_up, grad, hidden, slope, sems, out_sems, side_sems = refs[6:]
    for copy in wide_copies(info, table, parts, w_up, sems):
        copy.start()
    outs = list(wide_out(info, order, keep, grad, out_sems))
    for j in range(2):
        wait_wide(w_up, sems, j)

        @pl.loop(0, 3)
        def _(chunk):
            at = pl.ds(pl.multiple_of(j * D + chunk * 256, 256), 256)
            sums = []
            for half, source in enumerate((own, other)):
                value, derivative = gelu_parts(dot(source[...], w_up[:, at]))
                value = value.astype(BF16)
                hidden[half, :, at] = value
                slope[half, :, at] = derivative.astype(BF16)
                sums.append(dot(seed_t[:, half * SEGL : (half + 1) * SEGL], value))
            grad[:, at] = (sums[0] + sums[1]).astype(BF16)
            for i, (source, target) in enumerate(((hidden, hidden_out), (slope, slope_out))):
                pltpu.make_async_copy(
                    source.at[:, :, at], target.at[:, :, at], side_sems.at[i]
                ).start()

        for owner, copy in outs:
            if owner == j:
                copy.start()
    wait_out(grad, out_sems)
    wait_whole(hidden, side_sems.at[0])
    wait_whole(slope, side_sems.at[1])


def down_kernel(tables, order, info, seed, own, other, slope_in, *refs):
    down_parts, up_parts = refs[0:2], refs[2:4]
    keep = refs[4:6]
    own_grad, other_grad = refs[6:8]
    w_down, w_up, grad, slope, total, normed_t, down_sems, up_sems, out_sems, side_sems = refs[8:]
    for copy in wide_copies(info, tables[0], down_parts, w_down, down_sems):
        copy.start()
    for copy in wide_copies(info, tables[1], up_parts, w_up, up_sems):
        copy.start()
    for j in range(2):
        at = pl.ds(j * D, D)
        pltpu.make_async_copy(slope_in.at[:, :, at], slope.at[:, :, at], side_sems.at[j]).start()
    outs = list(wide_out(info, order, keep, grad, out_sems))
    total[...] = jnp.zeros_like(total)
    normed_t[:, :SEGL] = flip(own[...]).astype(BF16)
    normed_t[:, SEGL:] = flip(other[...]).astype(BF16)
    for j in range(2):
        wait_wide(w_down, down_sems, j)
        wait_wide(w_up, up_sems, j)
        wait_whole(slope.at[:, :, pl.ds(j * D, D)], side_sems.at[j])

        @pl.loop(0, 3)
        def _(chunk):
            at = pl.ds(pl.multiple_of(j * D + chunk * 256, 256), 256)
            sums = []
            for half in range(2):
                back = dot(seed[half], w_down[:, at]).astype(BF16).astype(F32)
                back = (back * slope[half, :, at].astype(F32)).astype(BF16)
                sums.append(dot(normed_t[:, half * SEGL : (half + 1) * SEGL], back))
                total[half] += dot(back, w_up[:, at], 1, 1)
            grad[:, at] = (sums[0] + sums[1]).astype(BF16)

        for owner, copy in outs:
            if owner == j:
                copy.start()
    own_grad[...] = total[0]
    other_grad[...] = total[1].astype(BF16)
    wait_out(grad, out_sems)


def mix_back_kernel(table, order, info, own, other, seed, residual, gain, heads_out, dens_t, *refs):
    parts = refs[0:4]
    resid_grad, head_grad, coef_grad, gain_grad, bias_grad, keep, send = refs[4:11]
    w_out, grad, mix, mix_t, sem, out_sem = refs[11:]
    step = pl.program_id(0)

    @pl.when(step == 0)
    def _():
        for copy in narrow_copies(info, table, parts, [(48, w_out)], sem):
            copy.start()
        normed_grad = (own[...] + other[...].astype(F32)).astype(BF16).astype(F32)
        centred, scale = layer_stats(residual[...])
        unit = centred * scale
        gain_grad[...] = jnp.sum(normed_grad * unit, axis=0, keepdims=True)
        bias_grad[...] = jnp.sum(normed_grad, axis=0, keepdims=True)
        back = normed_grad * gain[...]
        back = back - jnp.mean(back, axis=-1, keepdims=True) - unit * jnp.mean(
            back * unit, axis=-1, keepdims=True
        )
        back = seed[...].astype(F32) + scale * back
        resid_grad[...] = back
        mix[...] = back.astype(BF16)
        mix_t[...] = flip(mix[...]).astype(BF16)
        wait_whole(w_out, sem)

        @pl.loop(0, 3)
        def _(chunk):
            at = pl.ds(aligned(chunk, 256), 256)
            head_grad[:, at] = dot(mix[...], w_out[:, at]).astype(BF16)
            grad[:, at] = dot(mix_t[...], heads_out[:, at]).astype(BF16)

        for copy in out_narrow(info, order, keep, send, [(0, grad)], out_sem):
            copy.start()

    pair_grad = head_grad[:, pl.ds(aligned(step, 128), 128)].astype(F32)
    sums = [
        dot(dens_t[h], jnp.where(half_lanes(h), pair_grad, 0.0).astype(BF16)) for h in range(2)
    ]
    coef_grad[...] = (sums[0] + sums[1]).astype(BF16)

    @pl.when(step == PAIRS - 1)
    def _():
        wait_whole(grad, out_sem)


def attend_back_kernel(
    attn_t, q, k, v, grad, local_t, dens_t, coef, gauss, *refs
):
    dq_out, dk_out, dv_out, gauss_grad, dq_t, dk_sum, dv_sum, rows_of = refs
    keys_t = flip(k[...]).astype(BF16)
    grad_t = flip(grad[...])
    logits = dot(gauss[0], q[...], 1, 1)
    centres = centre_column()
    gauss_columns = flip(gauss[0])
    dk_sum[...] = jnp.zeros_like(dk_sum)
    dv_sum[...] = jnp.zeros_like(dv_sum)
    rows_of[...] = jnp.zeros_like(rows_of)
    only = lambda h, value: jnp.where(half_lanes(h), value.astype(F32), 0.0).astype(BF16)
    for h in range(2):
        rows = slice(h * DH, (h + 1) * DH)
        values, queries, grads = only(h, v[...]), only(h, q[...]), only(h, grad[...])
        delta = jnp.sum(grad_t[rows] * local_t[rows], axis=0, keepdims=True)
        for block in range(2):
            n = 256 * (block + 1)
            at = slice(256 * block, n)
            probs = attn_t[h, :n, at]
            prob_grad = dot(values[:n], grad[at], 1, 1)
            score_grad = (probs.astype(F32) * (prob_grad - delta[:, at])).astype(BF16)
            dv_sum[:n] += dot(probs, grads[at])
            dk_sum[:n] += dot(score_grad, queries[at])
            dq_t[rows, at] = dot(keys_t[rows, :n], score_grad) * DH**-0.5
        mu, spread, var_logit = density_rows(logits, h)
        inverse = 1.0 / spread
        offset = mu - centres
        weighted = dot(only(h, coef[...]), grad[...], 1, 1) * dens_t[h].astype(F32)
        first = weighted * offset
        sum0 = jnp.sum(weighted, axis=0, keepdims=True)
        sum1 = jnp.sum(first, axis=0, keepdims=True)
        sum2 = jnp.sum(first * offset, axis=0, keepdims=True)
        mean_grad = -sum1 * inverse * mu * (1.0 - mu)
        spread_grad = 0.5 * inverse * (sum2 * inverse - sum0)
        var_grad = spread_grad * 0.05 * jax.nn.sigmoid(var_logit)
        rows_of[h : h + 1] = mean_grad
        rows_of[2 + h : 3 + h] = var_grad
        column = gauss_columns[rows]
        dq_t[rows] += column[:, h : h + 1] * mean_grad + column[:, 2 + h : 3 + h] * var_grad
    dq_out[...] = jnp.transpose(dq_t[...]).astype(BF16)
    dk_out[...] = (dk_sum[...] * DH**-0.5).astype(BF16)
    dv_out[...] = dv_sum[...]
    high = rows_of[...].astype(BF16)
    both = dot(high, q[...]) + dot((rows_of[...] - high.astype(F32)).astype(BF16), q[...])
    gauss_grad[0:1] = jnp.where(half_lanes(0), both[0:1], both[1:2])
    gauss_grad[1:2] = jnp.where(half_lanes(0), both[2:3], both[3:4])


def qkv_grad_kernel(orders, near, info, x, dq, dk, dv, coef_grad, ridge_t, *refs):
    if near:
        gauss_grad, gain_grad, bias_grad = refs[:3]
        layout = refs[3][...]
        refs = refs[4:]
    keep_qk, send_qk, keep_v, send_v, dv_out, x_t, gq, gk, gv, small, sems = refs
    x_t[...] = flip(x[...]).astype(BF16)
    scale = column_validity(info) * info[4].astype(F32)

    def weight(source, out):
        @pl.loop(0, 3)
        def _(chunk):
            at = pl.ds(aligned(chunk, 256), 256)
            out[:, at] = dot(x_t[...], source[:, at]).astype(BF16)

    weight(dq, gq)
    weight(dk, gk)
    for copy in out_narrow(info, orders[0], keep_qk, send_qk, [(0, gq), (48, gk)], sems.at[0]):
        copy.start()

    @pl.loop(0, 3)
    def _(chunk):
        at = pl.ds(aligned(chunk, 256), 256)
        pooled_grad = dot(ridge_t[...], coef_grad[:, at])
        dv_out[:, at] = (dv[:, at] + pooled_grad * scale).astype(BF16)
        gv[:, at] = dot(x_t[...], dv_out[:, at]).astype(BF16)

    for copy in out_narrow(info, orders[1], keep_v, send_v, [(0, gv)], sems.at[1]):
        copy.start()
    if near:
        table = scatter_table(orders[1])
        gauss_mask, scale_mask = small_masks(info, [(0,) + row for row in table], layout)
        rows = (
            (gauss_mask, gauss_grad[0:1]),
            (gauss_mask, gauss_grad[1:2]),
            (scale_mask, gain_grad[...]),
            (scale_mask, bias_grad[...]),
        )
        small[...] = jnp.zeros_like(small)
        small[:, :128] = sum(
            dot(jnp.where(mask, row, 0.0).astype(BF16), small_places(layout, i, 128), 1, 1)
            for i, (mask, row) in enumerate(rows)
        ).astype(BF16)
        for n, (index, _, _, kc) in enumerate(table):
            pltpu.make_async_copy(
                small.at[pl.ds(16 * n, 16)],
                (keep_v, send_v)[kc].at[index + (pl.ds(48, 16),)],
                sems.at[2],
            ).start()
        wait_whole(small, sems.at[2])
    both = pltpu.make_async_copy(gq, gq, sems.at[0])
    both.wait()
    both.wait()
    wait_whole(gv, sems.at[1])


def finish_kernel(tables, info, dq, dk, dv, resid_grad, hidden, residual, *refs):
    qk, v_parts, down_parts = refs[0:4], refs[4:8], refs[8:10]
    token_keep, token_send, fed_keep, fed_send = refs[10:14]
    wq, wk, wv, w_down, sems, down_sems = refs[14:]
    for copy in narrow_copies(info, tables[0], qk, [(0, wq), (48, wk)], sems.at[0]):
        copy.start()
    for copy in narrow_copies(info, tables[1], v_parts, [(0, wv)], sems.at[1]):
        copy.start()
    for copy in wide_copies(info, tables[2], down_parts, w_down, down_sems):
        copy.start()
    first = info[5] == 0

    def split(value):
        top, bottom = value[:HALF_SEG], value[HALF_SEG:]
        return jnp.where(first, top, bottom), jnp.where(first, bottom, top).astype(BF16)

    pair_wait = pltpu.make_async_copy(wq, wq, sems.at[0])
    pair_wait.wait()
    pair_wait.wait()
    wait_whole(wv, sems.at[1])

    @pl.loop(0, 3)
    def _(chunk):
        at = pl.ds(aligned(chunk, 256), 256)
        part = dot(dq[...], wq[at, :], 1, 1) + dot(dk[...], wk[at, :], 1, 1)
        value = resid_grad[:, at] + part + dot(dv[...], wv[at, :], 1, 1)
        token_keep[:, at], token_send[:, at] = split(value)

    wait_out(w_down, down_sems)

    @pl.loop(0, 3)
    def _(chunk):
        at = pl.ds(aligned(chunk, 256), 256)
        value = residual[:, at] + dot(hidden[0], w_down[at, :], 1, 1)
        fed_keep[0, :, at], fed_send[0, :, at] = split(value)
        value = dot(hidden[1], w_down[at, :], 1, 1)
        fed_keep[1, :, at], fed_send[1, :, at] = split(value)


FULL = pl.BlockSpec()
ANY = pl.BlockSpec(memory_space=pl.ANY)
SCALARS = pl.BlockSpec(memory_space=SMEM)
MATRIX = (D, D)
HALF = FF // 2
HALF_SEG = SEGL // 2
WIDE = (D, HALF)
DMA = pltpu.SemaphoreType.DMA


def shape(dims, dtype=BF16):
    return jax.ShapeDtypeStruct(dims, dtype)


def run(body, name, args, in_specs, outs, out_specs, scratch=(), grid=None, cost=5.0, vmem=48):
    kwargs = {} if grid is None else {"grid": grid}
    args = [
        value
        if spec is SCALARS
        else pltpu.with_memory_space_constraint(value, pltpu.HBM)
        for value, spec in zip(args, in_specs)
    ]
    return pl.pallas_call(
        body,
        name=name,
        out_shape=tuple(pltpu.HBM(out.shape, out.dtype) for out in outs),
        in_specs=list(in_specs),
        out_specs=tuple(out_specs),
        scratch_shapes=list(scratch),
        cost_estimate=pl.CostEstimate(
            flops=int(cost * 2e8), bytes_accessed=int(1e6), transcendentals=0
        ),
        compiler_params=pltpu.CompilerParams(vmem_limit_bytes=vmem * 1024 * 1024),
        **kwargs,
    )(*args)


PAIR_COLUMNS = pl.BlockSpec((SEGL, 128), lambda p: (0, p))
PAIR_ROWS = pl.BlockSpec((128, SEGL), lambda p: (p, 0))
PAIR_COEF = pl.BlockSpec((NB, 128), lambda p: (0, p))
PAIR_ATTN = pl.BlockSpec((2, SEGL, SEGL), lambda p: (p, 0, 0))
PAIR_DENS = pl.BlockSpec((2, NB, SEGL), lambda p: (p, 0, 0))


def pair_block(*dims):
    return pl.BlockSpec((1,) + dims, lambda p: (p, 0, 0))


ORDER_QK, ORDER_V, ORDER_UP, ORDER_DOWN = "zyx", "zxy", "zxy", "zxy"
BACK_QK, BACK_V, BACK_UP, BACK_DOWN = "xyz", "yxz", "xyz", "yxz"


def local(
    tokens, lengths, mem_mask, cotangent, w_qkv, w_gauss, w_out, ln_gain, ln_bias, w_up, w_down
):
    dp_count = lax.axis_size("dp")
    dp, rank = lax.axis_index("dp"), lax.axis_index("tensor")
    core, segment = rank % 2, rank // 2
    near = dp_count == 8
    gauss_size, gain_size = w_gauss.size, ln_gain.size
    ridge = ridge_matrix()

    used = [
        jnp.clip(lax.dynamic_index_in_dim(lengths, at, 0, False) - segment * SEGL, 0, SEGL)
        for at in (core, 1 - core)
    ]
    pair = lax.dynamic_index_in_dim(mem_mask, core, 0, False)[1, 0]
    where = (dp, segment, core) if near else (0, 0, 0)
    info = jnp.stack([jnp.asarray(value, jnp.int32) for value in where + (used[0], pair, core)])

    own, other = to_segment_parts(tokens)
    theirs = swap(cotangent)
    everything = jnp.where(
        core == 0,
        jnp.concatenate([cotangent, theirs], axis=1),
        jnp.concatenate([theirs, cotangent], axis=1),
    )
    seed = jnp.stack(
        [lax.dynamic_index_in_dim(everything, at, 0, False) for at in (core, 1 - core)]
    )
    seed = jnp.stack(
        [
            jnp.where(jnp.arange(SEGL)[:, None] < count, part, 0.0).astype(BF16)
            for count, part in zip(used, seed)
        ]
    )
    seed_t = seed.reshape(2 * SEGL, D).T

    projections = jnp.concatenate([w_qkv, w_out.T[None]])
    if near:
        mine = lax.dynamic_slice_in_dim(projections, core * 48, 48, axis=1)
        partner = swap(lax.dynamic_slice_in_dim(projections, (1 - core) * 48, 48, axis=1))
        projections = jnp.where(
            core == 0,
            jnp.concatenate([mine, partner], axis=2),
            jnp.concatenate([partner, mine], axis=2),
        )
        small = jnp.concatenate(
            [w_gauss.reshape(-1)] + exact_triple(jnp.concatenate([ln_gain, ln_bias]))
        )
        small_rows = jnp.pad(small[None], ((0, 15), (0, 384 - small.size)))
        packed = jnp.concatenate([projections.reshape(192, 384), small_rows])
        along_z = spread(after(packed, other, theirs), "z")
        along_z[1] = after(along_z[1], seed, seed_t)
        qk_near = jnp.stack(spread(jnp.stack([part[:96] for part in along_z]), "y"))
        v_near = jnp.stack(spread(jnp.stack([part[96:] for part in along_z]), "x"))
        qk_far, v_far = xor_permute(qk_near, "x", 1), xor_permute(v_near, "y", 1)
        qk_swap, v_swap = swap(qk_near), swap(v_near)
        up_z = spread(after(w_up, qk_swap, v_swap), "z")
        qk_parts = [qk_near, qk_far, qk_swap, swap(after(qk_far, *up_z[1:]))]
        v_parts = [v_near, v_far, v_swap, swap(after(v_far, *up_z[1:]))]
        up_x = spread(after(jnp.stack(up_z), qk_parts[3], v_parts[3]), "x")
        down_z = spread(after(w_down.T, qk_parts[3], v_parts[3]), "z")
    else:
        every = lambda value: lax.all_gather(value, AXES, axis=0)
        cut = lambda value: value.reshape((8, dp_count // 8) + value.shape[1:])
        both = cut(every(projections).reshape(dp_count, 4, 4, -1, 192))
        both = both.transpose(0, 3, 1, 4, 2, 5).reshape(8, 4, 2, 48, 2, 384)
        both = both.transpose(0, 4, 2, 1, 3, 5)
        qk_parts = as_gathered(both[:, :, :, :2].reshape(8, 2, 2, 96, 384), ORDER_QK)
        v_parts = as_gathered(
            jnp.pad(both[:, :, :, 2:].reshape(8, 2, 2, 96, 384), ((0, 0),) * 3 + ((0, 16), (0, 0))),
            ORDER_V,
        )

        def wide(value):
            value = cut(every(value).reshape(dp_count, 4, -1, D)).transpose(0, 2, 1, 3, 4)
            value = value.reshape(8, 2, 2, 96, D)
            return lax.dynamic_slice_in_dim(value, core, 1, axis=2)

        double = lambda value: jnp.concatenate([value, value], axis=2)
        up_parts = as_gathered(double(wide(w_up)), ORDER_UP)[:2]
        down_parts = as_gathered(double(wide(w_down.T)), ORDER_DOWN)[:2]
    table_qk, table_v = piece_table(ORDER_QK), piece_table(ORDER_V)
    table_up, table_down = piece_table(ORDER_UP, 1), piece_table(ORDER_DOWN, 1)

    tall = shape((SEGL, D))
    row = shape((1, D), F32)
    small_in, small_out = [], []
    if near:
        small_in = [jnp.asarray(small_layout())]
        small_out = [shape((PAIRS, 16, 128)), row, row]
    x, q, k, v, coef, *small_params = run(
        functools.partial(qkv_kernel, table_qk, table_v, near),
        "qkv",
        [info, own, other, jnp.asarray(ridge)] + qk_parts + v_parts + small_in,
        [SCALARS, FULL, FULL, FULL] + [ANY] * 8 + [FULL] * len(small_in),
        [tall] * 4 + [shape((NB, D))] + small_out,
        [FULL] * (5 + len(small_out)),
        [VMEM(MATRIX, BF16)] * 3 + [VMEM((512, 384), BF16), DMA((3,))],
        cost=6.0,
        vmem=24,
    )
    coef = lax.ppermute(coef, "tensor", [(0, 2), (1, 3)])

    q_late = q
    if near:
        q_late = after(q, up_x[1])
        up_parts = spread(after(jnp.stack(up_x), q), "y")
        gauss_rows, norm_gain, norm_bias = small_params
    else:
        scales = every(jnp.stack([ln_gain, ln_bias]))
        gauss_parts = every(w_gauss.reshape(-1))
        norm_gain, norm_bias = scales[:, 0].reshape(1, D), scales[:, 1].reshape(1, D)
        gauss = gauss_parts.reshape(dp_count, 4, 2, 3, -1).transpose(2, 1, 3, 0, 4)
        gauss = gauss.reshape(2, PAIRS, 2, DH)
        spread_rows = jnp.eye(2, dtype=BF16)[None, None, :, :, None] * gauss[:, :, :, None, :]
        gauss_rows = spread_rows.transpose(1, 0, 2, 3, 4).reshape(PAIRS, 4, 128)
        gauss_rows = jnp.pad(gauss_rows, ((0, 0), (0, 12), (0, 0)))

    attn_t, local_t, dens_t = run(
        attend_kernel,
        "attend",
        [info, q_late, k, v, gauss_rows],
        [SCALARS] + [PAIR_COLUMNS] * 3 + [pair_block(16, 128)],
        [shape((H, SEGL, SEGL)), shape((D, SEGL), F32), shape((H, NB, SEGL))],
        [PAIR_ATTN, PAIR_ROWS, PAIR_DENS],
        [VMEM((SEGL, SEGL), F32)],
        grid=(PAIRS,),
        cost=12.0,
        vmem=14,
    )
    if near:
        down_z[1:] = lax.optimization_barrier((attn_t, coef, up_parts[1], *down_z[1:]))[3:]
        down_x = spread(jnp.stack(down_z), "x")
    whole = lambda *dims: pl.BlockSpec(dims, lambda p: (0,) * len(dims))
    heads_out, residual, normed = run(
        functools.partial(recall_kernel, table_v),
        "recall",
        [info, dens_t, coef, local_t, x, norm_gain, norm_bias] + v_parts,
        [SCALARS, PAIR_DENS, PAIR_COEF, PAIR_ROWS, whole(SEGL, D), whole(1, D), whole(1, D)]
        + [ANY] * 4,
        [tall, shape((SEGL, D), F32), tall],
        [whole(SEGL, D)] * 3,
        [VMEM(MATRIX, BF16), DMA(())],
        grid=(PAIRS,),
        cost=7.0,
        vmem=18,
    )
    if near:
        down_parts = spread(after(jnp.stack(down_x), normed), "y")
    normed_other = swap(normed)
    piece_dims = lambda order: tuple(SIZES[letter] for letter in order)
    hidden, slope, *keep_down = run(
        functools.partial(up_kernel, table_up, BACK_DOWN),
        "up",
        [info, normed, normed_other, seed_t] + up_parts,
        [SCALARS, FULL, FULL, FULL] + [ANY] * 2,
        [shape((2, SEGL, HALF))] * 2 + [shape(piece_dims(BACK_DOWN)[1:] + (96, D))] * 2,
        [ANY] * 4,
        [VMEM(WIDE, BF16)] * 2 + [VMEM((2, SEGL, HALF), BF16)] * 2 + [DMA((2,))] * 3,
        cost=12.0,
        vmem=22,
    )
    if near:
        down_1 = stage(lambda k: keep_down[k], BACK_DOWN[0])
    *keep_up, own_grad, other_grad = run(
        functools.partial(down_kernel, (table_down, table_up), BACK_UP),
        "down",
        [info, seed, normed, normed_other, slope] + down_parts + up_parts,
        [SCALARS] + [FULL] * 3 + [ANY] * 5,
        [shape(piece_dims(BACK_UP)[1:] + (96, D))] * 2 + [shape((SEGL, D), F32), tall],
        [ANY] * 2 + [FULL] * 2,
        [VMEM(WIDE, BF16)] * 3
        + [VMEM((2, SEGL, HALF), BF16), VMEM((2, SEGL, D), F32), VMEM((D, 2 * SEGL), BF16)]
        + [DMA((2,))] * 4,
        cost=15.0,
        vmem=30,
    )
    if near:
        up_1 = stage(lambda k: keep_up[k], BACK_UP[0])
        own_grad = after(own_grad, *down_1[1])
    other_grad = swap(other_grad)
    narrow_grad = [shape(piece_dims(BACK_V) + (48, 384))] * 2
    resid_grad, head_grad, coef_grad, gain_part, bias_part, keep_out, send_out = run(
        functools.partial(mix_back_kernel, table_v, BACK_V),
        "mix_back",
        [info, own_grad, other_grad, seed[0], residual, norm_gain, heads_out, dens_t] + v_parts,
        [SCALARS]
        + [whole(SEGL, D)] * 4
        + [whole(1, D), whole(SEGL, D), PAIR_DENS]
        + [ANY] * 4,
        [shape((SEGL, D), F32), tall, shape((NB, D)), row, row] + narrow_grad,
        [whole(SEGL, D), whole(SEGL, D), PAIR_COEF, whole(1, D), whole(1, D)] + [ANY] * 2,
        [VMEM(MATRIX, BF16)] * 2
        + [VMEM((SEGL, D), BF16), VMEM((D, SEGL), BF16)]
        + [DMA(())] * 2,
        grid=(PAIRS,),
        cost=6.0,
        vmem=26,
    )
    coef_grad = lax.ppermute(coef_grad, "tensor", [(2, 0), (3, 1)])
    if near:
        got_out = swap(send_out)
    dq, dk, dv, gauss_grad = run(
        attend_back_kernel,
        "attend_back",
        [attn_t, q, k, v, head_grad, local_t, dens_t, coef, gauss_rows],
        [PAIR_ATTN]
        + [PAIR_COLUMNS] * 4
        + [PAIR_ROWS, PAIR_DENS, PAIR_COEF, pair_block(16, 128)],
        [tall, tall, shape((SEGL, D), F32), shape((2, D), F32)],
        [PAIR_COLUMNS] * 3 + [pl.BlockSpec((2, 128), lambda p: (0, p))],
        [
            VMEM((128, SEGL), F32),
            VMEM((SEGL, 128), F32),
            VMEM((SEGL, 128), F32),
            VMEM((16, SEGL), F32),
        ],
        grid=(PAIRS,),
        cost=16.0,
        vmem=16,
    )
    if near:
        up_1 = (up_1[0], [after(a, dk, coef_grad, got_out) for a in up_1[1]])
        dq = after(dq, *up_1[1])
        down_1 = (down_1[0], [after(a, *up_1[1]) for a in down_1[1]])
        down_2 = stage(combined(*down_1), BACK_DOWN[1])
        up_2 = stage(combined(*up_1), BACK_UP[1])
    keep_qk, send_qk, keep_v, send_v, dv = run(
        functools.partial(qkv_grad_kernel, (BACK_QK, BACK_V), near),
        "qkv_grad",
        [info, x, dq, dk, dv, coef_grad, jnp.asarray(ridge.T)]
        + ([gauss_grad, gain_part, bias_part] + small_in if near else []),
        [SCALARS] + [FULL] * (10 if near else 6),
        [shape(piece_dims(BACK_QK) + (96, 384))] * 2
        + [shape(piece_dims(BACK_V) + (64, 384))] * 2
        + [tall],
        [ANY] * 4 + [FULL],
        [VMEM((D, SEGL), BF16)] + [VMEM(MATRIX, BF16)] * 3 + [VMEM((512, 384), BF16), DMA((3,))],
        cost=6.0,
        vmem=26,
    )

    if near:
        send_qk = after(send_qk, *down_2[1], *up_2[1])
        send_v = after(send_v, *down_2[1], *up_2[1])
        got_qk, got_v = swap(send_qk), swap(send_v)
        first_qk = [keep_qk[k].astype(F32) + got_qk[k].astype(F32) for k in range(2)]
        rest = ((keep_out, got_out), (keep_v, got_v))
        first_v = [
            jnp.concatenate([a[k].astype(F32) + b[k].astype(F32) for a, b in rest], axis=2)
            for k in range(2)
        ]
        first_qk[1], first_v[1] = first_qk[1].astype(BF16), first_v[1].astype(BF16)
        qk_1 = stage(lambda k: first_qk[k], BACK_QK[0])
        v_1 = stage(lambda k: first_v[k], BACK_V[0])
        down_2 = (down_2[0], [after(a, first_qk[1], first_v[1]) for a in down_2[1]])
        to_down, to_up = combined(*down_2), combined(*up_2)
        wide = [jnp.concatenate([to_down(k), to_up(k)]) for k in range(4)]
        wide[1:] = [value.astype(BF16) for value in wide[1:]]
        wide_3 = stage(lambda k: wide[k], "z")
        dq_late = after(dq, first_qk[1], first_v[1], *wide[1:])
    else:
        dq_late = dq

    token_keep, token_send, fed_keep, fed_send = run(
        functools.partial(finish_kernel, (table_qk, table_v, table_down)),
        "finish",
        [info, dq_late, dk, dv, resid_grad, hidden, residual] + qk_parts + v_parts + down_parts,
        [SCALARS] + [FULL] * 6 + [ANY] * 10,
        [shape((HALF_SEG, D), F32), shape((HALF_SEG, D))]
        + [shape((2, HALF_SEG, D), F32), shape((2, HALF_SEG, D))],
        [FULL] * 4,
        [VMEM(MATRIX, BF16)] * 3 + [VMEM(WIDE, BF16)] + [DMA((2,))] * 2,
        cost=14.0,
        vmem=32,
    )
    token_got, fed_got = swap(token_send).astype(F32), swap(fed_send).astype(F32)
    own_rows, their_rows = fed_keep[0] + fed_got[1], fed_keep[1] + fed_got[0]
    by_sequence = lambda mine, theirs: jnp.where(
        core == 0, jnp.stack([mine, theirs]), jnp.stack([theirs, mine])
    )
    output = by_sequence(own_rows, their_rows)
    grad_tokens = by_sequence(token_keep, token_got)

    if near:
        qk_2 = stage(combined(*qk_1), BACK_QK[1])
        v_2 = stage(combined(*v_1), BACK_V[1])
        to_qk, to_v = combined(*qk_2), combined(*v_2)
        joined = final_sum(*stage(lambda k: jnp.concatenate([to_qk(k), to_v(k)]), "z"))
        own_small = joined[192]
        narrow = joined[:192].reshape(4, 48, 384)
        mine = lax.dynamic_slice_in_dim(narrow, core * 192, 192, axis=2)
        partner = swap(lax.dynamic_slice_in_dim(narrow, (1 - core) * 192, 192, axis=2))
        narrow = jnp.where(
            core == 0,
            jnp.concatenate([mine, partner], axis=1),
            jnp.concatenate([partner, mine], axis=1),
        )
        own_wide = final_sum(*wide_3)
        own_up, own_down = own_wide[96:], own_wide[:96].T
    else:
        gauss_grad = gauss_grad.reshape(2, 4, 3, dp_count, -1).transpose(3, 1, 0, 2, 4)
        small_grads = jnp.concatenate(
            [value.reshape(dp_count * 4, -1) for value in (gauss_grad, gain_part, bias_part)],
            axis=1,
        )
        own_small = lax.psum_scatter(small_grads, AXES, scatter_dimension=0)
        pieces = [
            whole_from([keep_qk, send_qk], BACK_QK).reshape(8, 2, 2, 2, 48, 384),
            whole_from([keep_out, send_out], BACK_V)[:, :, :, None],
            whole_from([keep_v, send_v], BACK_V)[:, :, :, None, :48],
        ]
        pieces = jnp.concatenate(pieces, axis=3).transpose(0, 2, 4, 3, 1, 5)
        pieces = pieces.reshape(dp_count, D // dp_count, 4, 4, 192).transpose(0, 3, 2, 1, 4)
        total = lambda value: lax.psum_scatter(value.astype(F32), AXES, scatter_dimension=0)
        narrow = total(pieces.reshape((-1,) + pieces.shape[2:]))

        def owned(keep, order):
            mine = whole_from([jnp.stack(keep)], order)
            both = jnp.concatenate(
                [jnp.where(core == at, mine, jnp.zeros_like(mine)) for at in range(2)], axis=2
            )
            both = both.transpose(0, 3, 1, 2, 4).reshape(dp_count, D // dp_count, 4, D)
            both = both.transpose(0, 2, 1, 3)
            return total(both.reshape((-1,) + both.shape[2:]))

        own_up, own_down = owned(keep_up, BACK_UP), owned(keep_down, BACK_DOWN).T
    own_qkv, own_out = jnp.concatenate([narrow[:2], narrow[3:]]), narrow[2].T
    return (
        output,
        grad_tokens,
        own_qkv,
        own_small[:gauss_size].reshape(w_gauss.shape),
        own_out,
        own_small[gauss_size : gauss_size + gain_size],
        own_small[gauss_size + gain_size : gauss_size + 2 * gain_size],
        own_up,
        own_down,
    )


def solution(mesh):
    return jax.shard_map(
        local,
        mesh=mesh,
        in_specs=(
            P("dp", "tensor", None),
            P("dp"),
            P("dp", None, None),
            P("dp", "tensor", None),
            P(None, "dp", "tensor"),
            P(None, "tensor", "dp"),
            P("tensor", "dp"),
            P(("dp", "tensor")),
            P(("dp", "tensor")),
            P("dp", "tensor"),
            P("tensor", "dp"),
        ),
        out_specs=(
            P("dp", "tensor", None),
            P("dp", "tensor", None),
            P(None, "dp", "tensor"),
            P(None, "tensor", "dp"),
            P("tensor", "dp"),
            P(("dp", "tensor")),
            P(("dp", "tensor")),
            P("dp", "tensor"),
            P("tensor", "dp"),
        ),
        check_vma=False,
    )
```

```python
import functools

import jax
import jax.numpy as jnp
import numpy as np
from jax import lax
from jax.experimental import pallas as pl
from jax.experimental.pallas import tpu as pltpu
from jax.sharding import PartitionSpec as P

D = 768
H = 12
DH = 64
NB = 256
SEGL = 512
FF = 3072
PAIRS = H // 2
AXES = ("dp", "tensor")
F32 = jnp.float32
BF16 = jnp.bfloat16
BASIS_VAR = (1.0 / NB) ** 2
VMEM = pltpu.VMEM
SMEM = pltpu.SMEM


def ridge_matrix():
    centres = (np.arange(NB) + 0.5) / NB
    samples = (np.arange(SEGL) + 0.5) / SEGL
    rows = np.exp(-0.5 * ((samples[None, :] - centres[:, None]) * NB) ** 2)
    gram = rows @ rows.T + 0.5 * np.eye(NB)
    return np.linalg.solve(gram, rows).astype(np.float32).astype(jnp.bfloat16)


SIZES = {"z": 4, "y": 2, "x": 2, "c": 2}


def xor_permute(value, letter, k):
    dp_mask, tensor_mask = {"z": (2 * k, 0), "y": (k, 0), "x": (0, 2 * k), "c": (0, k)}[letter]
    dp_count, rank_count = lax.axis_size("dp"), lax.axis_size("tensor")
    pairs = [
        (d * rank_count + t, (d ^ dp_mask) * rank_count + (t ^ tensor_mask))
        for d in range(dp_count)
        for t in range(rank_count)
    ]
    return lax.ppermute(value, AXES, pairs)


def swap(value):
    return xor_permute(value, "c", 1)


def after(value, *others):
    return lax.optimization_barrier((value,) + others)[0]


def piece_table(order, cores=2):
    first, second, third = order
    table = []
    for at, (kc, k3) in enumerate([(0, 0), (0, 1), (1, 0), (1, 1)][: 2 * cores]):
        for i2 in range(SIZES[second]):
            for i1 in range(SIZES[first]):
                k = {first: i1, second: i2, third: k3}
                table.append((at, (i2, i1), k["z"] * 2 + k["y"], k["x"], kc))
    return table


def wide_table():
    return [
        (2 * ky + kx, (kz,), 2 * kz + ky, kx, 0)
        for ky in range(2)
        for kx in range(2)
        for kz in range(4)
    ]


def spread(piece, letter):
    return [piece] + [xor_permute(piece, letter, k) for k in range(1, SIZES[letter])]


def as_gathered(whole, order):
    first, second, third = order
    whole = whole.reshape((4, 2) + whole.shape[1:])
    at = {"z": 0, "y": 1, "x": 2, "c": 3}
    rest = list(range(4, whole.ndim))
    whole = whole.transpose([at["c"], at[third], at[second], at[first]] + rest)
    return [whole[0, 0], whole[0, 1], whole[1, 0], whole[1, 1]]


def stage(total, letter):
    own = total(0)
    arrived = [xor_permute(total(k).astype(BF16), letter, k) for k in range(1, SIZES[letter])]
    return own, arrived


def combined(own, arrived):
    return lambda k: sum((a[k].astype(F32) for a in arrived), own[k].astype(F32))


def final_sum(own, arrived):
    return sum((a.astype(F32) for a in arrived), own)


def whole_from(parts, order):
    first, second, third = order
    whole = jnp.stack(parts)
    at = {"c": 0, first: 1, second: 2, third: 3}
    rest = list(range(4, whole.ndim))
    whole = whole.transpose([at["z"], at["y"], at["x"], at["c"]] + rest)
    return whole.reshape((8,) + whole.shape[2:])


def to_segment_parts(local):
    core = lax.axis_index("tensor") % 2
    own = lax.dynamic_index_in_dim(local, core, 0, keepdims=False)
    return own, swap(lax.dynamic_index_in_dim(local, 1 - core, 0, keepdims=False))


def exact_triple(value):
    high = lax.reduce_precision(value, 8, 7)
    middle = lax.reduce_precision(value - high, 8, 7)
    return [part.astype(BF16) for part in (high, middle, value - high - middle)]


def dot(left, right, left_dim=1, right_dim=0):
    return lax.dot_general(
        left, right, (((left_dim,), (right_dim,)), ((), ())), preferred_element_type=F32
    )


def flip(value):
    return jnp.transpose(value.astype(F32))


def aligned(value, step):
    return pl.multiple_of(value * step, step)


def wide_copies(info, table, arrays, target, sems):
    for at, index, r, kx, _ in table:
        rows = pl.ds(aligned(info[0] ^ r, 96), 96)
        yield pltpu.make_async_copy(
            arrays[at].at[index], target.at[rows, pl.ds(kx * D, D)], sems.at[kx]
        )


def wait_wide(target, sems, j):
    block = target.at[:, pl.ds(j * D, D)]
    pltpu.make_async_copy(block, block, sems.at[j]).wait()


def narrow_copies(info, table, arrays, spots, sem):
    for at, index, r, kx, kc in table:
        rows = pl.ds(pl.multiple_of((info[0] ^ r) * 96 + (info[2] ^ kc) * 48, 48), 48)
        columns = pl.ds(aligned(info[1] ^ kx, 384), 384)
        for first, target in spots:
            yield pltpu.make_async_copy(
                arrays[at].at[index + (pl.ds(first, 48),)], target.at[rows, columns], sem
            )


def wait_whole(target, sem):
    pltpu.make_async_copy(target, target, sem).wait()


def out_narrow(info, order, keep, send, spots, sem):
    for index, r, kx, kc in scatter_table(order):
        rows = pl.ds(pl.multiple_of((info[0] ^ r) * 96 + (info[2] ^ kc) * 48, 48), 48)
        columns = pl.ds(aligned(info[1] ^ kx, 384), 384)
        for first, source in spots:
            yield pltpu.make_async_copy(
                source.at[rows, columns], (keep, send)[kc].at[index + (pl.ds(first, 48),)], sem
            )


def scatter_table(order, cores=2):
    a, b, c = order
    table = []
    for kc in range(cores):
        for i in range(SIZES[a]):
            for j in range(SIZES[b]):
                for l in range(SIZES[c]):
                    k = {a: i, b: j, c: l}
                    table.append(((i, j, l), k["z"] * 2 + k["y"], k["x"], kc))
    return table


def column_validity(info):
    return (lax.broadcasted_iota(jnp.int32, (SEGL, 1), 0) < info[3]).astype(F32)


def small_layout():
    column = np.arange(D)
    owner = [(column % DH // 8) * 4 + column // 192, column // 24]
    place = [column // DH % 3 * 8 + column % 8, 48 + column % 24]
    return np.stack(owner + place + [column] * 4).astype(np.int32)


def small_places(layout, i, count):
    row = lax.broadcasted_iota(jnp.int32, (count, D), 0)
    place = layout[2 + i // 2][None] + 24 * (i % 2)
    hit = row == place
    if i > 1 and count > 128:
        hit = hit | (row == place + 48) | (row == place + 96)
    return hit.astype(F32).astype(BF16)


def small_masks(info, table, owner):
    row = lax.broadcasted_iota(jnp.int32, (512, D), 0)
    device = row * 0 - 1
    me = info[0] * 4 + info[1] * 2 + info[2]
    for n, (_, _, r, kx, kc) in enumerate(table):
        device = jnp.where(row == 16 * n, me ^ (r * 4 + kx * 2 + kc), device)
    return device == owner[0:1], device == owner[1:2]


def qkv_kernel(table_qk, table_v, near, info, own, other, ridge, *refs):
    qk, v_parts = refs[0:4], refs[4:8]
    if near:
        layout = refs[8][...]
        refs = refs[:8] + refs[9:]
    x_out, q_out, k_out, v_out, coef_out = refs[8:13]
    if near:
        gauss_out, gain_out, bias_out = refs[13:16]
        refs = refs[:13] + refs[16:]
    wq, wk, wv, small, sems = refs[13:]
    copies = list(narrow_copies(info, table_qk, qk, [(0, wq), (48, wk)], sems.at[0]))
    copies += list(narrow_copies(info, table_v, v_parts, [(0, wv)], sems.at[1]))
    if near:
        for n, (at, index, _, _, _) in enumerate(table_v):
            copies.append(
                pltpu.make_async_copy(
                    v_parts[at].at[index + (pl.ds(96, 16),)], small.at[pl.ds(16 * n, 16)], sems.at[2]
                )
            )
    for copy in copies:
        copy.start()
    core = info[5]
    x_out[pl.ds(aligned(core, 256), 256), :] = own[...]
    x_out[pl.ds(aligned(1 - core, 256), 256), :] = other[...]
    scale = column_validity(info) * info[4].astype(F32)
    pair_wait = pltpu.make_async_copy(wq, wq, sems.at[0])
    pair_wait.wait()
    pair_wait.wait()

    def project(w, out):
        @pl.loop(0, 3)
        def _(step):
            at = pl.ds(aligned(step, 256), 256)
            out[:, at] = dot(x_out[...], w[:, at]).astype(BF16)

    project(wq, q_out)
    project(wk, k_out)
    wait_whole(wv, sems.at[1])

    @pl.loop(0, 3)
    def _(step):
        at = pl.ds(aligned(step, 256), 256)
        values = dot(x_out[...], wv[:, at]).astype(BF16)
        v_out[:, at] = values
        pooled = (values.astype(F32) * scale).astype(BF16)
        coef_out[:, at] = dot(ridge[...], pooled).astype(BF16)

    if near:
        wait_whole(small, sems.at[2])
        gauss_mask, scale_mask = small_masks(info, table_v, layout)
        rows = small[:, :256]

        def collect(at, mask):
            return jnp.sum(jnp.where(mask, dot(rows, small_places(layout, at, 256)), 0.0), axis=0, keepdims=True)

        means, variances = collect(0, gauss_mask), collect(1, gauss_mask)
        gain_out[...] = collect(2, scale_mask)
        bias_out[...] = collect(3, scale_mask)
        row = lax.broadcasted_iota(jnp.int32, (16, 128), 0)
        for p in range(PAIRS):
            at = slice(128 * p, 128 * (p + 1))
            value = jnp.where(row < 2, means[:, at], variances[:, at])
            for h in range(2):
                value = jnp.where((row % 2 == h) & ~half_lanes(h), 0.0, value)
            gauss_out[p] = jnp.where(row < 4, value, 0.0).astype(BF16)


def density_rows(logits, h):
    mean_logit, var_logit = logits[h : h + 1], logits[2 + h : 3 + h]
    mu = jax.nn.sigmoid(mean_logit)
    softplus = jnp.maximum(var_logit, 0.0) + jnp.log1p(jnp.exp(-jnp.abs(var_logit)))
    return mu, 0.05 * softplus + BASIS_VAR, var_logit


def centre_column():
    return (lax.broadcasted_iota(jnp.int32, (NB, 1), 0).astype(F32) + 0.5) / NB


def half_lanes(h):
    lane = lax.broadcasted_iota(jnp.int32, (1, 128), 1)
    return (lane < DH) if h == 0 else (lane >= DH)


def attend_kernel(info, q, k, v, gauss, attn_t, local_t, dens_t, bias):
    @pl.when(pl.program_id(0) == 0)
    def _():
        key = lax.broadcasted_iota(jnp.int32, (SEGL, SEGL), 0)
        query = lax.broadcasted_iota(jnp.int32, (SEGL, SEGL), 1)
        allowed = ((key < query) & (key < info[3])) | (key == query)
        bias[...] = jnp.where(allowed, 0.0, -1e30)

    values_t = flip(v[...]).astype(BF16)
    logits = dot(gauss[0], q[...], 1, 1)
    centres = centre_column()
    for h in range(2):
        rows = slice(h * DH, (h + 1) * DH)
        keys = jnp.where(half_lanes(h), k[...].astype(F32) * DH**-0.5, 0.0).astype(BF16)
        for block in range(2):
            n = 256 * (block + 1)
            at = slice(256 * block, n)
            scores = dot(keys[:n], q[at], 1, 1) + bias[:n, at]
            exponent = jnp.exp(scores - jnp.max(scores, axis=0, keepdims=True))
            total = jnp.sum(exponent, axis=0, keepdims=True)
            probs = (exponent * (1.0 / total)).astype(BF16)
            attn_t[h, :n, at] = probs
            local_t[rows, at] = dot(values_t[rows, :n], probs)
        mu, spread, _ = density_rows(logits, h)
        offset = mu - centres
        dens_t[h] = (
            jnp.sqrt(BASIS_VAR / spread) * jnp.exp(offset * offset * (-0.5 / spread))
        ).astype(BF16)


def layer_stats(residual):
    mean = jnp.mean(residual, axis=-1, keepdims=True)
    centred = residual - mean
    return centred, lax.rsqrt(jnp.mean(centred * centred, axis=-1, keepdims=True) + 1e-05)


def recall_kernel(table, info, dens_t, coef, local_t, x, gain, bias, *refs):
    parts = refs[0:4]
    heads_out, residual, normed = refs[4:7]
    w_out, sem = refs[7:]
    step = pl.program_id(0)

    @pl.when(step == 0)
    def _():
        for copy in narrow_copies(info, table, parts, [(48, w_out)], sem):
            copy.start()

    coef_t = flip(coef[...]).astype(BF16)
    recalled = [dot(coef_t[h * DH : (h + 1) * DH], dens_t[h]) for h in range(2)]
    both = local_t[...] + jnp.concatenate(recalled, axis=0)
    heads_out[:, pl.ds(aligned(step, 128), 128)] = flip(both).astype(BF16)

    @pl.when(step == PAIRS - 1)
    def _():
        wait_whole(w_out, sem)

        @pl.loop(0, 3)
        def _(chunk):
            at = pl.ds(aligned(chunk, 256), 256)
            residual[:, at] = x[:, at].astype(F32) + dot(heads_out[...], w_out[at, :], 1, 1)

        centred, scale = layer_stats(residual[...])
        normed[...] = (centred * scale * gain[...] + bias[...]).astype(BF16)


def gelu_parts(pre):
    c0, c1 = 0.7978845608028654, 0.044715
    square = pre * pre
    inner = jnp.tanh(c0 * pre * (1.0 + c1 * square))
    half = 0.5 * (1.0 + inner)
    slope = half + 0.5 * pre * (1.0 - inner * inner) * (c0 * (1.0 + 3.0 * c1 * square))
    return pre * half, slope


def wide_out(info, order, keep, source, sems):
    for index, r, kx, _ in scatter_table(order, 1):
        rows = pl.ds(aligned(info[0] ^ r, 96), 96)
        yield kx, pltpu.make_async_copy(
            source.at[rows, pl.ds(kx * D, D)], keep[index[0]].at[index[1:]], sems.at[kx]
        )


def wait_out(source, sems):
    for j in range(2):
        wait_wide(source, sems, j)


def up_kernel(table, order, info, own, other, seed_t, *refs):
    parts = refs[0:4]
    hidden_out, slope_out = refs[4:6]
    keep = refs[6:8]
    w_up, grad, hidden, slope, sems, out_sems, side_sems = refs[8:]
    for copy in wide_copies(info, table, parts, w_up, sems):
        copy.start()
    outs = list(wide_out(info, order, keep, grad, out_sems))
    for j in range(2):
        wait_wide(w_up, sems, j)

        @pl.loop(0, 3)
        def _(chunk):
            at = pl.ds(pl.multiple_of(j * D + chunk * 256, 256), 256)
            sums = []
            for half, source in enumerate((own, other)):
                value, derivative = gelu_parts(dot(source[...], w_up[:, at]))
                value = value.astype(BF16)
                hidden[half, :, at] = value
                slope[half, :, at] = derivative.astype(BF16)
                sums.append(dot(seed_t[:, half * SEGL : (half + 1) * SEGL], value))
            grad[:, at] = (sums[0] + sums[1]).astype(BF16)
            for i, (source, target) in enumerate(((hidden, hidden_out), (slope, slope_out))):
                pltpu.make_async_copy(
                    source.at[:, :, at], target.at[:, :, at], side_sems.at[i]
                ).start()

        for owner, copy in outs:
            if owner == j:
                copy.start()
    wait_out(grad, out_sems)
    wait_whole(hidden, side_sems.at[0])
    wait_whole(slope, side_sems.at[1])


def down_kernel(tables, order, info, seed, own, other, slope_in, *refs):
    down_parts, up_parts = refs[0:4], refs[4:8]
    keep = refs[8:10]
    own_grad, other_grad = refs[10:12]
    w_down, w_up, grad, slope, total, normed_t, down_sems, up_sems, out_sems, side_sems = refs[12:]
    for copy in wide_copies(info, tables[0], down_parts, w_down, down_sems):
        copy.start()
    for copy in wide_copies(info, tables[1], up_parts, w_up, up_sems):
        copy.start()
    for j in range(2):
        at = pl.ds(j * D, D)
        pltpu.make_async_copy(slope_in.at[:, :, at], slope.at[:, :, at], side_sems.at[j]).start()
    outs = list(wide_out(info, order, keep, grad, out_sems))
    total[...] = jnp.zeros_like(total)
    normed_t[:, :SEGL] = flip(own[...]).astype(BF16)
    normed_t[:, SEGL:] = flip(other[...]).astype(BF16)
    for j in range(2):
        wait_wide(w_down, down_sems, j)
        wait_wide(w_up, up_sems, j)
        wait_whole(slope.at[:, :, pl.ds(j * D, D)], side_sems.at[j])

        @pl.loop(0, 3)
        def _(chunk):
            at = pl.ds(pl.multiple_of(j * D + chunk * 256, 256), 256)
            sums = []
            for half in range(2):
                back = dot(seed[half], w_down[:, at]).astype(BF16).astype(F32)
                back = (back * slope[half, :, at].astype(F32)).astype(BF16)
                sums.append(dot(normed_t[:, half * SEGL : (half + 1) * SEGL], back))
                total[half] += dot(back, w_up[:, at], 1, 1)
            grad[:, at] = (sums[0] + sums[1]).astype(BF16)

        for owner, copy in outs:
            if owner == j:
                copy.start()
    own_grad[...] = total[0]
    other_grad[...] = total[1].astype(BF16)
    wait_out(grad, out_sems)


def mix_back_kernel(table, order, info, own, other, seed, residual, gain, heads_out, dens_t, *refs):
    parts = refs[0:4]
    resid_grad, head_grad, coef_grad, gain_grad, bias_grad, keep, send = refs[4:11]
    w_out, grad, mix, mix_t, sem, out_sem = refs[11:]
    step = pl.program_id(0)

    @pl.when(step == 0)
    def _():
        for copy in narrow_copies(info, table, parts, [(48, w_out)], sem):
            copy.start()
        normed_grad = (own[...] + other[...].astype(F32)).astype(BF16).astype(F32)
        centred, scale = layer_stats(residual[...])
        unit = centred * scale
        gain_grad[...] = jnp.sum(normed_grad * unit, axis=0, keepdims=True)
        bias_grad[...] = jnp.sum(normed_grad, axis=0, keepdims=True)
        back = normed_grad * gain[...]
        back = back - jnp.mean(back, axis=-1, keepdims=True) - unit * jnp.mean(
            back * unit, axis=-1, keepdims=True
        )
        back = seed[...].astype(F32) + scale * back
        resid_grad[...] = back
        mix[...] = back.astype(BF16)
        mix_t[...] = flip(mix[...]).astype(BF16)
        wait_whole(w_out, sem)

        @pl.loop(0, 3)
        def _(chunk):
            at = pl.ds(aligned(chunk, 256), 256)
            head_grad[:, at] = dot(mix[...], w_out[:, at]).astype(BF16)
            grad[:, at] = dot(mix_t[...], heads_out[:, at]).astype(BF16)

        for copy in out_narrow(info, order, keep, send, [(0, grad)], out_sem):
            copy.start()

    pair_grad = head_grad[:, pl.ds(aligned(step, 128), 128)].astype(F32)
    sums = [
        dot(dens_t[h], jnp.where(half_lanes(h), pair_grad, 0.0).astype(BF16)) for h in range(2)
    ]
    coef_grad[...] = (sums[0] + sums[1]).astype(BF16)

    @pl.when(step == PAIRS - 1)
    def _():
        wait_whole(grad, out_sem)


def attend_back_kernel(
    attn_t, q, k, v, grad, local_t, dens_t, coef, gauss, *refs
):
    dq_out, dk_out, dv_out, gauss_grad, dq_t, dk_sum, dv_sum, rows_of = refs
    keys_t = flip(k[...]).astype(BF16)
    grad_t = flip(grad[...])
    logits = dot(gauss[0], q[...], 1, 1)
    centres = centre_column()
    gauss_columns = flip(gauss[0])
    dk_sum[...] = jnp.zeros_like(dk_sum)
    dv_sum[...] = jnp.zeros_like(dv_sum)
    rows_of[...] = jnp.zeros_like(rows_of)
    only = lambda h, value: jnp.where(half_lanes(h), value.astype(F32), 0.0).astype(BF16)
    for h in range(2):
        rows = slice(h * DH, (h + 1) * DH)
        values, queries, grads = only(h, v[...]), only(h, q[...]), only(h, grad[...])
        delta = jnp.sum(grad_t[rows] * local_t[rows], axis=0, keepdims=True)
        for block in range(2):
            n = 256 * (block + 1)
            at = slice(256 * block, n)
            probs = attn_t[h, :n, at]
            prob_grad = dot(values[:n], grad[at], 1, 1)
            score_grad = (probs.astype(F32) * (prob_grad - delta[:, at])).astype(BF16)
            dv_sum[:n] += dot(probs, grads[at])
            dk_sum[:n] += dot(score_grad, queries[at])
            dq_t[rows, at] = dot(keys_t[rows, :n], score_grad) * DH**-0.5
        mu, spread, var_logit = density_rows(logits, h)
        inverse = 1.0 / spread
        offset = mu - centres
        weighted = dot(only(h, coef[...]), grad[...], 1, 1) * dens_t[h].astype(F32)
        first = weighted * offset
        sum0 = jnp.sum(weighted, axis=0, keepdims=True)
        sum1 = jnp.sum(first, axis=0, keepdims=True)
        sum2 = jnp.sum(first * offset, axis=0, keepdims=True)
        mean_grad = -sum1 * inverse * mu * (1.0 - mu)
        spread_grad = 0.5 * inverse * (sum2 * inverse - sum0)
        var_grad = spread_grad * 0.05 * jax.nn.sigmoid(var_logit)
        rows_of[h : h + 1] = mean_grad
        rows_of[2 + h : 3 + h] = var_grad
        column = gauss_columns[rows]
        dq_t[rows] += column[:, h : h + 1] * mean_grad + column[:, 2 + h : 3 + h] * var_grad
    dq_out[...] = jnp.transpose(dq_t[...]).astype(BF16)
    dk_out[...] = (dk_sum[...] * DH**-0.5).astype(BF16)
    dv_out[...] = dv_sum[...]
    high = rows_of[...].astype(BF16)
    both = dot(high, q[...]) + dot((rows_of[...] - high.astype(F32)).astype(BF16), q[...])
    gauss_grad[0:1] = jnp.where(half_lanes(0), both[0:1], both[1:2])
    gauss_grad[1:2] = jnp.where(half_lanes(0), both[2:3], both[3:4])


def qkv_grad_kernel(orders, near, info, x, dq, dk, dv, coef_grad, ridge_t, *refs):
    if near:
        gauss_grad, gain_grad, bias_grad = refs[:3]
        layout = refs[3][...]
        refs = refs[4:]
    keep_qk, send_qk, keep_v, send_v, dv_out, x_t, gq, gk, gv, small, sems = refs
    x_t[...] = flip(x[...]).astype(BF16)
    scale = column_validity(info) * info[4].astype(F32)

    def weight(source, out):
        @pl.loop(0, 3)
        def _(chunk):
            at = pl.ds(aligned(chunk, 256), 256)
            out[:, at] = dot(x_t[...], source[:, at]).astype(BF16)

    weight(dq, gq)
    weight(dk, gk)
    for copy in out_narrow(info, orders[0], keep_qk, send_qk, [(0, gq), (48, gk)], sems.at[0]):
        copy.start()

    @pl.loop(0, 3)
    def _(chunk):
        at = pl.ds(aligned(chunk, 256), 256)
        pooled_grad = dot(ridge_t[...], coef_grad[:, at])
        dv_out[:, at] = (dv[:, at] + pooled_grad * scale).astype(BF16)
        gv[:, at] = dot(x_t[...], dv_out[:, at]).astype(BF16)

    for copy in out_narrow(info, orders[1], keep_v, send_v, [(0, gv)], sems.at[1]):
        copy.start()
    if near:
        table = scatter_table(orders[1])
        gauss_mask, scale_mask = small_masks(info, [(0,) + row for row in table], layout)
        rows = (
            (gauss_mask, gauss_grad[0:1]),
            (gauss_mask, gauss_grad[1:2]),
            (scale_mask, gain_grad[...]),
            (scale_mask, bias_grad[...]),
        )
        small[...] = jnp.zeros_like(small)
        small[:, :128] = sum(
            dot(jnp.where(mask, row, 0.0).astype(BF16), small_places(layout, i, 128), 1, 1)
            for i, (mask, row) in enumerate(rows)
        ).astype(BF16)
        for n, (index, _, _, kc) in enumerate(table):
            pltpu.make_async_copy(
                small.at[pl.ds(16 * n, 16)],
                (keep_v, send_v)[kc].at[index + (pl.ds(48, 16),)],
                sems.at[2],
            ).start()
        wait_whole(small, sems.at[2])
    both = pltpu.make_async_copy(gq, gq, sems.at[0])
    both.wait()
    both.wait()
    wait_whole(gv, sems.at[1])


def finish_kernel(tables, info, dq, dk, dv, resid_grad, hidden, residual, *refs):
    qk, v_parts, down_parts = refs[0:4], refs[4:8], refs[8:12]
    token_keep, token_send, fed_keep, fed_send = refs[12:16]
    wq, wk, wv, w_down, sems, down_sems = refs[16:]
    for copy in narrow_copies(info, tables[0], qk, [(0, wq), (48, wk)], sems.at[0]):
        copy.start()
    for copy in narrow_copies(info, tables[1], v_parts, [(0, wv)], sems.at[1]):
        copy.start()
    for copy in wide_copies(info, tables[2], down_parts, w_down, down_sems):
        copy.start()
    first = info[5] == 0

    def split(value):
        top, bottom = value[:HALF_SEG], value[HALF_SEG:]
        return jnp.where(first, top, bottom), jnp.where(first, bottom, top).astype(BF16)

    pair_wait = pltpu.make_async_copy(wq, wq, sems.at[0])
    pair_wait.wait()
    pair_wait.wait()
    wait_whole(wv, sems.at[1])

    @pl.loop(0, 3)
    def _(chunk):
        at = pl.ds(aligned(chunk, 256), 256)
        part = dot(dq[...], wq[at, :], 1, 1) + dot(dk[...], wk[at, :], 1, 1)
        value = resid_grad[:, at] + part + dot(dv[...], wv[at, :], 1, 1)
        token_keep[:, at], token_send[:, at] = split(value)

    wait_out(w_down, down_sems)

    @pl.loop(0, 3)
    def _(chunk):
        at = pl.ds(aligned(chunk, 256), 256)
        value = residual[:, at] + dot(hidden[0], w_down[at, :], 1, 1)
        fed_keep[0, :, at], fed_send[0, :, at] = split(value)
        value = dot(hidden[1], w_down[at, :], 1, 1)
        fed_keep[1, :, at], fed_send[1, :, at] = split(value)


FULL = pl.BlockSpec()
ANY = pl.BlockSpec(memory_space=pl.ANY)
SCALARS = pl.BlockSpec(memory_space=SMEM)
MATRIX = (D, D)
HALF = FF // 2
HALF_SEG = SEGL // 2
WIDE = (D, HALF)
DMA = pltpu.SemaphoreType.DMA


def shape(dims, dtype=BF16):
    return jax.ShapeDtypeStruct(dims, dtype)


def run(body, name, args, in_specs, outs, out_specs, scratch=(), grid=None, cost=5.0, vmem=48):
    kwargs = {} if grid is None else {"grid": grid}
    args = [
        value
        if spec is SCALARS
        else pltpu.with_memory_space_constraint(value, pltpu.HBM)
        for value, spec in zip(args, in_specs)
    ]
    return pl.pallas_call(
        body,
        name=name,
        out_shape=tuple(pltpu.HBM(out.shape, out.dtype) for out in outs),
        in_specs=list(in_specs),
        out_specs=tuple(out_specs),
        scratch_shapes=list(scratch),
        cost_estimate=pl.CostEstimate(
            flops=int(cost * 2e8), bytes_accessed=int(1e6), transcendentals=0
        ),
        compiler_params=pltpu.CompilerParams(vmem_limit_bytes=vmem * 1024 * 1024),
        **kwargs,
    )(*args)


PAIR_COLUMNS = pl.BlockSpec((SEGL, 128), lambda p: (0, p))
PAIR_ROWS = pl.BlockSpec((128, SEGL), lambda p: (p, 0))
PAIR_COEF = pl.BlockSpec((NB, 128), lambda p: (0, p))
PAIR_ATTN = pl.BlockSpec((2, SEGL, SEGL), lambda p: (p, 0, 0))
PAIR_DENS = pl.BlockSpec((2, NB, SEGL), lambda p: (p, 0, 0))


def pair_block(*dims):
    return pl.BlockSpec((1,) + dims, lambda p: (p, 0, 0))


ORDER_QK, ORDER_V = "zyx", "zxy"
BACK_QK, BACK_V, BACK_UP, BACK_DOWN = "xyz", "yxz", "yxz", "xyz"


def local(
    tokens, lengths, mem_mask, cotangent, w_qkv, w_gauss, w_out, ln_gain, ln_bias, w_up, w_down
):
    dp_count = lax.axis_size("dp")
    dp, rank = lax.axis_index("dp"), lax.axis_index("tensor")
    core, segment = rank % 2, rank // 2
    near = dp_count == 8
    gauss_size, gain_size = w_gauss.size, ln_gain.size
    ridge = ridge_matrix()

    used = [
        jnp.clip(lax.dynamic_index_in_dim(lengths, at, 0, False) - segment * SEGL, 0, SEGL)
        for at in (core, 1 - core)
    ]
    pair = lax.dynamic_index_in_dim(mem_mask, core, 0, False)[1, 0]
    where = (dp, segment, core) if near else (0, 0, 0)
    info = jnp.stack([jnp.asarray(value, jnp.int32) for value in where + (used[0], pair, core)])

    own, other = to_segment_parts(tokens)
    theirs = swap(cotangent)
    everything = jnp.where(
        core == 0,
        jnp.concatenate([cotangent, theirs], axis=1),
        jnp.concatenate([theirs, cotangent], axis=1),
    )
    seed = jnp.stack(
        [lax.dynamic_index_in_dim(everything, at, 0, False) for at in (core, 1 - core)]
    )
    seed = jnp.stack(
        [
            jnp.where(jnp.arange(SEGL)[:, None] < count, part, 0.0).astype(BF16)
            for count, part in zip(used, seed)
        ]
    )
    seed_t = seed.reshape(2 * SEGL, D).T

    projections = jnp.concatenate([w_qkv, w_out.T[None]])
    if near:
        mine = lax.dynamic_slice_in_dim(projections, core * 48, 48, axis=1)
        partner = swap(lax.dynamic_slice_in_dim(projections, (1 - core) * 48, 48, axis=1))
        projections = jnp.where(
            core == 0,
            jnp.concatenate([mine, partner], axis=2),
            jnp.concatenate([partner, mine], axis=2),
        )
        small = jnp.concatenate(
            [w_gauss.reshape(-1)] + exact_triple(jnp.concatenate([ln_gain, ln_bias]))
        )
        small_rows = jnp.pad(small[None], ((0, 15), (0, 384 - small.size)))
        packed = jnp.concatenate([projections.reshape(192, 384), small_rows])
        along_z = spread(packed, "z")
        along_z[1] = after(along_z[1], seed, seed_t, other)
        qk_near = jnp.stack(spread(jnp.stack([part[:96] for part in along_z]), "y"))
        v_near = jnp.stack(spread(jnp.stack([part[96:] for part in along_z]), "x"))
        qk_far, v_far = xor_permute(qk_near, "x", 1), xor_permute(v_near, "y", 1)
        qk_swap, v_swap = swap(qk_near), swap(v_near)
        up_z = spread(after(w_up, qk_swap, v_swap), "z")
        qk_parts = [qk_near, qk_far, qk_swap, swap(after(qk_far, *up_z[1:]))]
        v_parts = [v_near, v_far, v_swap, swap(after(v_far, *up_z[1:]))]
        up_z = after(jnp.stack(up_z), qk_parts[3], v_parts[3])
        up_x, up_y = xor_permute(up_z, "x", 1), xor_permute(up_z, "y", 1)
        down_z = spread(after(w_down.T, qk_parts[3], v_parts[3]), "z")
    else:
        every = lambda value: lax.all_gather(value, AXES, axis=0)
        cut = lambda value: value.reshape((8, dp_count // 8) + value.shape[1:])
        both = cut(every(projections).reshape(dp_count, 4, 4, -1, 192))
        both = both.transpose(0, 3, 1, 4, 2, 5).reshape(8, 4, 2, 48, 2, 384)
        both = both.transpose(0, 4, 2, 1, 3, 5)
        qk_parts = as_gathered(both[:, :, :, :2].reshape(8, 2, 2, 96, 384), ORDER_QK)
        v_parts = as_gathered(
            jnp.pad(both[:, :, :, 2:].reshape(8, 2, 2, 96, 384), ((0, 0),) * 3 + ((0, 16), (0, 0))),
            ORDER_V,
        )

        def wide(value):
            value = cut(every(value).reshape(dp_count, 4, -1, D)).transpose(0, 2, 1, 3, 4)
            value = value.reshape(8, 2, 2, 96, D)
            return lax.dynamic_slice_in_dim(value, core, 1, axis=2)

        def in_parts(whole):
            whole = whole.reshape((4, 2, 2) + whole.shape[3:])
            return [whole[:, ky, kx] for ky in range(2) for kx in range(2)]

        up_parts, down_parts = in_parts(wide(w_up)), in_parts(wide(w_down.T))
    table_qk, table_v = piece_table(ORDER_QK), piece_table(ORDER_V)
    table_wide = wide_table()

    tall = shape((SEGL, D))
    row = shape((1, D), F32)
    small_in, small_out = [], []
    if near:
        small_in = [jnp.asarray(small_layout())]
        small_out = [shape((PAIRS, 16, 128)), row, row]
    x, q, k, v, coef, *small_params = run(
        functools.partial(qkv_kernel, table_qk, table_v, near),
        "qkv",
        [info, own, other, jnp.asarray(ridge)] + qk_parts + v_parts + small_in,
        [SCALARS, FULL, FULL, FULL] + [ANY] * 8 + [FULL] * len(small_in),
        [tall] * 4 + [shape((NB, D))] + small_out,
        [FULL] * (5 + len(small_out)),
        [VMEM(MATRIX, BF16)] * 3 + [VMEM((512, 384), BF16), DMA((3,))],
        cost=6.0,
        vmem=24,
    )
    coef = lax.ppermute(coef, "tensor", [(0, 2), (1, 3)])

    q_late = q
    if near:
        q_late = after(q, up_x, up_y)
        up_parts = [up_z, up_x, up_y, xor_permute(after(up_x, q), "y", 1)]
        gauss_rows, norm_gain, norm_bias = small_params
    else:
        scales = every(jnp.stack([ln_gain, ln_bias]))
        gauss_parts = every(w_gauss.reshape(-1))
        norm_gain, norm_bias = scales[:, 0].reshape(1, D), scales[:, 1].reshape(1, D)
        gauss = gauss_parts.reshape(dp_count, 4, 2, 3, -1).transpose(2, 1, 3, 0, 4)
        gauss = gauss.reshape(2, PAIRS, 2, DH)
        spread_rows = jnp.eye(2, dtype=BF16)[None, None, :, :, None] * gauss[:, :, :, None, :]
        gauss_rows = spread_rows.transpose(1, 0, 2, 3, 4).reshape(PAIRS, 4, 128)
        gauss_rows = jnp.pad(gauss_rows, ((0, 0), (0, 12), (0, 0)))

    attn_t, local_t, dens_t = run(
        attend_kernel,
        "attend",
        [info, q_late, k, v, gauss_rows],
        [SCALARS] + [PAIR_COLUMNS] * 3 + [pair_block(16, 128)],
        [shape((H, SEGL, SEGL)), shape((D, SEGL), F32), shape((H, NB, SEGL))],
        [PAIR_ATTN, PAIR_ROWS, PAIR_DENS],
        [VMEM((SEGL, SEGL), F32)],
        grid=(PAIRS,),
        cost=12.0,
        vmem=14,
    )
    if near:
        down_z[1:] = lax.optimization_barrier((attn_t, coef, up_parts[3], *down_z[1:]))[3:]
        down_z = jnp.stack(down_z)
        down_x, down_y = xor_permute(down_z, "x", 1), xor_permute(down_z, "y", 1)
    whole = lambda *dims: pl.BlockSpec(dims, lambda p: (0,) * len(dims))
    heads_out, residual, normed = run(
        functools.partial(recall_kernel, table_v),
        "recall",
        [info, dens_t, coef, local_t, x, norm_gain, norm_bias] + v_parts,
        [SCALARS, PAIR_DENS, PAIR_COEF, PAIR_ROWS, whole(SEGL, D), whole(1, D), whole(1, D)]
        + [ANY] * 4,
        [tall, shape((SEGL, D), F32), tall],
        [whole(SEGL, D)] * 3,
        [VMEM(MATRIX, BF16), DMA(())],
        grid=(PAIRS,),
        cost=7.0,
        vmem=18,
    )
    if near:
        down_parts = [down_z, down_x, down_y, xor_permute(after(down_x, down_y, normed), "y", 1)]
    normed_other = swap(normed)
    piece_dims = lambda order: tuple(SIZES[letter] for letter in order)
    hidden, slope, *keep_down = run(
        functools.partial(up_kernel, table_wide, BACK_DOWN),
        "up",
        [info, normed, normed_other, seed_t] + up_parts,
        [SCALARS, FULL, FULL, FULL] + [ANY] * 4,
        [shape((2, SEGL, HALF))] * 2 + [shape(piece_dims(BACK_DOWN)[1:] + (96, D))] * 2,
        [ANY] * 4,
        [VMEM(WIDE, BF16)] * 2 + [VMEM((2, SEGL, HALF), BF16)] * 2 + [DMA((2,))] * 3,
        cost=12.0,
        vmem=22,
    )
    if near:
        down_1 = stage(lambda k: keep_down[k], BACK_DOWN[0])
    *keep_up, own_grad, other_grad = run(
        functools.partial(down_kernel, (table_wide, table_wide), BACK_UP),
        "down",
        [info, seed, normed, normed_other, slope] + down_parts + up_parts,
        [SCALARS] + [FULL] * 3 + [ANY] * 9,
        [shape(piece_dims(BACK_UP)[1:] + (96, D))] * 2 + [shape((SEGL, D), F32), tall],
        [ANY] * 2 + [FULL] * 2,
        [VMEM(WIDE, BF16)] * 3
        + [VMEM((2, SEGL, HALF), BF16), VMEM((2, SEGL, D), F32), VMEM((D, 2 * SEGL), BF16)]
        + [DMA((2,))] * 4,
        cost=15.0,
        vmem=30,
    )
    if near:
        up_1 = stage(lambda k: keep_up[k], BACK_UP[0])
        own_grad = after(own_grad, *down_1[1])
    other_grad = swap(other_grad)
    narrow_grad = [shape(piece_dims(BACK_V) + (48, 384))] * 2
    resid_grad, head_grad, coef_grad, gain_part, bias_part, keep_out, send_out = run(
        functools.partial(mix_back_kernel, table_v, BACK_V),
        "mix_back",
        [info, own_grad, other_grad, seed[0], residual, norm_gain, heads_out, dens_t] + v_parts,
        [SCALARS]
        + [whole(SEGL, D)] * 4
        + [whole(1, D), whole(SEGL, D), PAIR_DENS]
        + [ANY] * 4,
        [shape((SEGL, D), F32), tall, shape((NB, D)), row, row] + narrow_grad,
        [whole(SEGL, D), whole(SEGL, D), PAIR_COEF, whole(1, D), whole(1, D)] + [ANY] * 2,
        [VMEM(MATRIX, BF16)] * 2
        + [VMEM((SEGL, D), BF16), VMEM((D, SEGL), BF16)]
        + [DMA(())] * 2,
        grid=(PAIRS,),
        cost=6.0,
        vmem=26,
    )
    coef_grad = lax.ppermute(coef_grad, "tensor", [(2, 0), (3, 1)])
    if near:
        got_out = swap(send_out)
    dq, dk, dv, gauss_grad = run(
        attend_back_kernel,
        "attend_back",
        [attn_t, q, k, v, head_grad, local_t, dens_t, coef, gauss_rows],
        [PAIR_ATTN]
        + [PAIR_COLUMNS] * 4
        + [PAIR_ROWS, PAIR_DENS, PAIR_COEF, pair_block(16, 128)],
        [tall, tall, shape((SEGL, D), F32), shape((2, D), F32)],
        [PAIR_COLUMNS] * 3 + [pl.BlockSpec((2, 128), lambda p: (0, p))],
        [
            VMEM((128, SEGL), F32),
            VMEM((SEGL, 128), F32),
            VMEM((SEGL, 128), F32),
            VMEM((16, SEGL), F32),
        ],
        grid=(PAIRS,),
        cost=16.0,
        vmem=16,
    )
    if near:
        up_1 = (up_1[0], [after(a, dk, coef_grad, got_out) for a in up_1[1]])
        dq = after(dq, *up_1[1])
        down_1 = (down_1[0], [after(a, *up_1[1]) for a in down_1[1]])
        down_2 = stage(combined(*down_1), BACK_DOWN[1])
        up_2 = stage(combined(*up_1), BACK_UP[1])
    keep_qk, send_qk, keep_v, send_v, dv = run(
        functools.partial(qkv_grad_kernel, (BACK_QK, BACK_V), near),
        "qkv_grad",
        [info, x, dq, dk, dv, coef_grad, jnp.asarray(ridge.T)]
        + ([gauss_grad, gain_part, bias_part] + small_in if near else []),
        [SCALARS] + [FULL] * (10 if near else 6),
        [shape(piece_dims(BACK_QK) + (96, 384))] * 2
        + [shape(piece_dims(BACK_V) + (64, 384))] * 2
        + [tall],
        [ANY] * 4 + [FULL],
        [VMEM((D, SEGL), BF16)] + [VMEM(MATRIX, BF16)] * 3 + [VMEM((512, 384), BF16), DMA((3,))],
        cost=6.0,
        vmem=26,
    )

    if near:
        send_qk = after(send_qk, *down_2[1], *up_2[1])
        send_v = after(send_v, *down_2[1], *up_2[1])
        got_qk, got_v = swap(send_qk), swap(send_v)
        first_qk = [keep_qk[k].astype(F32) + got_qk[k].astype(F32) for k in range(2)]
        rest = ((keep_out, got_out), (keep_v, got_v))
        first_v = [
            jnp.concatenate([a[k].astype(F32) + b[k].astype(F32) for a, b in rest], axis=2)
            for k in range(2)
        ]
        first_qk[1], first_v[1] = first_qk[1].astype(BF16), first_v[1].astype(BF16)
        qk_1 = stage(lambda k: first_qk[k], BACK_QK[0])
        v_1 = stage(lambda k: first_v[k], BACK_V[0])
        down_2 = (down_2[0], [after(a, first_qk[1], first_v[1]) for a in down_2[1]])
        to_down, to_up = combined(*down_2), combined(*up_2)
        wide = [jnp.concatenate([to_down(k), to_up(k)]) for k in range(4)]
        wide[1:] = [value.astype(BF16) for value in wide[1:]]
        wide_3 = stage(lambda k: wide[k], "z")
        dq_late = after(dq, first_qk[1], first_v[1], *wide[1:])
    else:
        dq_late = dq

    token_keep, token_send, fed_keep, fed_send = run(
        functools.partial(finish_kernel, (table_qk, table_v, table_wide)),
        "finish",
        [info, dq_late, dk, dv, resid_grad, hidden, residual] + qk_parts + v_parts + down_parts,
        [SCALARS] + [FULL] * 6 + [ANY] * 12,
        [shape((HALF_SEG, D), F32), shape((HALF_SEG, D))]
        + [shape((2, HALF_SEG, D), F32), shape((2, HALF_SEG, D))],
        [FULL] * 4,
        [VMEM(MATRIX, BF16)] * 3 + [VMEM(WIDE, BF16)] + [DMA((2,))] * 2,
        cost=14.0,
        vmem=32,
    )
    token_got, fed_got = swap(token_send).astype(F32), swap(fed_send).astype(F32)
    own_rows, their_rows = fed_keep[0] + fed_got[1], fed_keep[1] + fed_got[0]
    by_sequence = lambda mine, theirs: jnp.where(
        core == 0, jnp.stack([mine, theirs]), jnp.stack([theirs, mine])
    )
    output = by_sequence(own_rows, their_rows)
    grad_tokens = by_sequence(token_keep, token_got)

    if near:
        qk_2 = stage(combined(*qk_1), BACK_QK[1])
        v_2 = stage(combined(*v_1), BACK_V[1])
        to_qk, to_v = combined(*qk_2), combined(*v_2)
        last = [jnp.concatenate([to_qk(k), to_v(k)]) for k in range(4)]
        last[1:] = [value.astype(BF16) for value in last[1:]]
        joined = final_sum(*stage(lambda k: last[k], "z"))
        own_small = joined[192]
        narrow = joined[:192].reshape(4, 48, 384)
        mine = lax.dynamic_slice_in_dim(narrow, core * 192, 192, axis=2)
        partner = swap(lax.dynamic_slice_in_dim(narrow, (1 - core) * 192, 192, axis=2))
        narrow = jnp.where(
            core == 0,
            jnp.concatenate([mine, partner], axis=1),
            jnp.concatenate([partner, mine], axis=1),
        )
        own_wide = final_sum(*wide_3)
        own_up, own_down = own_wide[96:], own_wide[:96].T
    else:
        gauss_grad = gauss_grad.reshape(2, 4, 3, dp_count, -1).transpose(3, 1, 0, 2, 4)
        small_grads = jnp.concatenate(
            [value.reshape(dp_count * 4, -1) for value in (gauss_grad, gain_part, bias_part)],
            axis=1,
        )
        own_small = lax.psum_scatter(small_grads, AXES, scatter_dimension=0)
        pieces = [
            whole_from([keep_qk, send_qk], BACK_QK).reshape(8, 2, 2, 2, 48, 384),
            whole_from([keep_out, send_out], BACK_V)[:, :, :, None],
            whole_from([keep_v, send_v], BACK_V)[:, :, :, None, :48],
        ]
        pieces = jnp.concatenate(pieces, axis=3).transpose(0, 2, 4, 3, 1, 5)
        pieces = pieces.reshape(dp_count, D // dp_count, 4, 4, 192).transpose(0, 3, 2, 1, 4)
        total = lambda value: lax.psum_scatter(value.astype(F32), AXES, scatter_dimension=0)
        narrow = total(pieces.reshape((-1,) + pieces.shape[2:]))

        def owned(keep, order):
            mine = whole_from([jnp.stack(keep)], order)
            both = jnp.concatenate(
                [jnp.where(core == at, mine, jnp.zeros_like(mine)) for at in range(2)], axis=2
            )
            both = both.transpose(0, 3, 1, 2, 4).reshape(dp_count, D // dp_count, 4, D)
            both = both.transpose(0, 2, 1, 3)
            return total(both.reshape((-1,) + both.shape[2:]))

        own_up, own_down = owned(keep_up, BACK_UP), owned(keep_down, BACK_DOWN).T
    own_qkv, own_out = jnp.concatenate([narrow[:2], narrow[3:]]), narrow[2].T
    return (
        output,
        grad_tokens,
        own_qkv,
        own_small[:gauss_size].reshape(w_gauss.shape),
        own_out,
        own_small[gauss_size : gauss_size + gain_size],
        own_small[gauss_size + gain_size : gauss_size + 2 * gain_size],
        own_up,
        own_down,
    )


def solution(mesh):
    return jax.shard_map(
        local,
        mesh=mesh,
        in_specs=(
            P("dp", "tensor", None),
            P("dp"),
            P("dp", None, None),
            P("dp", "tensor", None),
            P(None, "dp", "tensor"),
            P(None, "tensor", "dp"),
            P("tensor", "dp"),
            P(("dp", "tensor")),
            P(("dp", "tensor")),
            P("dp", "tensor"),
            P("tensor", "dp"),
        ),
        out_specs=(
            P("dp", "tensor", None),
            P("dp", "tensor", None),
            P(None, "dp", "tensor"),
            P(None, "tensor", "dp"),
            P("tensor", "dp"),
            P(("dp", "tensor")),
            P(("dp", "tensor")),
            P("dp", "tensor"),
            P("tensor", "dp"),
        ),
        check_vma=False,
    )
```

```python
import functools

import jax
import jax.numpy as jnp
import numpy as np
from jax import lax
from jax.experimental import pallas as pl
from jax.experimental.pallas import tpu as pltpu
from jax.sharding import PartitionSpec as P

D = 768
H = 12
DH = 64
NB = 256
SEGL = 512
FF = 3072
PAIRS = H // 2
AXES = ("dp", "tensor")
F32 = jnp.float32
BF16 = jnp.bfloat16
BASIS_VAR = (1.0 / NB) ** 2
VMEM = pltpu.VMEM
SMEM = pltpu.SMEM


def ridge_matrix():
    centres = (np.arange(NB) + 0.5) / NB
    samples = (np.arange(SEGL) + 0.5) / SEGL
    rows = np.exp(-0.5 * ((samples[None, :] - centres[:, None]) * NB) ** 2)
    gram = rows @ rows.T + 0.5 * np.eye(NB)
    return np.linalg.solve(gram, rows).astype(np.float32).astype(jnp.bfloat16)


SIZES = {"z": 4, "y": 2, "x": 2, "c": 2}


def xor_permute(value, letter, k):
    dp_mask, tensor_mask = {"z": (2 * k, 0), "y": (k, 0), "x": (0, 2 * k), "c": (0, k)}[letter]
    dp_count, rank_count = lax.axis_size("dp"), lax.axis_size("tensor")
    pairs = [
        (d * rank_count + t, (d ^ dp_mask) * rank_count + (t ^ tensor_mask))
        for d in range(dp_count)
        for t in range(rank_count)
    ]
    return lax.ppermute(value, AXES, pairs)


def swap(value):
    return xor_permute(value, "c", 1)


def after(value, *others):
    return lax.optimization_barrier((value,) + others)[0]


def piece_table(order, cores=2):
    first, second, third = order
    table = []
    for at, (kc, k3) in enumerate([(0, 0), (0, 1), (1, 0), (1, 1)][: 2 * cores]):
        for i2 in range(SIZES[second]):
            for i1 in range(SIZES[first]):
                k = {first: i1, second: i2, third: k3}
                table.append((at, (i2, i1), k["z"] * 2 + k["y"], k["x"], kc))
    return table


def wide_table():
    return [
        (2 * ky + kx, (kz,), 2 * kz + ky, kx, 0)
        for ky in range(2)
        for kx in range(2)
        for kz in range(4)
    ]


def spread(piece, letter):
    return [piece] + [xor_permute(piece, letter, k) for k in range(1, SIZES[letter])]


def as_gathered(whole, order):
    first, second, third = order
    whole = whole.reshape((4, 2) + whole.shape[1:])
    at = {"z": 0, "y": 1, "x": 2, "c": 3}
    rest = list(range(4, whole.ndim))
    whole = whole.transpose([at["c"], at[third], at[second], at[first]] + rest)
    return [whole[0, 0], whole[0, 1], whole[1, 0], whole[1, 1]]


def stage(total, letter):
    own = total(0)
    arrived = [xor_permute(total(k).astype(BF16), letter, k) for k in range(1, SIZES[letter])]
    return own, arrived


def combined(own, arrived):
    return lambda k: sum((a[k].astype(F32) for a in arrived), own[k].astype(F32))


def final_sum(own, arrived):
    return sum((a.astype(F32) for a in arrived), own)


def whole_from(parts, order):
    first, second, third = order
    whole = jnp.stack(parts)
    at = {"c": 0, first: 1, second: 2, third: 3}
    rest = list(range(4, whole.ndim))
    whole = whole.transpose([at["z"], at["y"], at["x"], at["c"]] + rest)
    return whole.reshape((8,) + whole.shape[2:])


def to_segment_parts(local):
    core = lax.axis_index("tensor") % 2
    own = lax.dynamic_index_in_dim(local, core, 0, keepdims=False)
    return own, swap(lax.dynamic_index_in_dim(local, 1 - core, 0, keepdims=False))


def exact_triple(value):
    high = lax.reduce_precision(value, 8, 7)
    middle = lax.reduce_precision(value - high, 8, 7)
    return [part.astype(BF16) for part in (high, middle, value - high - middle)]


def dot(left, right, left_dim=1, right_dim=0):
    return lax.dot_general(
        left, right, (((left_dim,), (right_dim,)), ((), ())), preferred_element_type=F32
    )


def flip(value):
    return jnp.transpose(value.astype(F32))


def aligned(value, step):
    return pl.multiple_of(value * step, step)


def wide_copies(info, table, arrays, target, sems):
    for at, index, r, kx, _ in table:
        rows = pl.ds(aligned(info[0] ^ r, 96), 96)
        yield pltpu.make_async_copy(
            arrays[at].at[index], target.at[rows, pl.ds(kx * D, D)], sems.at[kx]
        )


def wait_wide(target, sems, j):
    block = target.at[:, pl.ds(j * D, D)]
    pltpu.make_async_copy(block, block, sems.at[j]).wait()


def narrow_copies(info, table, arrays, spots, sem):
    for at, index, r, kx, kc in table:
        rows = pl.ds(pl.multiple_of((info[0] ^ r) * 96 + (info[2] ^ kc) * 48, 48), 48)
        columns = pl.ds(aligned(info[1] ^ kx, 384), 384)
        for first, target in spots:
            yield pltpu.make_async_copy(
                arrays[at].at[index + (pl.ds(first, 48),)], target.at[rows, columns], sem
            )


def wait_whole(target, sem):
    pltpu.make_async_copy(target, target, sem).wait()


def out_narrow(info, order, keep, send, spots, sem):
    for index, r, kx, kc in scatter_table(order):
        rows = pl.ds(pl.multiple_of((info[0] ^ r) * 96 + (info[2] ^ kc) * 48, 48), 48)
        columns = pl.ds(aligned(info[1] ^ kx, 384), 384)
        for first, source in spots:
            yield pltpu.make_async_copy(
                source.at[rows, columns], (keep, send)[kc].at[index + (pl.ds(first, 48),)], sem
            )


def scatter_table(order, cores=2):
    a, b, c = order
    table = []
    for kc in range(cores):
        for i in range(SIZES[a]):
            for j in range(SIZES[b]):
                for l in range(SIZES[c]):
                    k = {a: i, b: j, c: l}
                    table.append(((i, j, l), k["z"] * 2 + k["y"], k["x"], kc))
    return table


def column_validity(info):
    return (lax.broadcasted_iota(jnp.int32, (SEGL, 1), 0) < info[3]).astype(F32)


def small_layout():
    column = np.arange(D)
    owner = [(column % DH // 8) * 4 + column // 192, column // 24]
    place = [column // DH % 3 * 8 + column % 8, 48 + column % 24]
    return np.stack(owner + place + [column] * 4).astype(np.int32)


def small_places(layout, i, count):
    row = lax.broadcasted_iota(jnp.int32, (count, D), 0)
    place = layout[2 + i // 2][None] + 24 * (i % 2)
    hit = row == place
    if i > 1 and count > 128:
        hit = hit | (row == place + 48) | (row == place + 96)
    return hit.astype(F32).astype(BF16)


def small_masks(info, table, owner):
    row = lax.broadcasted_iota(jnp.int32, (512, D), 0)
    device = row * 0 - 1
    me = info[0] * 4 + info[1] * 2 + info[2]
    for n, (_, _, r, kx, kc) in enumerate(table):
        device = jnp.where(row == 16 * n, me ^ (r * 4 + kx * 2 + kc), device)
    return device == owner[0:1], device == owner[1:2]


def qkv_kernel(table_qk, table_v, near, info, own, other, ridge, *refs):
    qk, v_parts = refs[0:4], refs[4:8]
    if near:
        layout = refs[8][...]
        refs = refs[:8] + refs[9:]
    x_out, q_out, k_out, v_out, coef_out = refs[8:13]
    if near:
        gauss_out, gain_out, bias_out = refs[13:16]
        refs = refs[:13] + refs[16:]
    wq, wk, wv, small, sems = refs[13:]
    copies = list(narrow_copies(info, table_qk, qk, [(0, wq), (48, wk)], sems.at[0]))
    copies += list(narrow_copies(info, table_v, v_parts, [(0, wv)], sems.at[1]))
    if near:
        for n, (at, index, _, _, _) in enumerate(table_v):
            copies.append(
                pltpu.make_async_copy(
                    v_parts[at].at[index + (pl.ds(96, 16),)], small.at[pl.ds(16 * n, 16)], sems.at[2]
                )
            )
    for copy in copies:
        copy.start()
    core = info[5]
    x_out[pl.ds(aligned(core, 256), 256), :] = own[...]
    x_out[pl.ds(aligned(1 - core, 256), 256), :] = other[...]
    scale = column_validity(info) * info[4].astype(F32)
    pair_wait = pltpu.make_async_copy(wq, wq, sems.at[0])
    pair_wait.wait()
    pair_wait.wait()

    def project(w, out):
        @pl.loop(0, 3)
        def _(step):
            at = pl.ds(aligned(step, 256), 256)
            out[:, at] = dot(x_out[...], w[:, at]).astype(BF16)

    project(wq, q_out)
    project(wk, k_out)
    wait_whole(wv, sems.at[1])

    @pl.loop(0, 3)
    def _(step):
        at = pl.ds(aligned(step, 256), 256)
        values = dot(x_out[...], wv[:, at]).astype(BF16)
        v_out[:, at] = values
        pooled = (values.astype(F32) * scale).astype(BF16)
        coef_out[:, at] = dot(ridge[...], pooled).astype(BF16)

    if near:
        wait_whole(small, sems.at[2])
        gauss_mask, scale_mask = small_masks(info, table_v, layout)
        rows = small[:, :256]

        def collect(at, mask):
            return jnp.sum(jnp.where(mask, dot(rows, small_places(layout, at, 256)), 0.0), axis=0, keepdims=True)

        means, variances = collect(0, gauss_mask), collect(1, gauss_mask)
        gain_out[...] = collect(2, scale_mask)
        bias_out[...] = collect(3, scale_mask)
        row = lax.broadcasted_iota(jnp.int32, (16, 128), 0)
        for p in range(PAIRS):
            at = slice(128 * p, 128 * (p + 1))
            value = jnp.where(row < 2, means[:, at], variances[:, at])
            for h in range(2):
                value = jnp.where((row % 2 == h) & ~half_lanes(h), 0.0, value)
            gauss_out[p] = jnp.where(row < 4, value, 0.0).astype(BF16)


def density_rows(logits, h):
    mean_logit, var_logit = logits[h : h + 1], logits[2 + h : 3 + h]
    mu = jax.nn.sigmoid(mean_logit)
    softplus = jnp.maximum(var_logit, 0.0) + jnp.log1p(jnp.exp(-jnp.abs(var_logit)))
    return mu, 0.05 * softplus + BASIS_VAR, var_logit


def centre_column():
    return (lax.broadcasted_iota(jnp.int32, (NB, 1), 0).astype(F32) + 0.5) / NB


def half_lanes(h):
    lane = lax.broadcasted_iota(jnp.int32, (1, 128), 1)
    return (lane < DH) if h == 0 else (lane >= DH)


def attend_kernel(info, q, k, v, gauss, attn_t, local_t, dens_t, bias):
    @pl.when(pl.program_id(0) == 0)
    def _():
        key = lax.broadcasted_iota(jnp.int32, (SEGL, SEGL), 0)
        query = lax.broadcasted_iota(jnp.int32, (SEGL, SEGL), 1)
        allowed = ((key < query) & (key < info[3])) | (key == query)
        bias[...] = jnp.where(allowed, 0.0, -1e30)

    values_t = flip(v[...]).astype(BF16)
    logits = dot(gauss[0], q[...], 1, 1)
    centres = centre_column()
    for h in range(2):
        rows = slice(h * DH, (h + 1) * DH)
        keys = jnp.where(half_lanes(h), k[...].astype(F32) * DH**-0.5, 0.0).astype(BF16)
        for block in range(2):
            n = 256 * (block + 1)
            at = slice(256 * block, n)
            scores = dot(keys[:n], q[at], 1, 1) + bias[:n, at]
            exponent = jnp.exp(scores - jnp.max(scores, axis=0, keepdims=True))
            total = jnp.sum(exponent, axis=0, keepdims=True)
            probs = (exponent * (1.0 / total)).astype(BF16)
            attn_t[h, :n, at] = probs
            local_t[rows, at] = dot(values_t[rows, :n], probs)
        mu, spread, _ = density_rows(logits, h)
        offset = mu - centres
        dens_t[h] = (
            jnp.sqrt(BASIS_VAR / spread) * jnp.exp(offset * offset * (-0.5 / spread))
        ).astype(BF16)


def layer_stats(residual):
    mean = jnp.mean(residual, axis=-1, keepdims=True)
    centred = residual - mean
    return centred, lax.rsqrt(jnp.mean(centred * centred, axis=-1, keepdims=True) + 1e-05)


def recall_kernel(table, info, dens_t, coef, local_t, x, gain, bias, *refs):
    parts = refs[0:4]
    heads_out, residual, normed = refs[4:7]
    w_out, sem = refs[7:]
    step = pl.program_id(0)

    @pl.when(step == 0)
    def _():
        for copy in narrow_copies(info, table, parts, [(48, w_out)], sem):
            copy.start()

    coef_t = flip(coef[...]).astype(BF16)
    recalled = [dot(coef_t[h * DH : (h + 1) * DH], dens_t[h]) for h in range(2)]
    both = local_t[...] + jnp.concatenate(recalled, axis=0)
    heads_out[:, pl.ds(aligned(step, 128), 128)] = flip(both).astype(BF16)

    @pl.when(step == PAIRS - 1)
    def _():
        wait_whole(w_out, sem)

        @pl.loop(0, 3)
        def _(chunk):
            at = pl.ds(aligned(chunk, 256), 256)
            residual[:, at] = x[:, at].astype(F32) + dot(heads_out[...], w_out[at, :], 1, 1)

        centred, scale = layer_stats(residual[...])
        normed[...] = (centred * scale * gain[...] + bias[...]).astype(BF16)


def gelu_parts(pre):
    c0, c1 = 0.7978845608028654, 0.044715
    square = pre * pre
    inner = jnp.tanh(c0 * pre * (1.0 + c1 * square))
    half = 0.5 * (1.0 + inner)
    slope = half + 0.5 * pre * (1.0 - inner * inner) * (c0 * (1.0 + 3.0 * c1 * square))
    return pre * half, slope


def wide_out(info, order, keep, source, sems):
    for index, r, kx, _ in scatter_table(order, 1):
        rows = pl.ds(aligned(info[0] ^ r, 96), 96)
        yield kx, pltpu.make_async_copy(
            source.at[rows, pl.ds(kx * D, D)], keep[index[0]].at[index[1:]], sems.at[kx]
        )


def wait_out(source, sems):
    for j in range(2):
        wait_wide(source, sems, j)


def up_kernel(table, order, info, own, other, seed_t, *refs):
    parts = refs[0:4]
    hidden_out, slope_out = refs[4:6]
    keep = refs[6:8]
    w_up, grad, hidden, slope, sems, out_sems, side_sems = refs[8:]
    for copy in wide_copies(info, table, parts, w_up, sems):
        copy.start()
    outs = list(wide_out(info, order, keep, grad, out_sems))
    for j in range(2):
        wait_wide(w_up, sems, j)

        @pl.loop(0, 3)
        def _(chunk):
            at = pl.ds(pl.multiple_of(j * D + chunk * 256, 256), 256)
            sums = []
            for half, source in enumerate((own, other)):
                value, derivative = gelu_parts(dot(source[...], w_up[:, at]))
                value = value.astype(BF16)
                hidden[half, :, at] = value
                slope[half, :, at] = derivative.astype(BF16)
                sums.append(dot(seed_t[:, half * SEGL : (half + 1) * SEGL], value))
            grad[:, at] = (sums[0] + sums[1]).astype(BF16)
            for i, (source, target) in enumerate(((hidden, hidden_out), (slope, slope_out))):
                pltpu.make_async_copy(
                    source.at[:, :, at], target.at[:, :, at], side_sems.at[i]
                ).start()

        for owner, copy in outs:
            if owner == j:
                copy.start()
    wait_out(grad, out_sems)
    wait_whole(hidden, side_sems.at[0])
    wait_whole(slope, side_sems.at[1])


def down_kernel(tables, order, info, seed, own, other, slope_in, *refs):
    down_parts, up_parts = refs[0:4], refs[4:8]
    keep = refs[8:10]
    own_grad, other_grad = refs[10:12]
    w_down, w_up, grad, slope, hidden_grad, normed_t = refs[12:18]
    down_sems, up_sems, out_sems, side_sems = refs[18:]
    for copy in wide_copies(info, tables[0], down_parts, w_down, down_sems):
        copy.start()
    for copy in wide_copies(info, tables[1], up_parts, w_up, up_sems):
        copy.start()
    for j in range(2):
        at = pl.ds(j * D, D)
        pltpu.make_async_copy(slope_in.at[:, :, at], slope.at[:, :, at], side_sems.at[j]).start()
    outs = list(wide_out(info, order, keep, grad, out_sems))
    normed_t[:, :SEGL] = flip(own[...]).astype(BF16)
    normed_t[:, SEGL:] = flip(other[...]).astype(BF16)
    for j in range(2):
        wait_wide(w_down, down_sems, j)
        wait_wide(w_up, up_sems, j)
        wait_whole(slope.at[:, :, pl.ds(j * D, D)], side_sems.at[j])

        @pl.loop(0, 3)
        def _(chunk):
            at = pl.ds(pl.multiple_of(j * D + chunk * 256, 256), 256)
            sums = []
            for half in range(2):
                back = dot(seed[half], w_down[:, at]).astype(BF16).astype(F32)
                back = (back * slope[half, :, at].astype(F32)).astype(BF16)
                sums.append(dot(normed_t[:, half * SEGL : (half + 1) * SEGL], back))
                hidden_grad[half, :, at] = back
            grad[:, at] = (sums[0] + sums[1]).astype(BF16)

        for owner, copy in outs:
            if owner == j:
                copy.start()

    @pl.loop(0, 3)
    def _(chunk):
        at = pl.ds(aligned(chunk, 256), 256)
        own_grad[:, at] = dot(hidden_grad[0], w_up[at, :], 1, 1)
        other_grad[:, at] = dot(hidden_grad[1], w_up[at, :], 1, 1).astype(BF16)

    wait_out(grad, out_sems)


def mix_back_kernel(table, order, info, own, other, seed, residual, gain, heads_out, dens_t, *refs):
    parts = refs[0:4]
    resid_grad, head_grad, coef_grad, gain_grad, bias_grad, keep, send = refs[4:11]
    w_out, grad, mix, mix_t, sem, out_sem = refs[11:]
    step = pl.program_id(0)

    @pl.when(step == 0)
    def _():
        for copy in narrow_copies(info, table, parts, [(48, w_out)], sem):
            copy.start()
        normed_grad = (own[...] + other[...].astype(F32)).astype(BF16).astype(F32)
        centred, scale = layer_stats(residual[...])
        unit = centred * scale
        gain_grad[...] = jnp.sum(normed_grad * unit, axis=0, keepdims=True)
        bias_grad[...] = jnp.sum(normed_grad, axis=0, keepdims=True)
        back = normed_grad * gain[...]
        back = back - jnp.mean(back, axis=-1, keepdims=True) - unit * jnp.mean(
            back * unit, axis=-1, keepdims=True
        )
        back = seed[0].astype(F32) + scale * back
        resid_grad[...] = back
        mix[...] = back.astype(BF16)
        mix_t[...] = flip(mix[...]).astype(BF16)
        wait_whole(w_out, sem)

        @pl.loop(0, 3)
        def _(chunk):
            at = pl.ds(aligned(chunk, 256), 256)
            head_grad[:, at] = dot(mix[...], w_out[:, at]).astype(BF16)
            grad[:, at] = dot(mix_t[...], heads_out[:, at]).astype(BF16)

        for copy in out_narrow(info, order, keep, send, [(0, grad)], out_sem):
            copy.start()

    pair_grad = head_grad[:, pl.ds(aligned(step, 128), 128)].astype(F32)
    sums = [
        dot(dens_t[h], jnp.where(half_lanes(h), pair_grad, 0.0).astype(BF16)) for h in range(2)
    ]
    coef_grad[...] = (sums[0] + sums[1]).astype(BF16)

    @pl.when(step == PAIRS - 1)
    def _():
        wait_whole(grad, out_sem)


def attend_back_kernel(
    attn_t, q, k, v, grad, local_t, dens_t, coef, gauss, *refs
):
    dq_out, dk_out, dv_out, gauss_grad, dq_t, dk_sum, dv_sum, rows_of = refs
    keys_t = flip(k[...]).astype(BF16)
    grad_t = flip(grad[...])
    logits = dot(gauss[0], q[...], 1, 1)
    centres = centre_column()
    gauss_columns = flip(gauss[0])
    dk_sum[...] = jnp.zeros_like(dk_sum)
    dv_sum[...] = jnp.zeros_like(dv_sum)
    rows_of[...] = jnp.zeros_like(rows_of)
    only = lambda h, value: jnp.where(half_lanes(h), value.astype(F32), 0.0).astype(BF16)
    for h in range(2):
        rows = slice(h * DH, (h + 1) * DH)
        values, queries, grads = only(h, v[...]), only(h, q[...]), only(h, grad[...])
        delta = jnp.sum(grad_t[rows] * local_t[rows], axis=0, keepdims=True)
        for block in range(2):
            n = 256 * (block + 1)
            at = slice(256 * block, n)
            probs = attn_t[h, :n, at]
            prob_grad = dot(values[:n], grad[at], 1, 1)
            score_grad = (probs.astype(F32) * (prob_grad - delta[:, at])).astype(BF16)
            dv_sum[:n] += dot(probs, grads[at])
            dk_sum[:n] += dot(score_grad, queries[at])
            dq_t[rows, at] = dot(keys_t[rows, :n], score_grad) * DH**-0.5
        mu, spread, var_logit = density_rows(logits, h)
        inverse = 1.0 / spread
        offset = mu - centres
        weighted = dot(only(h, coef[...]), grad[...], 1, 1) * dens_t[h].astype(F32)
        first = weighted * offset
        sum0 = jnp.sum(weighted, axis=0, keepdims=True)
        sum1 = jnp.sum(first, axis=0, keepdims=True)
        sum2 = jnp.sum(first * offset, axis=0, keepdims=True)
        mean_grad = -sum1 * inverse * mu * (1.0 - mu)
        spread_grad = 0.5 * inverse * (sum2 * inverse - sum0)
        var_grad = spread_grad * 0.05 * jax.nn.sigmoid(var_logit)
        rows_of[h : h + 1] = mean_grad
        rows_of[2 + h : 3 + h] = var_grad
        column = gauss_columns[rows]
        dq_t[rows] += column[:, h : h + 1] * mean_grad + column[:, 2 + h : 3 + h] * var_grad
    dq_out[...] = jnp.transpose(dq_t[...]).astype(BF16)
    dk_out[...] = (dk_sum[...] * DH**-0.5).astype(BF16)
    dv_out[...] = dv_sum[...]
    high = rows_of[...].astype(BF16)
    both = dot(high, q[...]) + dot((rows_of[...] - high.astype(F32)).astype(BF16), q[...])
    gauss_grad[0:1] = jnp.where(half_lanes(0), both[0:1], both[1:2])
    gauss_grad[1:2] = jnp.where(half_lanes(0), both[2:3], both[3:4])


def qkv_grad_kernel(orders, near, info, x, dq, dk, dv, coef_grad, ridge_t, *refs):
    if near:
        gauss_grad, gain_grad, bias_grad = refs[:3]
        layout = refs[3][...]
        refs = refs[4:]
    keep_qk, send_qk, keep_v, send_v, dv_out, x_t, gq, gk, gv, small, sems = refs
    x_t[...] = flip(x[...]).astype(BF16)
    scale = column_validity(info) * info[4].astype(F32)

    def weight(source, out):
        @pl.loop(0, 3)
        def _(chunk):
            at = pl.ds(aligned(chunk, 256), 256)
            out[:, at] = dot(x_t[...], source[:, at]).astype(BF16)

    weight(dq, gq)
    weight(dk, gk)
    for copy in out_narrow(info, orders[0], keep_qk, send_qk, [(0, gq), (48, gk)], sems.at[0]):
        copy.start()

    @pl.loop(0, 3)
    def _(chunk):
        at = pl.ds(aligned(chunk, 256), 256)
        pooled_grad = dot(ridge_t[...], coef_grad[:, at])
        dv_out[:, at] = (dv[:, at] + pooled_grad * scale).astype(BF16)
        gv[:, at] = dot(x_t[...], dv_out[:, at]).astype(BF16)

    for copy in out_narrow(info, orders[1], keep_v, send_v, [(0, gv)], sems.at[1]):
        copy.start()
    if near:
        table = scatter_table(orders[1])
        gauss_mask, scale_mask = small_masks(info, [(0,) + row for row in table], layout)
        rows = (
            (gauss_mask, gauss_grad[0:1]),
            (gauss_mask, gauss_grad[1:2]),
            (scale_mask, gain_grad[...]),
            (scale_mask, bias_grad[...]),
        )
        small[...] = jnp.zeros_like(small)
        small[:, :128] = sum(
            dot(jnp.where(mask, row, 0.0).astype(BF16), small_places(layout, i, 128), 1, 1)
            for i, (mask, row) in enumerate(rows)
        ).astype(BF16)
        for n, (index, _, _, kc) in enumerate(table):
            pltpu.make_async_copy(
                small.at[pl.ds(16 * n, 16)],
                (keep_v, send_v)[kc].at[index + (pl.ds(48, 16),)],
                sems.at[2],
            ).start()
        wait_whole(small, sems.at[2])
    both = pltpu.make_async_copy(gq, gq, sems.at[0])
    both.wait()
    both.wait()
    wait_whole(gv, sems.at[1])


def finish_kernel(tables, info, dq, dk, dv, resid_grad, hidden, residual, *refs):
    qk, v_parts, down_parts = refs[0:4], refs[4:8], refs[8:12]
    token_keep, token_send, fed_keep, fed_send = refs[12:16]
    wq, wk, wv, w_down, sems, down_sems = refs[16:]
    for copy in narrow_copies(info, tables[0], qk, [(0, wq), (48, wk)], sems.at[0]):
        copy.start()
    for copy in narrow_copies(info, tables[1], v_parts, [(0, wv)], sems.at[1]):
        copy.start()
    for copy in wide_copies(info, tables[2], down_parts, w_down, down_sems):
        copy.start()
    first = info[5] == 0

    def split(value):
        top, bottom = value[:HALF_SEG], value[HALF_SEG:]
        return jnp.where(first, top, bottom), jnp.where(first, bottom, top).astype(BF16)

    pair_wait = pltpu.make_async_copy(wq, wq, sems.at[0])
    pair_wait.wait()
    pair_wait.wait()
    wait_whole(wv, sems.at[1])

    @pl.loop(0, 3)
    def _(chunk):
        at = pl.ds(aligned(chunk, 256), 256)
        part = dot(dq[...], wq[at, :], 1, 1) + dot(dk[...], wk[at, :], 1, 1)
        value = resid_grad[:, at] + part + dot(dv[...], wv[at, :], 1, 1)
        token_keep[:, at], token_send[:, at] = split(value)

    wait_out(w_down, down_sems)

    @pl.loop(0, 3)
    def _(chunk):
        at = pl.ds(aligned(chunk, 256), 256)
        value = residual[:, at] + dot(hidden[0], w_down[at, :], 1, 1)
        fed_keep[0, :, at], fed_send[0, :, at] = split(value)
        value = dot(hidden[1], w_down[at, :], 1, 1)
        fed_keep[1, :, at], fed_send[1, :, at] = split(value)


FULL = pl.BlockSpec()
ANY = pl.BlockSpec(memory_space=pl.ANY)
FREE = pl.BlockSpec((SEGL, D), lambda: (0, 0))
FREE_ROWS = pl.BlockSpec((SEGL, D), lambda p: (0, 0))
SCALARS = pl.BlockSpec(memory_space=SMEM)
MATRIX = (D, D)
HALF = FF // 2
HALF_SEG = SEGL // 2
WIDE = (D, HALF)
DMA = pltpu.SemaphoreType.DMA


def shape(dims, dtype=BF16):
    return jax.ShapeDtypeStruct(dims, dtype)


def run(body, name, args, in_specs, outs, out_specs, scratch=(), grid=None, cost=5.0, vmem=48):
    kwargs = {} if grid is None else {"grid": grid}
    args = [
        value
        if any(spec is free for free in (SCALARS, FREE, FREE_ROWS))
        else pltpu.with_memory_space_constraint(value, pltpu.HBM)
        for value, spec in zip(args, in_specs)
    ]
    return pl.pallas_call(
        body,
        name=name,
        out_shape=tuple(pltpu.HBM(out.shape, out.dtype) for out in outs),
        in_specs=list(in_specs),
        out_specs=tuple(out_specs),
        scratch_shapes=list(scratch),
        cost_estimate=pl.CostEstimate(
            flops=int(cost * 2e8), bytes_accessed=int(1e6), transcendentals=0
        ),
        compiler_params=pltpu.CompilerParams(vmem_limit_bytes=vmem * 1024 * 1024),
        **kwargs,
    )(*args)


PAIR_COLUMNS = pl.BlockSpec((SEGL, 128), lambda p: (0, p))
PAIR_ROWS = pl.BlockSpec((128, SEGL), lambda p: (p, 0))
PAIR_COEF = pl.BlockSpec((NB, 128), lambda p: (0, p))
PAIR_ATTN = pl.BlockSpec((2, SEGL, SEGL), lambda p: (p, 0, 0))
PAIR_DENS = pl.BlockSpec((2, NB, SEGL), lambda p: (p, 0, 0))


def pair_block(*dims):
    return pl.BlockSpec((1,) + dims, lambda p: (p, 0, 0))


ORDER_QK, ORDER_V = "zyx", "zxy"
BACK_QK, BACK_V, BACK_UP, BACK_DOWN = "xyz", "yxz", "yxz", "xyz"


def local(
    tokens, lengths, mem_mask, cotangent, w_qkv, w_gauss, w_out, ln_gain, ln_bias, w_up, w_down
):
    dp_count = lax.axis_size("dp")
    dp, rank = lax.axis_index("dp"), lax.axis_index("tensor")
    core, segment = rank % 2, rank // 2
    near = dp_count == 8
    gauss_size, gain_size = w_gauss.size, ln_gain.size
    ridge = ridge_matrix()

    used = [
        jnp.clip(lax.dynamic_index_in_dim(lengths, at, 0, False) - segment * SEGL, 0, SEGL)
        for at in (core, 1 - core)
    ]
    pair = lax.dynamic_index_in_dim(mem_mask, core, 0, False)[1, 0]
    where = (dp, segment, core) if near else (0, 0, 0)
    info = jnp.stack([jnp.asarray(value, jnp.int32) for value in where + (used[0], pair, core)])

    own, other = to_segment_parts(tokens)
    theirs = swap(cotangent)
    everything = jnp.where(
        core == 0,
        jnp.concatenate([cotangent, theirs], axis=1),
        jnp.concatenate([theirs, cotangent], axis=1),
    )
    seed = jnp.stack(
        [lax.dynamic_index_in_dim(everything, at, 0, False) for at in (core, 1 - core)]
    )
    seed = jnp.stack(
        [
            jnp.where(jnp.arange(SEGL)[:, None] < count, part, 0.0).astype(BF16)
            for count, part in zip(used, seed)
        ]
    )
    seed_t = seed.reshape(2 * SEGL, D).T

    projections = jnp.concatenate([w_qkv, w_out.T[None]])
    if near:
        mine = lax.dynamic_slice_in_dim(projections, core * 48, 48, axis=1)
        partner = swap(lax.dynamic_slice_in_dim(projections, (1 - core) * 48, 48, axis=1))
        projections = jnp.where(
            core == 0,
            jnp.concatenate([mine, partner], axis=2),
            jnp.concatenate([partner, mine], axis=2),
        )
        small = jnp.concatenate(
            [w_gauss.reshape(-1)] + exact_triple(jnp.concatenate([ln_gain, ln_bias]))
        )
        small_rows = jnp.pad(small[None], ((0, 15), (0, 384 - small.size)))
        packed = jnp.concatenate([projections.reshape(192, 384), small_rows])
        along_z = spread(after(packed, other, theirs), "z")
        along_z[1] = after(along_z[1], seed, seed_t, info)
        qk_near = jnp.stack(spread(jnp.stack([part[:96] for part in along_z]), "y"))
        v_near = jnp.stack(spread(jnp.stack([part[96:] for part in along_z]), "x"))
        qk_far, v_far = xor_permute(qk_near, "x", 1), xor_permute(v_near, "y", 1)
        qk_swap, v_swap = swap(qk_near), swap(v_near)
        up_z = spread(after(w_up, qk_swap, v_swap), "z")
        qk_parts = [qk_near, qk_far, qk_swap, swap(after(qk_far, *up_z[1:]))]
        v_parts = [v_near, v_far, v_swap, swap(after(v_far, *up_z[1:]))]
        up_z = after(jnp.stack(up_z), qk_parts[3], v_parts[3])
        up_x, up_y = xor_permute(up_z, "x", 1), xor_permute(up_z, "y", 1)
        down_z = spread(after(w_down.T, qk_parts[3], v_parts[3]), "z")
    else:
        every = lambda value: lax.all_gather(value, AXES, axis=0)
        cut = lambda value: value.reshape((8, dp_count // 8) + value.shape[1:])
        both = cut(every(projections).reshape(dp_count, 4, 4, -1, 192))
        both = both.transpose(0, 3, 1, 4, 2, 5).reshape(8, 4, 2, 48, 2, 384)
        both = both.transpose(0, 4, 2, 1, 3, 5)
        qk_parts = as_gathered(both[:, :, :, :2].reshape(8, 2, 2, 96, 384), ORDER_QK)
        v_parts = as_gathered(
            jnp.pad(both[:, :, :, 2:].reshape(8, 2, 2, 96, 384), ((0, 0),) * 3 + ((0, 16), (0, 0))),
            ORDER_V,
        )

        def wide(value):
            value = cut(every(value).reshape(dp_count, 4, -1, D)).transpose(0, 2, 1, 3, 4)
            value = value.reshape(8, 2, 2, 96, D)
            return lax.dynamic_slice_in_dim(value, core, 1, axis=2)

        def in_parts(whole):
            whole = whole.reshape((4, 2, 2) + whole.shape[3:])
            return [whole[:, ky, kx] for ky in range(2) for kx in range(2)]

        up_parts, down_parts = in_parts(wide(w_up)), in_parts(wide(w_down.T))
    table_qk, table_v = piece_table(ORDER_QK), piece_table(ORDER_V)
    table_wide = wide_table()

    tall = shape((SEGL, D))
    row = shape((1, D), F32)
    small_in, small_out = [], []
    if near:
        small_in = [jnp.asarray(small_layout())]
        small_out = [shape((PAIRS, 16, 128)), row, row]
    x, q, k, v, coef, *small_params = run(
        functools.partial(qkv_kernel, table_qk, table_v, near),
        "qkv",
        [info, own, other, jnp.asarray(ridge)] + qk_parts + v_parts + small_in,
        [SCALARS, FULL, FULL, FULL] + [ANY] * 8 + [FULL] * len(small_in),
        [tall] * 4 + [shape((NB, D))] + small_out,
        [FULL] * (5 + len(small_out)),
        [VMEM(MATRIX, BF16)] * 3 + [VMEM((512, 384), BF16), DMA((3,))],
        cost=6.0,
        vmem=24,
    )
    coef = lax.ppermute(coef, "tensor", [(0, 2), (1, 3)])

    q_late = q
    if near:
        q_late = after(q, up_x, up_y)
        up_parts = [up_z, up_x, up_y, xor_permute(after(up_x, q), "y", 1)]
        gauss_rows, norm_gain, norm_bias = small_params
    else:
        scales = every(jnp.stack([ln_gain, ln_bias]))
        gauss_parts = every(w_gauss.reshape(-1))
        norm_gain, norm_bias = scales[:, 0].reshape(1, D), scales[:, 1].reshape(1, D)
        gauss = gauss_parts.reshape(dp_count, 4, 2, 3, -1).transpose(2, 1, 3, 0, 4)
        gauss = gauss.reshape(2, PAIRS, 2, DH)
        spread_rows = jnp.eye(2, dtype=BF16)[None, None, :, :, None] * gauss[:, :, :, None, :]
        gauss_rows = spread_rows.transpose(1, 0, 2, 3, 4).reshape(PAIRS, 4, 128)
        gauss_rows = jnp.pad(gauss_rows, ((0, 0), (0, 12), (0, 0)))

    attn_t, local_t, dens_t = run(
        attend_kernel,
        "attend",
        [info, q_late, k, v, gauss_rows],
        [SCALARS] + [PAIR_COLUMNS] * 3 + [pair_block(16, 128)],
        [shape((H, SEGL, SEGL)), shape((D, SEGL), F32), shape((H, NB, SEGL))],
        [PAIR_ATTN, PAIR_ROWS, PAIR_DENS],
        [VMEM((SEGL, SEGL), F32)],
        grid=(PAIRS,),
        cost=12.0,
        vmem=14,
    )
    if near:
        down_z[1:] = lax.optimization_barrier((attn_t, coef, up_parts[3], *down_z[1:]))[3:]
        down_z = jnp.stack(down_z)
        down_x, down_y = xor_permute(down_z, "x", 1), xor_permute(down_z, "y", 1)
    whole = lambda *dims: pl.BlockSpec(dims, lambda p: (0,) * len(dims))
    heads_out, residual, normed = run(
        functools.partial(recall_kernel, table_v),
        "recall",
        [info, dens_t, coef, local_t, x, norm_gain, norm_bias] + v_parts,
        [SCALARS, PAIR_DENS, PAIR_COEF, PAIR_ROWS, whole(SEGL, D), whole(1, D), whole(1, D)]
        + [ANY] * 4,
        [tall, shape((SEGL, D), F32), tall],
        [whole(SEGL, D)] * 3,
        [VMEM(MATRIX, BF16), DMA(())],
        grid=(PAIRS,),
        cost=7.0,
        vmem=18,
    )
    if near:
        down_parts = [down_z, down_x, down_y, xor_permute(after(down_x, down_y, normed), "y", 1)]
    normed_other = swap(normed)
    piece_dims = lambda order: tuple(SIZES[letter] for letter in order)
    hidden, slope, *keep_down = run(
        functools.partial(up_kernel, table_wide, BACK_DOWN),
        "up",
        [info, normed, normed_other, seed_t] + up_parts,
        [SCALARS, FULL, FREE, FULL] + [ANY] * 4,
        [shape((2, SEGL, HALF))] * 2 + [shape(piece_dims(BACK_DOWN)[1:] + (96, D))] * 2,
        [ANY] * 4,
        [VMEM(WIDE, BF16)] * 2 + [VMEM((2, SEGL, HALF), BF16)] * 2 + [DMA((2,))] * 3,
        cost=12.0,
        vmem=22,
    )
    if near:
        down_1 = stage(lambda k: keep_down[k], BACK_DOWN[0])
    *keep_up, own_grad, other_grad = run(
        functools.partial(down_kernel, (table_wide, table_wide), BACK_UP),
        "down",
        [info, seed, normed, normed_other, slope] + down_parts + up_parts,
        [SCALARS] + [FULL] * 2 + [FREE] + [ANY] * 9,
        [shape(piece_dims(BACK_UP)[1:] + (96, D))] * 2 + [shape((SEGL, D), F32), tall],
        [ANY] * 2 + [FULL] * 2,
        [VMEM(WIDE, BF16)] * 3
        + [VMEM((2, SEGL, HALF), BF16)] * 2
        + [VMEM((D, 2 * SEGL), BF16)]
        + [DMA((2,))] * 4,
        cost=15.0,
        vmem=30,
    )
    if near:
        up_1 = stage(lambda k: keep_up[k], BACK_UP[0])
    other_grad = swap(other_grad)
    narrow_grad = [shape(piece_dims(BACK_V) + (48, 384))] * 2
    resid_grad, head_grad, coef_grad, gain_part, bias_part, keep_out, send_out = run(
        functools.partial(mix_back_kernel, table_v, BACK_V),
        "mix_back",
        [info, own_grad, other_grad, seed, residual, norm_gain, heads_out, dens_t] + v_parts,
        [SCALARS]
        + [whole(SEGL, D), FREE_ROWS, pl.BlockSpec((1, SEGL, D), lambda p: (0, 0, 0))]
        + [whole(SEGL, D), whole(1, D), whole(SEGL, D), PAIR_DENS]
        + [ANY] * 4,
        [shape((SEGL, D), F32), tall, shape((NB, D)), row, row] + narrow_grad,
        [whole(SEGL, D), whole(SEGL, D), PAIR_COEF, whole(1, D), whole(1, D)] + [ANY] * 2,
        [VMEM(MATRIX, BF16)] * 2
        + [VMEM((SEGL, D), BF16), VMEM((D, SEGL), BF16)]
        + [DMA(())] * 2,
        grid=(PAIRS,),
        cost=6.0,
        vmem=26,
    )
    coef_grad = lax.ppermute(coef_grad if not near else after(coef_grad, *down_1[1]), "tensor", [(2, 0), (3, 1)])
    if near:
        got_out = swap(send_out)
    dq, dk, dv, gauss_grad = run(
        attend_back_kernel,
        "attend_back",
        [attn_t, q, k, v, head_grad, local_t, dens_t, coef, gauss_rows],
        [PAIR_ATTN]
        + [PAIR_COLUMNS] * 4
        + [PAIR_ROWS, PAIR_DENS, PAIR_COEF, pair_block(16, 128)],
        [tall, tall, shape((SEGL, D), F32), shape((2, D), F32)],
        [PAIR_COLUMNS] * 3 + [pl.BlockSpec((2, 128), lambda p: (0, p))],
        [
            VMEM((128, SEGL), F32),
            VMEM((SEGL, 128), F32),
            VMEM((SEGL, 128), F32),
            VMEM((16, SEGL), F32),
        ],
        grid=(PAIRS,),
        cost=16.0,
        vmem=16,
    )
    if near:
        up_1 = (up_1[0], [after(a, dk, coef_grad, got_out) for a in up_1[1]])
        dq = after(dq, *up_1[1])
        down_1 = (down_1[0], [after(a, *up_1[1]) for a in down_1[1]])
        down_2 = stage(combined(*down_1), BACK_DOWN[1])
        up_2 = stage(combined(*up_1), BACK_UP[1])
    keep_qk, send_qk, keep_v, send_v, dv = run(
        functools.partial(qkv_grad_kernel, (BACK_QK, BACK_V), near),
        "qkv_grad",
        [info, x, dq, dk, dv, coef_grad, jnp.asarray(ridge.T)]
        + ([gauss_grad, gain_part, bias_part] + small_in if near else []),
        [SCALARS] + [FULL] * (10 if near else 6),
        [shape(piece_dims(BACK_QK) + (96, 384))] * 2
        + [shape(piece_dims(BACK_V) + (64, 384))] * 2
        + [tall],
        [ANY] * 4 + [FULL],
        [VMEM((D, SEGL), BF16)] + [VMEM(MATRIX, BF16)] * 3 + [VMEM((512, 384), BF16), DMA((3,))],
        cost=6.0,
        vmem=26,
    )

    if near:
        send_qk = after(send_qk, *down_2[1], *up_2[1])
        send_v = after(send_v, *down_2[1], *up_2[1])
        got_qk, got_v = swap(send_qk), swap(send_v)
        first_qk = [keep_qk[k].astype(F32) + got_qk[k].astype(F32) for k in range(2)]
        rest = ((keep_out, got_out), (keep_v, got_v))
        first_v = [
            jnp.concatenate([a[k].astype(F32) + b[k].astype(F32) for a, b in rest], axis=2)
            for k in range(2)
        ]
        first_qk[1], first_v[1] = first_qk[1].astype(BF16), first_v[1].astype(BF16)
        qk_1 = stage(lambda k: first_qk[k], BACK_QK[0])
        v_1 = stage(lambda k: first_v[k], BACK_V[0])
        down_2 = (down_2[0], [after(a, first_qk[1], first_v[1]) for a in down_2[1]])
        to_down, to_up = combined(*down_2), combined(*up_2)
        wide = [jnp.concatenate([to_down(k), to_up(k)]) for k in range(4)]
        wide[1:] = [value.astype(BF16) for value in wide[1:]]
        wide_3 = stage(lambda k: wide[k], "z")
        dq_late = after(dq, first_qk[1], first_v[1], *wide[1:])
    else:
        dq_late = dq

    token_keep, token_send, fed_keep, fed_send = run(
        functools.partial(finish_kernel, (table_qk, table_v, table_wide)),
        "finish",
        [info, dq_late, dk, dv, resid_grad, hidden, residual] + qk_parts + v_parts + down_parts,
        [SCALARS] + [FULL] * 6 + [ANY] * 12,
        [shape((HALF_SEG, D), F32), shape((HALF_SEG, D))]
        + [shape((2, HALF_SEG, D), F32), shape((2, HALF_SEG, D))],
        [FULL] * 4,
        [VMEM(MATRIX, BF16)] * 3 + [VMEM(WIDE, BF16)] + [DMA((2,))] * 2,
        cost=14.0,
        vmem=32,
    )
    token_got, fed_got = swap(token_send).astype(F32), swap(fed_send).astype(F32)
    own_rows, their_rows = fed_keep[0] + fed_got[1], fed_keep[1] + fed_got[0]
    by_sequence = lambda mine, theirs: jnp.where(
        core == 0, jnp.stack([mine, theirs]), jnp.stack([theirs, mine])
    )
    output = by_sequence(own_rows, their_rows)
    grad_tokens = by_sequence(token_keep, token_got)

    if near:
        qk_2 = stage(combined(*qk_1), BACK_QK[1])
        v_2 = stage(combined(*v_1), BACK_V[1])
        to_qk, to_v = combined(*qk_2), combined(*v_2)
        last = [jnp.concatenate([to_qk(k), to_v(k)]) for k in range(4)]
        last[1:] = [value.astype(BF16) for value in last[1:]]
        joined = final_sum(*stage(lambda k: last[k], "z"))
        own_small = joined[192]
        narrow = joined[:192].reshape(4, 48, 384)
        mine = lax.dynamic_slice_in_dim(narrow, core * 192, 192, axis=2)
        partner = swap(lax.dynamic_slice_in_dim(narrow, (1 - core) * 192, 192, axis=2))
        narrow = jnp.where(
            core == 0,
            jnp.concatenate([mine, partner], axis=1),
            jnp.concatenate([partner, mine], axis=1),
        )
        own_wide = final_sum(*wide_3)
        own_up, own_down = own_wide[96:], own_wide[:96].T
    else:
        gauss_grad = gauss_grad.reshape(2, 4, 3, dp_count, -1).transpose(3, 1, 0, 2, 4)
        small_grads = jnp.concatenate(
            [value.reshape(dp_count * 4, -1) for value in (gauss_grad, gain_part, bias_part)],
            axis=1,
        )
        own_small = lax.psum_scatter(small_grads, AXES, scatter_dimension=0)
        pieces = [
            whole_from([keep_qk, send_qk], BACK_QK).reshape(8, 2, 2, 2, 48, 384),
            whole_from([keep_out, send_out], BACK_V)[:, :, :, None],
            whole_from([keep_v, send_v], BACK_V)[:, :, :, None, :48],
        ]
        pieces = jnp.concatenate(pieces, axis=3).transpose(0, 2, 4, 3, 1, 5)
        pieces = pieces.reshape(dp_count, D // dp_count, 4, 4, 192).transpose(0, 3, 2, 1, 4)
        total = lambda value: lax.psum_scatter(value.astype(F32), AXES, scatter_dimension=0)
        narrow = total(pieces.reshape((-1,) + pieces.shape[2:]))

        def owned(keep, order):
            mine = whole_from([jnp.stack(keep)], order)
            both = jnp.concatenate(
                [jnp.where(core == at, mine, jnp.zeros_like(mine)) for at in range(2)], axis=2
            )
            both = both.transpose(0, 3, 1, 2, 4).reshape(dp_count, D // dp_count, 4, D)
            both = both.transpose(0, 2, 1, 3)
            return total(both.reshape((-1,) + both.shape[2:]))

        own_up, own_down = owned(keep_up, BACK_UP), owned(keep_down, BACK_DOWN).T
    own_qkv, own_out = jnp.concatenate([narrow[:2], narrow[3:]]), narrow[2].T
    return (
        output,
        grad_tokens,
        own_qkv,
        own_small[:gauss_size].reshape(w_gauss.shape),
        own_out,
        own_small[gauss_size : gauss_size + gain_size],
        own_small[gauss_size + gain_size : gauss_size + 2 * gain_size],
        own_up,
        own_down,
    )


def solution(mesh):
    return jax.shard_map(
        local,
        mesh=mesh,
        in_specs=(
            P("dp", "tensor", None),
            P("dp"),
            P("dp", None, None),
            P("dp", "tensor", None),
            P(None, "dp", "tensor"),
            P(None, "tensor", "dp"),
            P("tensor", "dp"),
            P(("dp", "tensor")),
            P(("dp", "tensor")),
            P("dp", "tensor"),
            P("tensor", "dp"),
        ),
        out_specs=(
            P("dp", "tensor", None),
            P("dp", "tensor", None),
            P(None, "dp", "tensor"),
            P(None, "tensor", "dp"),
            P("tensor", "dp"),
            P(("dp", "tensor")),
            P(("dp", "tensor")),
            P("dp", "tensor"),
            P("tensor", "dp"),
        ),
        check_vma=False,
    )
```

```python
import functools

import jax
import jax.numpy as jnp
import numpy as np
from jax import lax
from jax.experimental import pallas as pl
from jax.experimental.pallas import tpu as pltpu
from jax.sharding import PartitionSpec as P

D = 768
H = 12
DH = 64
NB = 256
SEGL = 512
FF = 3072
PAIRS = H // 2
AXES = ("dp", "tensor")
F32 = jnp.float32
BF16 = jnp.bfloat16
BASIS_VAR = (1.0 / NB) ** 2
VMEM = pltpu.VMEM
SMEM = pltpu.SMEM


def ridge_matrix():
    centres = (np.arange(NB) + 0.5) / NB
    samples = (np.arange(SEGL) + 0.5) / SEGL
    rows = np.exp(-0.5 * ((samples[None, :] - centres[:, None]) * NB) ** 2)
    gram = rows @ rows.T + 0.5 * np.eye(NB)
    return np.linalg.solve(gram, rows).astype(np.float32).astype(jnp.bfloat16)


SIZES = {"z": 4, "y": 2, "x": 2, "c": 2}


def xor_permute(value, letter, k):
    dp_mask, tensor_mask = {"z": (2 * k, 0), "y": (k, 0), "x": (0, 2 * k), "c": (0, k)}[letter]
    dp_count, rank_count = lax.axis_size("dp"), lax.axis_size("tensor")
    pairs = [
        (d * rank_count + t, (d ^ dp_mask) * rank_count + (t ^ tensor_mask))
        for d in range(dp_count)
        for t in range(rank_count)
    ]
    return lax.ppermute(value, AXES, pairs)


def swap(value):
    return xor_permute(value, "c", 1)


def after(value, *others):
    return lax.optimization_barrier((value,) + others)[0]


def piece_table(order, cores=2):
    first, second, third = order
    table = []
    for at, (kc, k3) in enumerate([(0, 0), (0, 1), (1, 0), (1, 1)][: 2 * cores]):
        for i2 in range(SIZES[second]):
            for i1 in range(SIZES[first]):
                k = {first: i1, second: i2, third: k3}
                table.append((at, (i2, i1), k["z"] * 2 + k["y"], k["x"], kc))
    return table


def wide_table():
    return [
        (2 * ky + kx, (kz,), 2 * kz + ky, kx, 0)
        for ky in range(2)
        for kx in range(2)
        for kz in range(4)
    ]


def spread(piece, letter):
    return [piece] + [xor_permute(piece, letter, k) for k in range(1, SIZES[letter])]


def as_gathered(whole, order):
    first, second, third = order
    whole = whole.reshape((4, 2) + whole.shape[1:])
    at = {"z": 0, "y": 1, "x": 2, "c": 3}
    rest = list(range(4, whole.ndim))
    whole = whole.transpose([at["c"], at[third], at[second], at[first]] + rest)
    return [whole[0, 0], whole[0, 1], whole[1, 0], whole[1, 1]]


def stage(total, letter):
    own = total(0)
    arrived = [xor_permute(total(k).astype(BF16), letter, k) for k in range(1, SIZES[letter])]
    return own, arrived


def combined(own, arrived):
    return lambda k: sum((a[k].astype(F32) for a in arrived), own[k].astype(F32))


def final_sum(own, arrived):
    return sum((a.astype(F32) for a in arrived), own)


def whole_from(parts, order):
    first, second, third = order
    whole = jnp.stack(parts)
    at = {"c": 0, first: 1, second: 2, third: 3}
    rest = list(range(4, whole.ndim))
    whole = whole.transpose([at["z"], at["y"], at["x"], at["c"]] + rest)
    return whole.reshape((8,) + whole.shape[2:])


def exact_triple(value):
    high = lax.reduce_precision(value, 8, 7)
    middle = lax.reduce_precision(value - high, 8, 7)
    return [part.astype(BF16) for part in (high, middle, value - high - middle)]


def dot(left, right, left_dim=1, right_dim=0):
    return lax.dot_general(
        left, right, (((left_dim,), (right_dim,)), ((), ())), preferred_element_type=F32
    )


def flip(value):
    return jnp.transpose(value.astype(F32))


def aligned(value, step):
    return pl.multiple_of(value * step, step)


def wide_copies(info, table, arrays, target, sems):
    for at, index, r, kx, _ in table:
        rows = pl.ds(aligned(info[0] ^ r, 96), 96)
        yield pltpu.make_async_copy(
            arrays[at].at[index], target.at[rows, pl.ds(kx * D, D)], sems.at[kx]
        )


def wait_wide(target, sems, j):
    block = target.at[:, pl.ds(j * D, D)]
    pltpu.make_async_copy(block, block, sems.at[j]).wait()


def narrow_copies(info, table, arrays, spots, sem):
    for at, index, r, kx, kc in table:
        rows = pl.ds(pl.multiple_of((info[0] ^ r) * 96 + (info[2] ^ kc) * 48, 48), 48)
        columns = pl.ds(aligned(info[1] ^ kx, 384), 384)
        for first, target in spots:
            yield pltpu.make_async_copy(
                arrays[at].at[index + (pl.ds(first, 48),)], target.at[rows, columns], sem
            )


def wait_whole(target, sem):
    pltpu.make_async_copy(target, target, sem).wait()


def out_narrow(info, order, keep, send, spots, sem):
    for index, r, kx, kc in scatter_table(order):
        rows = pl.ds(pl.multiple_of((info[0] ^ r) * 96 + (info[2] ^ kc) * 48, 48), 48)
        columns = pl.ds(aligned(info[1] ^ kx, 384), 384)
        for first, source in spots:
            yield pltpu.make_async_copy(
                source.at[rows, columns], (keep, send)[kc].at[index + (pl.ds(first, 48),)], sem
            )


def scatter_table(order, cores=2):
    a, b, c = order
    table = []
    for kc in range(cores):
        for i in range(SIZES[a]):
            for j in range(SIZES[b]):
                for l in range(SIZES[c]):
                    k = {a: i, b: j, c: l}
                    table.append(((i, j, l), k["z"] * 2 + k["y"], k["x"], kc))
    return table


def column_validity(info):
    return (lax.broadcasted_iota(jnp.int32, (SEGL, 1), 0) < info[3]).astype(F32)


def small_layout():
    column = np.arange(D)
    owner = [(column % DH // 8) * 4 + column // 192, column // 24]
    place = [column // DH % 3 * 8 + column % 8, 48 + column % 24]
    return np.stack(owner + place + [column] * 4).astype(np.int32)


def small_places(layout, i, count):
    row = lax.broadcasted_iota(jnp.int32, (count, D), 0)
    place = layout[2 + i // 2][None] + 24 * (i % 2)
    hit = row == place
    if i > 1 and count > 128:
        hit = hit | (row == place + 48) | (row == place + 96)
    return hit.astype(F32).astype(BF16)


def small_masks(info, table, owner):
    row = lax.broadcasted_iota(jnp.int32, (512, D), 0)
    device = row * 0 - 1
    me = info[0] * 4 + info[1] * 2 + info[2]
    for n, (_, _, r, kx, kc) in enumerate(table):
        device = jnp.where(row == 16 * n, me ^ (r * 4 + kx * 2 + kc), device)
    return device == owner[0:1], device == owner[1:2]


def qkv_kernel(table_qk, table_v, near, info, own, other, ridge, *refs):
    qk, v_parts = refs[0:4], refs[4:8]
    if near:
        layout = refs[8][...]
        refs = refs[:8] + refs[9:]
    x_out, q_out, k_out, v_out, coef_out = refs[8:13]
    if near:
        gauss_out, gain_out, bias_out = refs[13:16]
        refs = refs[:13] + refs[16:]
    wq, wk, wv, small, sems = refs[13:]
    copies = list(narrow_copies(info, table_qk, qk, [(0, wq), (48, wk)], sems.at[0]))
    copies += list(narrow_copies(info, table_v, v_parts, [(0, wv)], sems.at[1]))
    if near:
        for n, (at, index, _, _, _) in enumerate(table_v):
            copies.append(
                pltpu.make_async_copy(
                    v_parts[at].at[index + (pl.ds(96, 16),)], small.at[pl.ds(16 * n, 16)], sems.at[2]
                )
            )
    for copy in copies:
        copy.start()
    core = info[5]
    x_out[pl.ds(aligned(core, 256), 256), :] = own[core]
    x_out[pl.ds(aligned(1 - core, 256), 256), :] = other[core]
    scale = column_validity(info) * info[4].astype(F32)
    pair_wait = pltpu.make_async_copy(wq, wq, sems.at[0])
    pair_wait.wait()
    pair_wait.wait()

    def project(w, out):
        @pl.loop(0, 3)
        def _(step):
            at = pl.ds(aligned(step, 256), 256)
            out[:, at] = dot(x_out[...], w[:, at]).astype(BF16)

    project(wq, q_out)
    project(wk, k_out)
    wait_whole(wv, sems.at[1])

    @pl.loop(0, 3)
    def _(step):
        at = pl.ds(aligned(step, 256), 256)
        values = dot(x_out[...], wv[:, at]).astype(BF16)
        v_out[:, at] = values
        pooled = (values.astype(F32) * scale).astype(BF16)
        coef_out[:, at] = dot(ridge[...], pooled).astype(BF16)

    if near:
        wait_whole(small, sems.at[2])
        gauss_mask, scale_mask = small_masks(info, table_v, layout)
        rows = small[:, :256]

        def collect(at, mask):
            return jnp.sum(jnp.where(mask, dot(rows, small_places(layout, at, 256)), 0.0), axis=0, keepdims=True)

        means, variances = collect(0, gauss_mask), collect(1, gauss_mask)
        gain_out[...] = collect(2, scale_mask)
        bias_out[...] = collect(3, scale_mask)
        row = lax.broadcasted_iota(jnp.int32, (16, 128), 0)
        for p in range(PAIRS):
            at = slice(128 * p, 128 * (p + 1))
            value = jnp.where(row < 2, means[:, at], variances[:, at])
            for h in range(2):
                value = jnp.where((row % 2 == h) & ~half_lanes(h), 0.0, value)
            gauss_out[p] = jnp.where(row < 4, value, 0.0).astype(BF16)


def density_rows(logits, h):
    mean_logit, var_logit = logits[h : h + 1], logits[2 + h : 3 + h]
    mu = jax.nn.sigmoid(mean_logit)
    softplus = jnp.maximum(var_logit, 0.0) + jnp.log1p(jnp.exp(-jnp.abs(var_logit)))
    return mu, 0.05 * softplus + BASIS_VAR, var_logit


def centre_column():
    return (lax.broadcasted_iota(jnp.int32, (NB, 1), 0).astype(F32) + 0.5) / NB


def half_lanes(h):
    lane = lax.broadcasted_iota(jnp.int32, (1, 128), 1)
    return (lane < DH) if h == 0 else (lane >= DH)


def attend_kernel(info, q, k, v, gauss, attn_t, local_t, dens_t, bias):
    @pl.when(pl.program_id(0) == 0)
    def _():
        key = lax.broadcasted_iota(jnp.int32, (SEGL, SEGL), 0)
        query = lax.broadcasted_iota(jnp.int32, (SEGL, SEGL), 1)
        allowed = ((key < query) & (key < info[3])) | (key == query)
        bias[...] = jnp.where(allowed, 0.0, -1e30)

    values_t = flip(v[...]).astype(BF16)
    logits = dot(gauss[0], q[...], 1, 1)
    centres = centre_column()
    for h in range(2):
        rows = slice(h * DH, (h + 1) * DH)
        keys = jnp.where(half_lanes(h), k[...].astype(F32) * DH**-0.5, 0.0).astype(BF16)
        for block in range(2):
            n = 256 * (block + 1)
            at = slice(256 * block, n)
            scores = dot(keys[:n], q[at], 1, 1) + bias[:n, at]
            exponent = jnp.exp(scores - jnp.max(scores, axis=0, keepdims=True))
            total = jnp.sum(exponent, axis=0, keepdims=True)
            probs = (exponent * (1.0 / total)).astype(BF16)
            attn_t[h, :n, at] = probs
            local_t[rows, at] = dot(values_t[rows, :n], probs)
        mu, spread, _ = density_rows(logits, h)
        offset = mu - centres
        dens_t[h] = (
            jnp.sqrt(BASIS_VAR / spread) * jnp.exp(offset * offset * (-0.5 / spread))
        ).astype(BF16)


def layer_stats(residual):
    mean = jnp.mean(residual, axis=-1, keepdims=True)
    centred = residual - mean
    return centred, lax.rsqrt(jnp.mean(centred * centred, axis=-1, keepdims=True) + 1e-05)


def recall_kernel(table, info, dens_t, coef, local_t, x, gain, bias, *refs):
    parts = refs[0:4]
    heads_out, residual, normed = refs[4:7]
    w_out, sem = refs[7:]
    step = pl.program_id(0)

    @pl.when(step == 0)
    def _():
        for copy in narrow_copies(info, table, parts, [(48, w_out)], sem):
            copy.start()

    coef_t = flip(coef[...]).astype(BF16)
    recalled = [dot(coef_t[h * DH : (h + 1) * DH], dens_t[h]) for h in range(2)]
    both = local_t[...] + jnp.concatenate(recalled, axis=0)
    heads_out[:, pl.ds(aligned(step, 128), 128)] = flip(both).astype(BF16)

    @pl.when(step == PAIRS - 1)
    def _():
        wait_whole(w_out, sem)

        @pl.loop(0, 3)
        def _(chunk):
            at = pl.ds(aligned(chunk, 256), 256)
            residual[:, at] = x[:, at].astype(F32) + dot(heads_out[...], w_out[at, :], 1, 1)

        centred, scale = layer_stats(residual[...])
        normed[...] = (centred * scale * gain[...] + bias[...]).astype(BF16)


def gelu_parts(pre):
    c0, c1 = 0.7978845608028654, 0.044715
    square = pre * pre
    inner = jnp.tanh(c0 * pre * (1.0 + c1 * square))
    half = 0.5 * (1.0 + inner)
    slope = half + 0.5 * pre * (1.0 - inner * inner) * (c0 * (1.0 + 3.0 * c1 * square))
    return pre * half, slope


def wide_out(info, order, keep, source, sems):
    for index, r, kx, _ in scatter_table(order, 1):
        rows = pl.ds(aligned(info[0] ^ r, 96), 96)
        yield kx, pltpu.make_async_copy(
            source.at[rows, pl.ds(kx * D, D)], keep[index[0]].at[index[1:]], sems.at[kx]
        )


def wait_out(source, sems):
    for j in range(2):
        wait_wide(source, sems, j)


def up_kernel(table, order, info, own, other, seed_t, *refs):
    parts = refs[0:4]
    hidden_out, slope_out = refs[4:6]
    keep = refs[6:8]
    w_up, grad, hidden, slope, sems, out_sems, side_sems = refs[8:]
    for copy in wide_copies(info, table, parts, w_up, sems):
        copy.start()
    outs = list(wide_out(info, order, keep, grad, out_sems))
    for j in range(2):
        wait_wide(w_up, sems, j)

        @pl.loop(0, 3)
        def _(chunk):
            at = pl.ds(pl.multiple_of(j * D + chunk * 256, 256), 256)
            sums = []
            for half, source in enumerate((own, other)):
                value, derivative = gelu_parts(dot(source[...], w_up[:, at]))
                value = value.astype(BF16)
                hidden[half, :, at] = value
                slope[half, :, at] = derivative.astype(BF16)
                sums.append(dot(seed_t[:, half * SEGL : (half + 1) * SEGL], value))
            grad[:, at] = (sums[0] + sums[1]).astype(BF16)
            for i, (source, target) in enumerate(((hidden, hidden_out), (slope, slope_out))):
                pltpu.make_async_copy(
                    source.at[:, :, at], target.at[:, :, at], side_sems.at[i]
                ).start()

        for owner, copy in outs:
            if owner == j:
                copy.start()
    wait_out(grad, out_sems)
    wait_whole(hidden, side_sems.at[0])
    wait_whole(slope, side_sems.at[1])


def down_kernel(tables, order, info, seed, own, other, slope_in, *refs):
    down_parts, up_parts = refs[0:4], refs[4:8]
    keep = refs[8:10]
    own_grad, other_grad = refs[10:12]
    w_down, w_up, grad, slope, hidden_grad, normed_t = refs[12:18]
    down_sems, up_sems, out_sems, side_sems = refs[18:]
    for copy in wide_copies(info, tables[0], down_parts, w_down, down_sems):
        copy.start()
    for copy in wide_copies(info, tables[1], up_parts, w_up, up_sems):
        copy.start()
    for j in range(2):
        at = pl.ds(j * D, D)
        pltpu.make_async_copy(slope_in.at[:, :, at], slope.at[:, :, at], side_sems.at[j]).start()
    outs = list(wide_out(info, order, keep, grad, out_sems))
    normed_t[:, :SEGL] = flip(own[...]).astype(BF16)
    normed_t[:, SEGL:] = flip(other[...]).astype(BF16)
    for j in range(2):
        wait_wide(w_down, down_sems, j)
        wait_wide(w_up, up_sems, j)
        wait_whole(slope.at[:, :, pl.ds(j * D, D)], side_sems.at[j])

        @pl.loop(0, 3)
        def _(chunk):
            at = pl.ds(pl.multiple_of(j * D + chunk * 256, 256), 256)
            sums = []
            for half in range(2):
                back = dot(seed[half], w_down[:, at]).astype(BF16).astype(F32)
                back = (back * slope[half, :, at].astype(F32)).astype(BF16)
                sums.append(dot(normed_t[:, half * SEGL : (half + 1) * SEGL], back))
                hidden_grad[half, :, at] = back
            grad[:, at] = (sums[0] + sums[1]).astype(BF16)

        for owner, copy in outs:
            if owner == j:
                copy.start()

    @pl.loop(0, 3)
    def _(chunk):
        at = pl.ds(aligned(chunk, 256), 256)
        own_grad[:, at] = dot(hidden_grad[0], w_up[at, :], 1, 1)
        other_grad[:, at] = dot(hidden_grad[1], w_up[at, :], 1, 1).astype(BF16)

    wait_out(grad, out_sems)


def mix_back_kernel(table, order, info, own, other, seed, residual, gain, heads_out, dens_t, *refs):
    parts = refs[0:4]
    resid_grad, head_grad, coef_grad, gain_grad, bias_grad, keep, send = refs[4:11]
    w_out, grad, mix, mix_t, sem, out_sem = refs[11:]
    step = pl.program_id(0)

    @pl.when(step == 0)
    def _():
        for copy in narrow_copies(info, table, parts, [(48, w_out)], sem):
            copy.start()
        normed_grad = (own[...] + other[...].astype(F32)).astype(BF16).astype(F32)
        centred, scale = layer_stats(residual[...])
        unit = centred * scale
        gain_grad[...] = jnp.sum(normed_grad * unit, axis=0, keepdims=True)
        bias_grad[...] = jnp.sum(normed_grad, axis=0, keepdims=True)
        back = normed_grad * gain[...]
        back = back - jnp.mean(back, axis=-1, keepdims=True) - unit * jnp.mean(
            back * unit, axis=-1, keepdims=True
        )
        back = seed[0].astype(F32) + scale * back
        resid_grad[...] = back
        mix[...] = back.astype(BF16)
        mix_t[...] = flip(mix[...]).astype(BF16)
        wait_whole(w_out, sem)

        @pl.loop(0, 3)
        def _(chunk):
            at = pl.ds(aligned(chunk, 256), 256)
            head_grad[:, at] = dot(mix[...], w_out[:, at]).astype(BF16)
            grad[:, at] = dot(mix_t[...], heads_out[:, at]).astype(BF16)

        for copy in out_narrow(info, order, keep, send, [(0, grad)], out_sem):
            copy.start()

    pair_grad = head_grad[:, pl.ds(aligned(step, 128), 128)].astype(F32)
    sums = [
        dot(dens_t[h], jnp.where(half_lanes(h), pair_grad, 0.0).astype(BF16)) for h in range(2)
    ]
    coef_grad[...] = (sums[0] + sums[1]).astype(BF16)

    @pl.when(step == PAIRS - 1)
    def _():
        wait_whole(grad, out_sem)


def attend_back_kernel(
    attn_t, q, k, v, grad, local_t, dens_t, coef, gauss, *refs
):
    dq_out, dk_out, dv_out, gauss_grad, dq_t, dk_sum, dv_sum, rows_of = refs
    keys_t = flip(k[...]).astype(BF16)
    grad_t = flip(grad[...])
    logits = dot(gauss[0], q[...], 1, 1)
    centres = centre_column()
    gauss_columns = flip(gauss[0])
    dk_sum[...] = jnp.zeros_like(dk_sum)
    dv_sum[...] = jnp.zeros_like(dv_sum)
    rows_of[...] = jnp.zeros_like(rows_of)
    only = lambda h, value: jnp.where(half_lanes(h), value.astype(F32), 0.0).astype(BF16)
    for h in range(2):
        rows = slice(h * DH, (h + 1) * DH)
        values, queries, grads = only(h, v[...]), only(h, q[...]), only(h, grad[...])
        delta = jnp.sum(grad_t[rows] * local_t[rows], axis=0, keepdims=True)
        for block in range(2):
            n = 256 * (block + 1)
            at = slice(256 * block, n)
            probs = attn_t[h, :n, at]
            prob_grad = dot(values[:n], grad[at], 1, 1)
            score_grad = (probs.astype(F32) * (prob_grad - delta[:, at])).astype(BF16)
            dv_sum[:n] += dot(probs, grads[at])
            dk_sum[:n] += dot(score_grad, queries[at])
            dq_t[rows, at] = dot(keys_t[rows, :n], score_grad) * DH**-0.5
        mu, spread, var_logit = density_rows(logits, h)
        inverse = 1.0 / spread
        offset = mu - centres
        weighted = dot(only(h, coef[...]), grad[...], 1, 1) * dens_t[h].astype(F32)
        first = weighted * offset
        sum0 = jnp.sum(weighted, axis=0, keepdims=True)
        sum1 = jnp.sum(first, axis=0, keepdims=True)
        sum2 = jnp.sum(first * offset, axis=0, keepdims=True)
        mean_grad = -sum1 * inverse * mu * (1.0 - mu)
        spread_grad = 0.5 * inverse * (sum2 * inverse - sum0)
        var_grad = spread_grad * 0.05 * jax.nn.sigmoid(var_logit)
        rows_of[h : h + 1] = mean_grad
        rows_of[2 + h : 3 + h] = var_grad
        column = gauss_columns[rows]
        dq_t[rows] += column[:, h : h + 1] * mean_grad + column[:, 2 + h : 3 + h] * var_grad
    dq_out[...] = jnp.transpose(dq_t[...]).astype(BF16)
    dk_out[...] = (dk_sum[...] * DH**-0.5).astype(BF16)
    dv_out[...] = dv_sum[...]
    high = rows_of[...].astype(BF16)
    both = dot(high, q[...]) + dot((rows_of[...] - high.astype(F32)).astype(BF16), q[...])
    gauss_grad[0:1] = jnp.where(half_lanes(0), both[0:1], both[1:2])
    gauss_grad[1:2] = jnp.where(half_lanes(0), both[2:3], both[3:4])


def qkv_grad_kernel(orders, near, info, x, dq, dk, dv, coef_grad, ridge_t, *refs):
    if near:
        gauss_grad, gain_grad, bias_grad = refs[:3]
        layout = refs[3][...]
        refs = refs[4:]
    keep_qk, send_qk, keep_v, send_v, dv_out, x_t, gq, gk, gv, small, sems = refs
    x_t[...] = flip(x[...]).astype(BF16)
    scale = column_validity(info) * info[4].astype(F32)

    def weight(source, out):
        @pl.loop(0, 3)
        def _(chunk):
            at = pl.ds(aligned(chunk, 256), 256)
            out[:, at] = dot(x_t[...], source[:, at]).astype(BF16)

    weight(dq, gq)
    weight(dk, gk)
    for copy in out_narrow(info, orders[0], keep_qk, send_qk, [(0, gq), (48, gk)], sems.at[0]):
        copy.start()

    @pl.loop(0, 3)
    def _(chunk):
        at = pl.ds(aligned(chunk, 256), 256)
        pooled_grad = dot(ridge_t[...], coef_grad[:, at])
        dv_out[:, at] = (dv[:, at] + pooled_grad * scale).astype(BF16)
        gv[:, at] = dot(x_t[...], dv_out[:, at]).astype(BF16)

    for copy in out_narrow(info, orders[1], keep_v, send_v, [(0, gv)], sems.at[1]):
        copy.start()
    if near:
        table = scatter_table(orders[1])
        gauss_mask, scale_mask = small_masks(info, [(0,) + row for row in table], layout)
        rows = (
            (gauss_mask, gauss_grad[0:1]),
            (gauss_mask, gauss_grad[1:2]),
            (scale_mask, gain_grad[...]),
            (scale_mask, bias_grad[...]),
        )
        small[...] = jnp.zeros_like(small)
        small[:, :128] = sum(
            dot(jnp.where(mask, row, 0.0).astype(BF16), small_places(layout, i, 128), 1, 1)
            for i, (mask, row) in enumerate(rows)
        ).astype(BF16)
        for n, (index, _, _, kc) in enumerate(table):
            pltpu.make_async_copy(
                small.at[pl.ds(16 * n, 16)],
                (keep_v, send_v)[kc].at[index + (pl.ds(48, 16),)],
                sems.at[2],
            ).start()
        wait_whole(small, sems.at[2])
    both = pltpu.make_async_copy(gq, gq, sems.at[0])
    both.wait()
    both.wait()
    wait_whole(gv, sems.at[1])


def finish_kernel(tables, info, dq, dk, dv, resid_grad, hidden, residual, *refs):
    qk, v_parts, down_parts = refs[0:4], refs[4:8], refs[8:12]
    token_keep, token_send, fed_keep, fed_send = refs[12:16]
    wq, wk, wv, w_down, sems, down_sems = refs[16:]
    for copy in narrow_copies(info, tables[0], qk, [(0, wq), (48, wk)], sems.at[0]):
        copy.start()
    for copy in narrow_copies(info, tables[1], v_parts, [(0, wv)], sems.at[1]):
        copy.start()
    for copy in wide_copies(info, tables[2], down_parts, w_down, down_sems):
        copy.start()
    first = info[5] == 0

    def split(value):
        top, bottom = value[:HALF_SEG], value[HALF_SEG:]
        return jnp.where(first, top, bottom), jnp.where(first, bottom, top).astype(BF16)

    pair_wait = pltpu.make_async_copy(wq, wq, sems.at[0])
    pair_wait.wait()
    pair_wait.wait()
    wait_whole(wv, sems.at[1])

    @pl.loop(0, 3)
    def _(chunk):
        at = pl.ds(aligned(chunk, 256), 256)
        part = dot(dq[...], wq[at, :], 1, 1) + dot(dk[...], wk[at, :], 1, 1)
        value = resid_grad[:, at] + part + dot(dv[...], wv[at, :], 1, 1)
        token_keep[:, at], token_send[:, at] = split(value)

    wait_out(w_down, down_sems)

    @pl.loop(0, 3)
    def _(chunk):
        at = pl.ds(aligned(chunk, 256), 256)
        value = residual[:, at] + dot(hidden[0], w_down[at, :], 1, 1)
        fed_keep[0, :, at], fed_send[0, :, at] = split(value)
        value = dot(hidden[1], w_down[at, :], 1, 1)
        fed_keep[1, :, at], fed_send[1, :, at] = split(value)


FULL = pl.BlockSpec()
ANY = pl.BlockSpec(memory_space=pl.ANY)
FREE = pl.BlockSpec((SEGL, D), lambda: (0, 0))
FREE_ROWS = pl.BlockSpec((SEGL, D), lambda p: (0, 0))
SCALARS = pl.BlockSpec(memory_space=SMEM)
MATRIX = (D, D)
HALF = FF // 2
HALF_SEG = SEGL // 2
WIDE = (D, HALF)
DMA = pltpu.SemaphoreType.DMA


def shape(dims, dtype=BF16):
    return jax.ShapeDtypeStruct(dims, dtype)


def run(body, name, args, in_specs, outs, out_specs, scratch=(), grid=None, cost=5.0, vmem=48):
    kwargs = {} if grid is None else {"grid": grid}
    args = [
        value
        if any(spec is free for free in (SCALARS, FREE, FREE_ROWS))
        else pltpu.with_memory_space_constraint(value, pltpu.HBM)
        for value, spec in zip(args, in_specs)
    ]
    return pl.pallas_call(
        body,
        name=name,
        out_shape=tuple(pltpu.HBM(out.shape, out.dtype) for out in outs),
        in_specs=list(in_specs),
        out_specs=tuple(out_specs),
        scratch_shapes=list(scratch),
        cost_estimate=pl.CostEstimate(
            flops=int(cost * 2e8), bytes_accessed=int(1e6), transcendentals=0
        ),
        compiler_params=pltpu.CompilerParams(vmem_limit_bytes=vmem * 1024 * 1024),
        **kwargs,
    )(*args)


PAIR_COLUMNS = pl.BlockSpec((SEGL, 128), lambda p: (0, p))
PAIR_ROWS = pl.BlockSpec((128, SEGL), lambda p: (p, 0))
PAIR_COEF = pl.BlockSpec((NB, 128), lambda p: (0, p))
PAIR_ATTN = pl.BlockSpec((2, SEGL, SEGL), lambda p: (p, 0, 0))
PAIR_DENS = pl.BlockSpec((2, NB, SEGL), lambda p: (p, 0, 0))


def pair_block(*dims):
    return pl.BlockSpec((1,) + dims, lambda p: (p, 0, 0))


ORDER_QK, ORDER_V = "zyx", "zxy"
BACK_QK, BACK_V, BACK_UP, BACK_DOWN = "xyz", "yxz", "yxz", "xyz"


def local(
    tokens, lengths, mem_mask, cotangent, w_qkv, w_gauss, w_out, ln_gain, ln_bias, w_up, w_down
):
    dp_count = lax.axis_size("dp")
    dp, rank = lax.axis_index("dp"), lax.axis_index("tensor")
    core, segment = rank % 2, rank // 2
    near = dp_count == 8
    gauss_size, gain_size = w_gauss.size, ln_gain.size
    ridge = ridge_matrix()

    used = [
        jnp.clip(lax.dynamic_index_in_dim(lengths, at, 0, False) - segment * SEGL, 0, SEGL)
        for at in (core, 1 - core)
    ]
    pair = lax.dynamic_index_in_dim(mem_mask, core, 0, False)[1, 0]
    where = (dp, segment, core) if near else (0, 0, 0)
    info = jnp.stack([jnp.asarray(value, jnp.int32) for value in where + (used[0], pair, core)])

    their_tokens = swap(tokens)
    theirs = swap(cotangent)
    everything = jnp.where(
        core == 0,
        jnp.concatenate([cotangent, theirs], axis=1),
        jnp.concatenate([theirs, cotangent], axis=1),
    )
    seed = jnp.stack(
        [lax.dynamic_index_in_dim(everything, at, 0, False) for at in (core, 1 - core)]
    )
    seed = jnp.stack(
        [
            jnp.where(jnp.arange(SEGL)[:, None] < count, part, 0.0).astype(BF16)
            for count, part in zip(used, seed)
        ]
    )
    seed_t = seed.reshape(2 * SEGL, D).T

    projections = jnp.concatenate([w_qkv, w_out.T[None]])
    if near:
        mine = lax.dynamic_slice_in_dim(projections, core * 48, 48, axis=1)
        partner = swap(lax.dynamic_slice_in_dim(projections, (1 - core) * 48, 48, axis=1))
        projections = jnp.where(
            core == 0,
            jnp.concatenate([mine, partner], axis=2),
            jnp.concatenate([partner, mine], axis=2),
        )
        small = jnp.concatenate(
            [w_gauss.reshape(-1)] + exact_triple(jnp.concatenate([ln_gain, ln_bias]))
        )
        small_rows = jnp.pad(small[None], ((0, 15), (0, 384 - small.size)))
        packed = jnp.concatenate([projections.reshape(192, 384), small_rows])
        along_z = spread(after(packed, their_tokens, theirs), "z")
        along_z[1] = after(along_z[1], seed, seed_t, info)
        qk_near = jnp.stack(spread(jnp.stack([part[:96] for part in along_z]), "y"))
        v_near = jnp.stack(spread(jnp.stack([part[96:] for part in along_z]), "x"))
        qk_far, v_far = xor_permute(qk_near, "x", 1), xor_permute(v_near, "y", 1)
        qk_swap, v_swap = swap(qk_near), swap(v_near)
        up_z = spread(after(w_up, qk_swap, v_swap), "z")
        qk_parts = [qk_near, qk_far, qk_swap, swap(after(qk_far, *up_z[1:]))]
        v_parts = [v_near, v_far, v_swap, swap(after(v_far, *up_z[1:]))]
        up_z = after(jnp.stack(up_z), qk_parts[3], v_parts[3])
        up_x, up_y = xor_permute(up_z, "x", 1), xor_permute(up_z, "y", 1)
        down_z = spread(after(w_down.T, qk_parts[3], v_parts[3]), "z")
    else:
        every = lambda value: lax.all_gather(value, AXES, axis=0)
        cut = lambda value: value.reshape((8, dp_count // 8) + value.shape[1:])
        both = cut(every(projections).reshape(dp_count, 4, 4, -1, 192))
        both = both.transpose(0, 3, 1, 4, 2, 5).reshape(8, 4, 2, 48, 2, 384)
        both = both.transpose(0, 4, 2, 1, 3, 5)
        qk_parts = as_gathered(both[:, :, :, :2].reshape(8, 2, 2, 96, 384), ORDER_QK)
        v_parts = as_gathered(
            jnp.pad(both[:, :, :, 2:].reshape(8, 2, 2, 96, 384), ((0, 0),) * 3 + ((0, 16), (0, 0))),
            ORDER_V,
        )

        def wide(value):
            value = cut(every(value).reshape(dp_count, 4, -1, D)).transpose(0, 2, 1, 3, 4)
            value = value.reshape(8, 2, 2, 96, D)
            return lax.dynamic_slice_in_dim(value, core, 1, axis=2)

        def in_parts(whole):
            whole = whole.reshape((4, 2, 2) + whole.shape[3:])
            return [whole[:, ky, kx] for ky in range(2) for kx in range(2)]

        up_parts, down_parts = in_parts(wide(w_up)), in_parts(wide(w_down.T))
    table_qk, table_v = piece_table(ORDER_QK), piece_table(ORDER_V)
    table_wide = wide_table()

    tall = shape((SEGL, D))
    row = shape((1, D), F32)
    small_in, small_out = [], []
    if near:
        small_in = [jnp.asarray(small_layout())]
        small_out = [shape((PAIRS, 16, 128)), row, row]
    x, q, k, v, coef, *small_params = run(
        functools.partial(qkv_kernel, table_qk, table_v, near),
        "qkv",
        [info, tokens, their_tokens, jnp.asarray(ridge)] + qk_parts + v_parts + small_in,
        [SCALARS, FULL, FULL, FULL] + [ANY] * 8 + [FULL] * len(small_in),
        [tall] * 4 + [shape((NB, D))] + small_out,
        [FULL] * (5 + len(small_out)),
        [VMEM(MATRIX, BF16)] * 3 + [VMEM((512, 384), BF16), DMA((3,))],
        cost=6.0,
        vmem=24,
    )
    coef = lax.ppermute(coef, "tensor", [(0, 2), (1, 3)])

    q_late = q
    if near:
        q_late = after(q, up_x, up_y)
        up_parts = [up_z, up_x, up_y, xor_permute(after(up_x, q), "y", 1)]
        gauss_rows, norm_gain, norm_bias = small_params
    else:
        scales = every(jnp.stack([ln_gain, ln_bias]))
        gauss_parts = every(w_gauss.reshape(-1))
        norm_gain, norm_bias = scales[:, 0].reshape(1, D), scales[:, 1].reshape(1, D)
        gauss = gauss_parts.reshape(dp_count, 4, 2, 3, -1).transpose(2, 1, 3, 0, 4)
        gauss = gauss.reshape(2, PAIRS, 2, DH)
        spread_rows = jnp.eye(2, dtype=BF16)[None, None, :, :, None] * gauss[:, :, :, None, :]
        gauss_rows = spread_rows.transpose(1, 0, 2, 3, 4).reshape(PAIRS, 4, 128)
        gauss_rows = jnp.pad(gauss_rows, ((0, 0), (0, 12), (0, 0)))

    attn_t, local_t, dens_t = run(
        attend_kernel,
        "attend",
        [info, q_late, k, v, gauss_rows],
        [SCALARS] + [PAIR_COLUMNS] * 3 + [pair_block(16, 128)],
        [shape((H, SEGL, SEGL)), shape((D, SEGL), F32), shape((H, NB, SEGL))],
        [PAIR_ATTN, PAIR_ROWS, PAIR_DENS],
        [VMEM((SEGL, SEGL), F32)],
        grid=(PAIRS,),
        cost=12.0,
        vmem=14,
    )
    if near:
        down_z[1:] = lax.optimization_barrier((attn_t, coef, up_parts[3], *down_z[1:]))[3:]
        down_z = jnp.stack(down_z)
        down_x, down_y = xor_permute(down_z, "x", 1), xor_permute(down_z, "y", 1)
    whole = lambda *dims: pl.BlockSpec(dims, lambda p: (0,) * len(dims))
    heads_out, residual, normed = run(
        functools.partial(recall_kernel, table_v),
        "recall",
        [info, dens_t, coef, local_t, x, norm_gain, norm_bias] + v_parts,
        [SCALARS, PAIR_DENS, PAIR_COEF, PAIR_ROWS, whole(SEGL, D), whole(1, D), whole(1, D)]
        + [ANY] * 4,
        [tall, shape((SEGL, D), F32), tall],
        [whole(SEGL, D)] * 3,
        [VMEM(MATRIX, BF16), DMA(())],
        grid=(PAIRS,),
        cost=7.0,
        vmem=18,
    )
    if near:
        down_parts = [down_z, down_x, down_y, xor_permute(after(down_x, down_y, normed), "y", 1)]
    normed_other = swap(normed)
    piece_dims = lambda order: tuple(SIZES[letter] for letter in order)
    hidden, slope, *keep_down = run(
        functools.partial(up_kernel, table_wide, BACK_DOWN),
        "up",
        [info, normed, normed_other, seed_t] + up_parts,
        [SCALARS, FULL, FREE, FULL] + [ANY] * 4,
        [shape((2, SEGL, HALF))] * 2 + [shape(piece_dims(BACK_DOWN)[1:] + (96, D))] * 2,
        [ANY] * 4,
        [VMEM(WIDE, BF16)] * 2 + [VMEM((2, SEGL, HALF), BF16)] * 2 + [DMA((2,))] * 3,
        cost=12.0,
        vmem=22,
    )
    if near:
        down_1 = stage(lambda k: keep_down[k], BACK_DOWN[0])
    *keep_up, own_grad, other_grad = run(
        functools.partial(down_kernel, (table_wide, table_wide), BACK_UP),
        "down",
        [info, seed, normed, normed_other, slope] + down_parts + up_parts,
        [SCALARS] + [FULL] * 2 + [FREE] + [ANY] * 9,
        [shape(piece_dims(BACK_UP)[1:] + (96, D))] * 2 + [shape((SEGL, D), F32), tall],
        [ANY] * 2 + [FULL] * 2,
        [VMEM(WIDE, BF16)] * 3
        + [VMEM((2, SEGL, HALF), BF16)] * 2
        + [VMEM((D, 2 * SEGL), BF16)]
        + [DMA((2,))] * 4,
        cost=15.0,
        vmem=30,
    )
    if near:
        up_1 = stage(lambda k: keep_up[k], BACK_UP[0])
    other_grad = swap(other_grad)
    narrow_grad = [shape(piece_dims(BACK_V) + (48, 384))] * 2
    resid_grad, head_grad, coef_grad, gain_part, bias_part, keep_out, send_out = run(
        functools.partial(mix_back_kernel, table_v, BACK_V),
        "mix_back",
        [info, own_grad, other_grad, seed, residual, norm_gain, heads_out, dens_t] + v_parts,
        [SCALARS]
        + [whole(SEGL, D), FREE_ROWS, pl.BlockSpec((1, SEGL, D), lambda p: (0, 0, 0))]
        + [whole(SEGL, D), whole(1, D), whole(SEGL, D), PAIR_DENS]
        + [ANY] * 4,
        [shape((SEGL, D), F32), tall, shape((NB, D)), row, row] + narrow_grad,
        [whole(SEGL, D), whole(SEGL, D), PAIR_COEF, whole(1, D), whole(1, D)] + [ANY] * 2,
        [VMEM(MATRIX, BF16)] * 2
        + [VMEM((SEGL, D), BF16), VMEM((D, SEGL), BF16)]
        + [DMA(())] * 2,
        grid=(PAIRS,),
        cost=6.0,
        vmem=26,
    )
    coef_grad = lax.ppermute(coef_grad if not near else after(coef_grad, *down_1[1]), "tensor", [(2, 0), (3, 1)])
    if near:
        got_out = swap(send_out)
    dq, dk, dv, gauss_grad = run(
        attend_back_kernel,
        "attend_back",
        [attn_t, q, k, v, head_grad, local_t, dens_t, coef, gauss_rows],
        [PAIR_ATTN]
        + [PAIR_COLUMNS] * 4
        + [PAIR_ROWS, PAIR_DENS, PAIR_COEF, pair_block(16, 128)],
        [tall, tall, shape((SEGL, D), F32), shape((2, D), F32)],
        [PAIR_COLUMNS] * 3 + [pl.BlockSpec((2, 128), lambda p: (0, p))],
        [
            VMEM((128, SEGL), F32),
            VMEM((SEGL, 128), F32),
            VMEM((SEGL, 128), F32),
            VMEM((16, SEGL), F32),
        ],
        grid=(PAIRS,),
        cost=16.0,
        vmem=16,
    )
    if near:
        up_1 = (up_1[0], [after(a, dk, coef_grad, got_out) for a in up_1[1]])
        dq = after(dq, *up_1[1])
        down_1 = (down_1[0], [after(a, *up_1[1]) for a in down_1[1]])
        down_2 = stage(combined(*down_1), BACK_DOWN[1])
        up_2 = stage(combined(*up_1), BACK_UP[1])
    keep_qk, send_qk, keep_v, send_v, dv = run(
        functools.partial(qkv_grad_kernel, (BACK_QK, BACK_V), near),
        "qkv_grad",
        [info, x, dq, dk, dv, coef_grad, jnp.asarray(ridge.T)]
        + ([gauss_grad, gain_part, bias_part] + small_in if near else []),
        [SCALARS] + [FULL] * (10 if near else 6),
        [shape(piece_dims(BACK_QK) + (96, 384))] * 2
        + [shape(piece_dims(BACK_V) + (64, 384))] * 2
        + [tall],
        [ANY] * 4 + [FULL],
        [VMEM((D, SEGL), BF16)] + [VMEM(MATRIX, BF16)] * 3 + [VMEM((512, 384), BF16), DMA((3,))],
        cost=6.0,
        vmem=26,
    )

    if near:
        send_qk = after(send_qk, *down_2[1], *up_2[1])
        send_v = after(send_v, *down_2[1], *up_2[1])
        got_qk, got_v = swap(send_qk), swap(send_v)
        first_qk = [keep_qk[k].astype(F32) + got_qk[k].astype(F32) for k in range(2)]
        rest = ((keep_out, got_out), (keep_v, got_v))
        first_v = [
            jnp.concatenate([a[k].astype(F32) + b[k].astype(F32) for a, b in rest], axis=2)
            for k in range(2)
        ]
        first_qk[1], first_v[1] = first_qk[1].astype(BF16), first_v[1].astype(BF16)
        qk_1 = stage(lambda k: first_qk[k], BACK_QK[0])
        v_1 = stage(lambda k: first_v[k], BACK_V[0])
        down_2 = (down_2[0], [after(a, first_qk[1], first_v[1]) for a in down_2[1]])
        to_down, to_up = combined(*down_2), combined(*up_2)
        wide = [jnp.concatenate([to_down(k), to_up(k)]) for k in range(4)]
        wide[1:] = [value.astype(BF16) for value in wide[1:]]
        wide_3 = stage(lambda k: wide[k], "z")
        dq_late = after(dq, first_qk[1], first_v[1], *wide[1:])
    else:
        dq_late = dq

    token_keep, token_send, fed_keep, fed_send = run(
        functools.partial(finish_kernel, (table_qk, table_v, table_wide)),
        "finish",
        [info, dq_late, dk, dv, resid_grad, hidden, residual] + qk_parts + v_parts + down_parts,
        [SCALARS] + [FULL] * 6 + [ANY] * 12,
        [shape((HALF_SEG, D), F32), shape((HALF_SEG, D))]
        + [shape((2, HALF_SEG, D), F32), shape((2, HALF_SEG, D))],
        [FULL] * 4,
        [VMEM(MATRIX, BF16)] * 3 + [VMEM(WIDE, BF16)] + [DMA((2,))] * 2,
        cost=14.0,
        vmem=32,
    )
    if near:
        qk_1 = (qk_1[0], [after(value, token_send) for value in qk_1[1]])
        v_1 = (v_1[0], [after(value, token_send) for value in v_1[1]])
        qk_2 = stage(combined(*qk_1), BACK_QK[1])
        v_2 = stage(combined(*v_1), BACK_V[1])
        token_send = after(token_send, v_1[1][0], qk_1[1][0])
        fed_send = after(fed_send, v_1[1][0], qk_1[1][0])
    token_got, fed_got = swap(token_send).astype(F32), swap(fed_send).astype(F32)
    own_rows, their_rows = fed_keep[0] + fed_got[1], fed_keep[1] + fed_got[0]
    by_sequence = lambda mine, theirs: jnp.where(
        core == 0, jnp.stack([mine, theirs]), jnp.stack([theirs, mine])
    )
    output = by_sequence(own_rows, their_rows)
    grad_tokens = by_sequence(token_keep, token_got)

    if near:
        wide_3 = (wide_3[0], [after(a, *qk_1[1], *v_1[1]) for a in wide_3[1]])
        to_qk, to_v = combined(*qk_2), combined(*v_2)
        last = [jnp.concatenate([to_qk(k), to_v(k)]) for k in range(4)]
        last[1:] = [value.astype(BF16) for value in last[1:]]
        joined, arrived = stage(lambda k: last[k], "z")
        arrived[0] = after(arrived[0], output, grad_tokens)
        joined = final_sum(joined, arrived)
        own_small = joined[192]
        narrow = joined[:192].reshape(4, 48, 384)
        mine = lax.dynamic_slice_in_dim(narrow, core * 192, 192, axis=2)
        partner = swap(lax.dynamic_slice_in_dim(narrow, (1 - core) * 192, 192, axis=2))
        narrow = jnp.where(
            core == 0,
            jnp.concatenate([mine, partner], axis=1),
            jnp.concatenate([partner, mine], axis=1),
        )
        own_wide = final_sum(*wide_3)
        own_up, own_down = own_wide[96:], own_wide[:96].T
    else:
        gauss_grad = gauss_grad.reshape(2, 4, 3, dp_count, -1).transpose(3, 1, 0, 2, 4)
        small_grads = jnp.concatenate(
            [value.reshape(dp_count * 4, -1) for value in (gauss_grad, gain_part, bias_part)],
            axis=1,
        )
        own_small = lax.psum_scatter(small_grads, AXES, scatter_dimension=0)
        pieces = [
            whole_from([keep_qk, send_qk], BACK_QK).reshape(8, 2, 2, 2, 48, 384),
            whole_from([keep_out, send_out], BACK_V)[:, :, :, None],
            whole_from([keep_v, send_v], BACK_V)[:, :, :, None, :48],
        ]
        pieces = jnp.concatenate(pieces, axis=3).transpose(0, 2, 4, 3, 1, 5)
        pieces = pieces.reshape(dp_count, D // dp_count, 4, 4, 192).transpose(0, 3, 2, 1, 4)
        total = lambda value: lax.psum_scatter(value.astype(F32), AXES, scatter_dimension=0)
        narrow = total(pieces.reshape((-1,) + pieces.shape[2:]))

        def owned(keep, order):
            mine = whole_from([jnp.stack(keep)], order)
            both = jnp.concatenate(
                [jnp.where(core == at, mine, jnp.zeros_like(mine)) for at in range(2)], axis=2
            )
            both = both.transpose(0, 3, 1, 2, 4).reshape(dp_count, D // dp_count, 4, D)
            both = both.transpose(0, 2, 1, 3)
            return total(both.reshape((-1,) + both.shape[2:]))

        own_up, own_down = owned(keep_up, BACK_UP), owned(keep_down, BACK_DOWN).T
    own_qkv, own_out = jnp.concatenate([narrow[:2], narrow[3:]]), narrow[2].T
    return (
        output,
        grad_tokens,
        own_qkv,
        own_small[:gauss_size].reshape(w_gauss.shape),
        own_out,
        own_small[gauss_size : gauss_size + gain_size],
        own_small[gauss_size + gain_size : gauss_size + 2 * gain_size],
        own_up,
        own_down,
    )


def solution(mesh):
    return jax.shard_map(
        local,
        mesh=mesh,
        in_specs=(
            P("dp", "tensor", None),
            P("dp"),
            P("dp", None, None),
            P("dp", "tensor", None),
            P(None, "dp", "tensor"),
            P(None, "tensor", "dp"),
            P("tensor", "dp"),
            P(("dp", "tensor")),
            P(("dp", "tensor")),
            P("dp", "tensor"),
            P("tensor", "dp"),
        ),
        out_specs=(
            P("dp", "tensor", None),
            P("dp", "tensor", None),
            P(None, "dp", "tensor"),
            P(None, "tensor", "dp"),
            P("tensor", "dp"),
            P(("dp", "tensor")),
            P(("dp", "tensor")),
            P("dp", "tensor"),
            P("tensor", "dp"),
        ),
        check_vma=False,
    )
```

```python
import functools

import jax
import jax.numpy as jnp
import numpy as np
from jax import lax
from jax.experimental import pallas as pl
from jax.experimental.pallas import tpu as pltpu
from jax.sharding import PartitionSpec as P

D = 768
H = 12
DH = 64
NB = 256
SEGL = 512
FF = 3072
PAIRS = H // 2
AXES = ("dp", "tensor")
F32 = jnp.float32
BF16 = jnp.bfloat16
BASIS_VAR = (1.0 / NB) ** 2
VMEM = pltpu.VMEM
SMEM = pltpu.SMEM


def ridge_matrix():
    centres = (np.arange(NB) + 0.5) / NB
    samples = (np.arange(SEGL) + 0.5) / SEGL
    rows = np.exp(-0.5 * ((samples[None, :] - centres[:, None]) * NB) ** 2)
    gram = rows @ rows.T + 0.5 * np.eye(NB)
    return np.linalg.solve(gram, rows).astype(np.float32).astype(jnp.bfloat16)


SIZES = {"z": 4, "y": 2, "x": 2, "c": 2}


def xor_permute(value, letter, k):
    dp_mask, tensor_mask = {"z": (2 * k, 0), "y": (k, 0), "x": (0, 2 * k), "c": (0, k)}[letter]
    dp_count, rank_count = lax.axis_size("dp"), lax.axis_size("tensor")
    pairs = [
        (d * rank_count + t, (d ^ dp_mask) * rank_count + (t ^ tensor_mask))
        for d in range(dp_count)
        for t in range(rank_count)
    ]
    return lax.ppermute(value, AXES, pairs)


def swap(value):
    return xor_permute(value, "c", 1)


def after(value, *others):
    return lax.optimization_barrier((value,) + others)[0]


def piece_table(order, cores=2):
    first, second, third = order
    table = []
    for at, (kc, k3) in enumerate([(0, 0), (0, 1), (1, 0), (1, 1)][: 2 * cores]):
        for i2 in range(SIZES[second]):
            for i1 in range(SIZES[first]):
                k = {first: i1, second: i2, third: k3}
                table.append((at, (i2, i1), k["z"] * 2 + k["y"], k["x"], kc))
    return table


def wide_table():
    return [
        (2 * ky + kx, (kz,), 2 * kz + ky, kx, 0)
        for ky in range(2)
        for kx in range(2)
        for kz in range(4)
    ]


def spread(piece, letter):
    return [piece] + [xor_permute(piece, letter, k) for k in range(1, SIZES[letter])]


def as_gathered(whole, order):
    first, second, third = order
    whole = whole.reshape((4, 2) + whole.shape[1:])
    at = {"z": 0, "y": 1, "x": 2, "c": 3}
    rest = list(range(4, whole.ndim))
    whole = whole.transpose([at["c"], at[third], at[second], at[first]] + rest)
    return [whole[0, 0], whole[0, 1], whole[1, 0], whole[1, 1]]


def stage(total, letter):
    own = total(0)
    arrived = [xor_permute(total(k).astype(BF16), letter, k) for k in range(1, SIZES[letter])]
    return own, arrived


def combined(own, arrived):
    return lambda k: sum((a[k].astype(F32) for a in arrived), own[k].astype(F32))


def final_sum(own, arrived):
    return sum((a.astype(F32) for a in arrived), own)


def whole_from(parts, order):
    first, second, third = order
    whole = jnp.stack(parts)
    at = {"c": 0, first: 1, second: 2, third: 3}
    rest = list(range(4, whole.ndim))
    whole = whole.transpose([at["z"], at["y"], at["x"], at["c"]] + rest)
    return whole.reshape((8,) + whole.shape[2:])


def exact_triple(value):
    high = lax.reduce_precision(value, 8, 7)
    middle = lax.reduce_precision(value - high, 8, 7)
    return [part.astype(BF16) for part in (high, middle, value - high - middle)]


def dot(left, right, left_dim=1, right_dim=0):
    return lax.dot_general(
        left, right, (((left_dim,), (right_dim,)), ((), ())), preferred_element_type=F32
    )


def flip(value):
    return jnp.transpose(value.astype(F32))


def aligned(value, step):
    return pl.multiple_of(value * step, step)


def wide_copies(info, table, arrays, target, sems):
    for at, index, r, kx, _ in table:
        rows = pl.ds(aligned(info[0] ^ r, 96), 96)
        yield pltpu.make_async_copy(
            arrays[at].at[index], target.at[rows, pl.ds(kx * D, D)], sems.at[kx]
        )


def wait_wide(target, sems, j):
    block = target.at[:, pl.ds(j * D, D)]
    pltpu.make_async_copy(block, block, sems.at[j]).wait()


def narrow_copies(info, table, arrays, spots, sem):
    for at, index, r, kx, kc in table:
        rows = pl.ds(pl.multiple_of((info[0] ^ r) * 96 + (info[2] ^ kc) * 48, 48), 48)
        columns = pl.ds(aligned(info[1] ^ kx, 384), 384)
        for first, target in spots:
            yield pltpu.make_async_copy(
                arrays[at].at[index + (pl.ds(first, 48),)], target.at[rows, columns], sem
            )


def wait_whole(target, sem):
    pltpu.make_async_copy(target, target, sem).wait()


def out_narrow(info, order, keep, send, spots, sem):
    for index, r, kx, kc in scatter_table(order):
        rows = pl.ds(pl.multiple_of((info[0] ^ r) * 96 + (info[2] ^ kc) * 48, 48), 48)
        columns = pl.ds(aligned(info[1] ^ kx, 384), 384)
        for first, source in spots:
            yield pltpu.make_async_copy(
                source.at[rows, columns], (keep, send)[kc].at[index + (pl.ds(first, 48),)], sem
            )


def scatter_table(order, cores=2):
    a, b, c = order
    table = []
    for kc in range(cores):
        for i in range(SIZES[a]):
            for j in range(SIZES[b]):
                for l in range(SIZES[c]):
                    k = {a: i, b: j, c: l}
                    table.append(((i, j, l), k["z"] * 2 + k["y"], k["x"], kc))
    return table


def column_validity(info):
    return (lax.broadcasted_iota(jnp.int32, (SEGL, 1), 0) < info[3]).astype(F32)


def small_layout():
    column = np.arange(D)
    owner = [(column % DH // 8) * 4 + column // 192, column // 24]
    place = [column // DH % 3 * 8 + column % 8, 48 + column % 24]
    return np.stack(owner + place + [column] * 4).astype(np.int32)


def small_places(layout, i, count):
    row = lax.broadcasted_iota(jnp.int32, (count, D), 0)
    place = layout[2 + i // 2][None] + 24 * (i % 2)
    hit = row == place
    if i > 1 and count > 128:
        hit = hit | (row == place + 48) | (row == place + 96)
    return hit.astype(F32).astype(BF16)


def small_masks(info, table, owner):
    row = lax.broadcasted_iota(jnp.int32, (512, D), 0)
    device = row * 0 - 1
    me = info[0] * 4 + info[1] * 2 + info[2]
    for n, (_, _, r, kx, kc) in enumerate(table):
        device = jnp.where(row == 16 * n, me ^ (r * 4 + kx * 2 + kc), device)
    return device == owner[0:1], device == owner[1:2]


def qkv_kernel(table_qk, table_v, near, info, own, other, ridge, *refs):
    qk, v_parts = refs[0:4], refs[4:8]
    if near:
        layout = refs[8][...]
        refs = refs[:8] + refs[9:]
    x_out, q_out, k_out, v_out, coef_out = refs[8:13]
    if near:
        gauss_out, gain_out, bias_out = refs[13:16]
        refs = refs[:13] + refs[16:]
    wq, wk, wv, small, sems = refs[13:]
    copies = list(narrow_copies(info, table_qk, qk, [(0, wq), (48, wk)], sems.at[0]))
    copies += list(narrow_copies(info, table_v, v_parts, [(0, wv)], sems.at[1]))
    if near:
        for n, (at, index, _, _, _) in enumerate(table_v):
            copies.append(
                pltpu.make_async_copy(
                    v_parts[at].at[index + (pl.ds(96, 16),)], small.at[pl.ds(16 * n, 16)], sems.at[2]
                )
            )
    for copy in copies:
        copy.start()
    core = info[5]
    x_out[pl.ds(aligned(core, 256), 256), :] = own[core]
    x_out[pl.ds(aligned(1 - core, 256), 256), :] = other[core]
    scale = column_validity(info) * info[4].astype(F32)
    pair_wait = pltpu.make_async_copy(wq, wq, sems.at[0])
    pair_wait.wait()
    pair_wait.wait()

    def project(w, out):
        @pl.loop(0, 3)
        def _(step):
            at = pl.ds(aligned(step, 256), 256)
            out[:, at] = dot(x_out[...], w[:, at]).astype(BF16)

    project(wq, q_out)
    project(wk, k_out)
    wait_whole(wv, sems.at[1])

    @pl.loop(0, 3)
    def _(step):
        at = pl.ds(aligned(step, 256), 256)
        values = dot(x_out[...], wv[:, at]).astype(BF16)
        v_out[:, at] = values
        pooled = (values.astype(F32) * scale).astype(BF16)
        coef_out[:, at] = dot(ridge[...], pooled).astype(BF16)

    if near:
        wait_whole(small, sems.at[2])
        gauss_mask, scale_mask = small_masks(info, table_v, layout)
        rows = small[:, :256]

        def collect(at, mask):
            return jnp.sum(jnp.where(mask, dot(rows, small_places(layout, at, 256)), 0.0), axis=0, keepdims=True)

        means, variances = collect(0, gauss_mask), collect(1, gauss_mask)
        gain_out[...] = collect(2, scale_mask)
        bias_out[...] = collect(3, scale_mask)
        row = lax.broadcasted_iota(jnp.int32, (16, 128), 0)
        for p in range(PAIRS):
            at = slice(128 * p, 128 * (p + 1))
            value = jnp.where(row < 2, means[:, at], variances[:, at])
            for h in range(2):
                value = jnp.where((row % 2 == h) & ~half_lanes(h), 0.0, value)
            gauss_out[p] = jnp.where(row < 4, value, 0.0).astype(BF16)


def density_rows(logits, h):
    mean_logit, var_logit = logits[h : h + 1], logits[2 + h : 3 + h]
    mu = jax.nn.sigmoid(mean_logit)
    softplus = jnp.maximum(var_logit, 0.0) + jnp.log1p(jnp.exp(-jnp.abs(var_logit)))
    return mu, 0.05 * softplus + BASIS_VAR, var_logit


def centre_column():
    return (lax.broadcasted_iota(jnp.int32, (NB, 1), 0).astype(F32) + 0.5) / NB


def half_lanes(h):
    lane = lax.broadcasted_iota(jnp.int32, (1, 128), 1)
    return (lane < DH) if h == 0 else (lane >= DH)


def attend_kernel(info, q, k, v, gauss, attn_t, local_t, dens_t, bias):
    @pl.when(pl.program_id(0) == 0)
    def _():
        key = lax.broadcasted_iota(jnp.int32, (SEGL, SEGL), 0)
        query = lax.broadcasted_iota(jnp.int32, (SEGL, SEGL), 1)
        allowed = ((key < query) & (key < info[3])) | (key == query)
        bias[...] = jnp.where(allowed, 0.0, -1e30)

    values_t = flip(v[...]).astype(BF16)
    logits = dot(gauss[0], q[...], 1, 1)
    centres = centre_column()
    for h in range(2):
        rows = slice(h * DH, (h + 1) * DH)
        keys = jnp.where(half_lanes(h), k[...].astype(F32) * DH**-0.5, 0.0).astype(BF16)
        for block in range(2):
            n = 256 * (block + 1)
            at = slice(256 * block, n)
            scores = dot(keys[:n], q[at], 1, 1) + bias[:n, at]
            exponent = jnp.exp(scores - jnp.max(scores, axis=0, keepdims=True))
            total = jnp.sum(exponent, axis=0, keepdims=True)
            probs = (exponent * (1.0 / total)).astype(BF16)
            attn_t[h, :n, at] = probs
            local_t[rows, at] = dot(values_t[rows, :n], probs)
        mu, spread, _ = density_rows(logits, h)
        offset = mu - centres
        dens_t[h] = (
            jnp.sqrt(BASIS_VAR / spread) * jnp.exp(offset * offset * (-0.5 / spread))
        ).astype(BF16)


def layer_stats(residual):
    mean = jnp.mean(residual, axis=-1, keepdims=True)
    centred = residual - mean
    return centred, lax.rsqrt(jnp.mean(centred * centred, axis=-1, keepdims=True) + 1e-05)


def recall_kernel(table, info, dens_t, coef, local_t, x, gain, bias, *refs):
    parts = refs[0:4]
    heads_out, residual, normed = refs[4:7]
    w_out, sem = refs[7:]
    step = pl.program_id(0)

    @pl.when(step == 0)
    def _():
        for copy in narrow_copies(info, table, parts, [(48, w_out)], sem):
            copy.start()

    coef_t = flip(coef[...]).astype(BF16)
    recalled = [dot(coef_t[h * DH : (h + 1) * DH], dens_t[h]) for h in range(2)]
    both = local_t[...] + jnp.concatenate(recalled, axis=0)
    heads_out[:, pl.ds(aligned(step, 128), 128)] = flip(both).astype(BF16)

    @pl.when(step == PAIRS - 1)
    def _():
        wait_whole(w_out, sem)

        @pl.loop(0, 3)
        def _(chunk):
            at = pl.ds(aligned(chunk, 256), 256)
            residual[:, at] = x[:, at].astype(F32) + dot(heads_out[...], w_out[at, :], 1, 1)

        centred, scale = layer_stats(residual[...])
        normed[...] = (centred * scale * gain[...] + bias[...]).astype(BF16)


def gelu_parts(pre):
    c0, c1 = 0.7978845608028654, 0.044715
    square = pre * pre
    inner = jnp.tanh(c0 * pre * (1.0 + c1 * square))
    half = 0.5 * (1.0 + inner)
    slope = half + 0.5 * pre * (1.0 - inner * inner) * (c0 * (1.0 + 3.0 * c1 * square))
    return pre * half, slope


def wide_out(info, order, keep, source, sems):
    for index, r, kx, _ in scatter_table(order, 1):
        rows = pl.ds(aligned(info[0] ^ r, 96), 96)
        yield kx, pltpu.make_async_copy(
            source.at[rows, pl.ds(kx * D, D)], keep[index[0]].at[index[1:]], sems.at[kx]
        )


def wait_out(source, sems):
    for j in range(2):
        wait_wide(source, sems, j)


def up_kernel(table, order, info, own, other, seed_in, *refs):
    parts = refs[0:4]
    hidden_out, slope_out = refs[4:6]
    keep = refs[6:8]
    w_up, grad, hidden, slope, seed_t, sems, out_sems, side_sems = refs[8:]
    seed_copy = pltpu.make_async_copy(seed_in, seed_t, side_sems.at[2])
    seed_copy.start()
    for copy in wide_copies(info, table, parts, w_up, sems):
        copy.start()
    outs = list(wide_out(info, order, keep, grad, out_sems))
    seed_copy.wait()
    for j in range(2):
        wait_wide(w_up, sems, j)

        @pl.loop(0, 3)
        def _(chunk):
            at = pl.ds(pl.multiple_of(j * D + chunk * 256, 256), 256)
            sums = []
            for half, source in enumerate((own, other)):
                value, derivative = gelu_parts(dot(source[...], w_up[:, at]))
                value = value.astype(BF16)
                hidden[half, :, at] = value
                slope[half, :, at] = derivative.astype(BF16)
                sums.append(dot(seed_t[:, half * SEGL : (half + 1) * SEGL], value))
            grad[:, at] = (sums[0] + sums[1]).astype(BF16)
            for i, (source, target) in enumerate(((hidden, hidden_out), (slope, slope_out))):
                pltpu.make_async_copy(
                    source.at[:, :, at], target.at[:, :, at], side_sems.at[i]
                ).start()

        for owner, copy in outs:
            if owner == j:
                copy.start()
    wait_out(grad, out_sems)
    wait_whole(hidden, side_sems.at[0])
    wait_whole(slope, side_sems.at[1])


def down_kernel(tables, order, info, seed, own, other, slope_in, *refs):
    down_parts, up_parts = refs[0:4], refs[4:8]
    keep = refs[8:10]
    own_grad, other_grad = refs[10:12]
    w_down, w_up, grad, slope, hidden_grad, normed_t = refs[12:18]
    down_sems, up_sems, out_sems, side_sems = refs[18:]
    for copy in wide_copies(info, tables[0], down_parts, w_down, down_sems):
        copy.start()
    for copy in wide_copies(info, tables[1], up_parts, w_up, up_sems):
        copy.start()
    for j in range(2):
        at = pl.ds(j * D, D)
        pltpu.make_async_copy(slope_in.at[:, :, at], slope.at[:, :, at], side_sems.at[j]).start()
    outs = list(wide_out(info, order, keep, grad, out_sems))
    normed_t[:, :SEGL] = flip(own[...]).astype(BF16)
    normed_t[:, SEGL:] = flip(other[...]).astype(BF16)
    for j in range(2):
        wait_wide(w_down, down_sems, j)
        wait_wide(w_up, up_sems, j)
        wait_whole(slope.at[:, :, pl.ds(j * D, D)], side_sems.at[j])

        @pl.loop(0, 3)
        def _(chunk):
            at = pl.ds(pl.multiple_of(j * D + chunk * 256, 256), 256)
            sums = []
            for half in range(2):
                back = dot(seed[half], w_down[:, at]).astype(BF16).astype(F32)
                back = (back * slope[half, :, at].astype(F32)).astype(BF16)
                sums.append(dot(normed_t[:, half * SEGL : (half + 1) * SEGL], back))
                hidden_grad[half, :, at] = back
            grad[:, at] = (sums[0] + sums[1]).astype(BF16)

        for owner, copy in outs:
            if owner == j:
                copy.start()

    @pl.loop(0, 3)
    def _(chunk):
        at = pl.ds(aligned(chunk, 256), 256)
        own_grad[:, at] = dot(hidden_grad[0], w_up[at, :], 1, 1)
        other_grad[:, at] = dot(hidden_grad[1], w_up[at, :], 1, 1).astype(BF16)

    wait_out(grad, out_sems)


def mix_back_kernel(table, order, info, own, other, seed, residual, gain, heads_out, dens_t, *refs):
    parts = refs[0:4]
    resid_grad, head_grad, coef_grad, gain_grad, bias_grad, keep, send = refs[4:11]
    w_out, grad, mix, mix_t, sem, out_sem = refs[11:]
    step = pl.program_id(0)

    @pl.when(step == 0)
    def _():
        for copy in narrow_copies(info, table, parts, [(48, w_out)], sem):
            copy.start()
        normed_grad = (own[...] + other[...].astype(F32)).astype(BF16).astype(F32)
        centred, scale = layer_stats(residual[...])
        unit = centred * scale
        gain_grad[...] = jnp.sum(normed_grad * unit, axis=0, keepdims=True)
        bias_grad[...] = jnp.sum(normed_grad, axis=0, keepdims=True)
        back = normed_grad * gain[...]
        back = back - jnp.mean(back, axis=-1, keepdims=True) - unit * jnp.mean(
            back * unit, axis=-1, keepdims=True
        )
        back = seed[0].astype(F32) + scale * back
        resid_grad[...] = back
        mix[...] = back.astype(BF16)
        mix_t[...] = flip(mix[...]).astype(BF16)
        wait_whole(w_out, sem)

        @pl.loop(0, 3)
        def _(chunk):
            at = pl.ds(aligned(chunk, 256), 256)
            head_grad[:, at] = dot(mix[...], w_out[:, at]).astype(BF16)
            grad[:, at] = dot(mix_t[...], heads_out[:, at]).astype(BF16)

        for copy in out_narrow(info, order, keep, send, [(0, grad)], out_sem):
            copy.start()

    pair_grad = head_grad[:, pl.ds(aligned(step, 128), 128)].astype(F32)
    sums = [
        dot(dens_t[h], jnp.where(half_lanes(h), pair_grad, 0.0).astype(BF16)) for h in range(2)
    ]
    coef_grad[...] = (sums[0] + sums[1]).astype(BF16)

    @pl.when(step == PAIRS - 1)
    def _():
        wait_whole(grad, out_sem)


def attend_back_kernel(
    attn_t, q, k, v, grad, local_t, dens_t, coef, gauss, *refs
):
    dq_out, dk_out, dv_out, gauss_grad, dq_t, dk_sum, dv_sum, rows_of = refs
    keys_t = flip(k[...]).astype(BF16)
    grad_t = flip(grad[...])
    logits = dot(gauss[0], q[...], 1, 1)
    centres = centre_column()
    gauss_columns = flip(gauss[0])
    dk_sum[...] = jnp.zeros_like(dk_sum)
    dv_sum[...] = jnp.zeros_like(dv_sum)
    rows_of[...] = jnp.zeros_like(rows_of)
    only = lambda h, value: jnp.where(half_lanes(h), value.astype(F32), 0.0).astype(BF16)
    for h in range(2):
        rows = slice(h * DH, (h + 1) * DH)
        values, queries, grads = only(h, v[...]), only(h, q[...]), only(h, grad[...])
        delta = jnp.sum(grad_t[rows] * local_t[rows], axis=0, keepdims=True)
        for block in range(2):
            n = 256 * (block + 1)
            at = slice(256 * block, n)
            probs = attn_t[h, :n, at]
            prob_grad = dot(values[:n], grad[at], 1, 1)
            score_grad = (probs.astype(F32) * (prob_grad - delta[:, at])).astype(BF16)
            dv_sum[:n] += dot(probs, grads[at])
            dk_sum[:n] += dot(score_grad, queries[at])
            dq_t[rows, at] = dot(keys_t[rows, :n], score_grad) * DH**-0.5
        mu, spread, var_logit = density_rows(logits, h)
        inverse = 1.0 / spread
        offset = mu - centres
        weighted = dot(only(h, coef[...]), grad[...], 1, 1) * dens_t[h].astype(F32)
        first = weighted * offset
        sum0 = jnp.sum(weighted, axis=0, keepdims=True)
        sum1 = jnp.sum(first, axis=0, keepdims=True)
        sum2 = jnp.sum(first * offset, axis=0, keepdims=True)
        mean_grad = -sum1 * inverse * mu * (1.0 - mu)
        spread_grad = 0.5 * inverse * (sum2 * inverse - sum0)
        var_grad = spread_grad * 0.05 * jax.nn.sigmoid(var_logit)
        rows_of[h : h + 1] = mean_grad
        rows_of[2 + h : 3 + h] = var_grad
        column = gauss_columns[rows]
        dq_t[rows] += column[:, h : h + 1] * mean_grad + column[:, 2 + h : 3 + h] * var_grad
    dq_out[...] = jnp.transpose(dq_t[...]).astype(BF16)
    dk_out[...] = (dk_sum[...] * DH**-0.5).astype(BF16)
    dv_out[...] = dv_sum[...]
    high = rows_of[...].astype(BF16)
    both = dot(high, q[...]) + dot((rows_of[...] - high.astype(F32)).astype(BF16), q[...])
    gauss_grad[0:1] = jnp.where(half_lanes(0), both[0:1], both[1:2])
    gauss_grad[1:2] = jnp.where(half_lanes(0), both[2:3], both[3:4])


def qkv_grad_kernel(orders, near, info, x, dq, dk, dv, coef_grad, ridge_t, *refs):
    if near:
        gauss_grad, gain_grad, bias_grad = refs[:3]
        layout = refs[3][...]
        refs = refs[4:]
    keep_qk, send_qk, keep_v, send_v, dv_out, x_t, gq, gk, gv, small, sems = refs
    x_t[...] = flip(x[...]).astype(BF16)
    scale = column_validity(info) * info[4].astype(F32)

    def weight(source, out):
        @pl.loop(0, 3)
        def _(chunk):
            at = pl.ds(aligned(chunk, 256), 256)
            out[:, at] = dot(x_t[...], source[:, at]).astype(BF16)

    weight(dq, gq)
    weight(dk, gk)
    for copy in out_narrow(info, orders[0], keep_qk, send_qk, [(0, gq), (48, gk)], sems.at[0]):
        copy.start()

    @pl.loop(0, 3)
    def _(chunk):
        at = pl.ds(aligned(chunk, 256), 256)
        pooled_grad = dot(ridge_t[...], coef_grad[:, at])
        dv_out[:, at] = (dv[:, at] + pooled_grad * scale).astype(BF16)
        gv[:, at] = dot(x_t[...], dv_out[:, at]).astype(BF16)

    for copy in out_narrow(info, orders[1], keep_v, send_v, [(0, gv)], sems.at[1]):
        copy.start()
    if near:
        table = scatter_table(orders[1])
        gauss_mask, scale_mask = small_masks(info, [(0,) + row for row in table], layout)
        rows = (
            (gauss_mask, gauss_grad[0:1]),
            (gauss_mask, gauss_grad[1:2]),
            (scale_mask, gain_grad[...]),
            (scale_mask, bias_grad[...]),
        )
        small[...] = jnp.zeros_like(small)
        small[:, :128] = sum(
            dot(jnp.where(mask, row, 0.0).astype(BF16), small_places(layout, i, 128), 1, 1)
            for i, (mask, row) in enumerate(rows)
        ).astype(BF16)
        for n, (index, _, _, kc) in enumerate(table):
            pltpu.make_async_copy(
                small.at[pl.ds(16 * n, 16)],
                (keep_v, send_v)[kc].at[index + (pl.ds(48, 16),)],
                sems.at[2],
            ).start()
        wait_whole(small, sems.at[2])
    both = pltpu.make_async_copy(gq, gq, sems.at[0])
    both.wait()
    both.wait()
    wait_whole(gv, sems.at[1])


def finish_kernel(tables, info, dq, dk, dv, resid_grad, hidden, residual, *refs):
    qk, v_parts, down_parts = refs[0:4], refs[4:8], refs[8:12]
    token_keep, token_send, fed_keep, fed_send = refs[12:16]
    wq, wk, wv, w_down, sems, down_sems = refs[16:]
    for copy in narrow_copies(info, tables[0], qk, [(0, wq), (48, wk)], sems.at[0]):
        copy.start()
    for copy in narrow_copies(info, tables[1], v_parts, [(0, wv)], sems.at[1]):
        copy.start()
    for copy in wide_copies(info, tables[2], down_parts, w_down, down_sems):
        copy.start()
    first = info[5] == 0

    def split(value):
        top, bottom = value[:HALF_SEG], value[HALF_SEG:]
        return jnp.where(first, top, bottom), jnp.where(first, bottom, top).astype(BF16)

    pair_wait = pltpu.make_async_copy(wq, wq, sems.at[0])
    pair_wait.wait()
    pair_wait.wait()
    wait_whole(wv, sems.at[1])

    @pl.loop(0, 3)
    def _(chunk):
        at = pl.ds(aligned(chunk, 256), 256)
        part = dot(dq[...], wq[at, :], 1, 1) + dot(dk[...], wk[at, :], 1, 1)
        value = resid_grad[:, at] + part + dot(dv[...], wv[at, :], 1, 1)
        token_keep[:, at], token_send[:, at] = split(value)

    wait_out(w_down, down_sems)

    @pl.loop(0, 3)
    def _(chunk):
        at = pl.ds(aligned(chunk, 256), 256)
        value = residual[:, at] + dot(hidden[0], w_down[at, :], 1, 1)
        fed_keep[0, :, at], fed_send[0, :, at] = split(value)
        value = dot(hidden[1], w_down[at, :], 1, 1)
        fed_keep[1, :, at], fed_send[1, :, at] = split(value)


FULL = pl.BlockSpec()
ANY = pl.BlockSpec(memory_space=pl.ANY)
FREE = pl.BlockSpec((SEGL, D), lambda: (0, 0))
FREE_ROWS = pl.BlockSpec((SEGL, D), lambda p: (0, 0))
SCALARS = pl.BlockSpec(memory_space=SMEM)
MATRIX = (D, D)
HALF = FF // 2
HALF_SEG = SEGL // 2
WIDE = (D, HALF)
DMA = pltpu.SemaphoreType.DMA


def shape(dims, dtype=BF16):
    return jax.ShapeDtypeStruct(dims, dtype)


def run(body, name, args, in_specs, outs, out_specs, scratch=(), grid=None, cost=5.0, vmem=48):
    kwargs = {} if grid is None else {"grid": grid}
    args = [
        value
        if any(spec is free for free in (SCALARS, FREE, FREE_ROWS))
        else pltpu.with_memory_space_constraint(value, pltpu.HBM)
        for value, spec in zip(args, in_specs)
    ]
    return pl.pallas_call(
        body,
        name=name,
        out_shape=tuple(pltpu.HBM(out.shape, out.dtype) for out in outs),
        in_specs=list(in_specs),
        out_specs=tuple(out_specs),
        scratch_shapes=list(scratch),
        cost_estimate=pl.CostEstimate(
            flops=int(cost * 2e8), bytes_accessed=int(1e6), transcendentals=0
        ),
        compiler_params=pltpu.CompilerParams(vmem_limit_bytes=vmem * 1024 * 1024),
        **kwargs,
    )(*args)


PAIR_COLUMNS = pl.BlockSpec((SEGL, 128), lambda p: (0, p))
PAIR_ROWS = pl.BlockSpec((128, SEGL), lambda p: (p, 0))
PAIR_COEF = pl.BlockSpec((NB, 128), lambda p: (0, p))
PAIR_ATTN = pl.BlockSpec((2, SEGL, SEGL), lambda p: (p, 0, 0))
PAIR_DENS = pl.BlockSpec((2, NB, SEGL), lambda p: (p, 0, 0))


def pair_block(*dims):
    return pl.BlockSpec((1,) + dims, lambda p: (p, 0, 0))


ORDER_QK, ORDER_V = "zyx", "zxy"
BACK_QK, BACK_V, BACK_UP, BACK_DOWN = "xyz", "yxz", "yxz", "xyz"


def local(
    tokens, lengths, mem_mask, cotangent, w_qkv, w_gauss, w_out, ln_gain, ln_bias, w_up, w_down
):
    dp_count = lax.axis_size("dp")
    dp, rank = lax.axis_index("dp"), lax.axis_index("tensor")
    core, segment = rank % 2, rank // 2
    near = dp_count == 8
    gauss_size, gain_size = w_gauss.size, ln_gain.size
    ridge = ridge_matrix()

    used = [
        jnp.clip(lax.dynamic_index_in_dim(lengths, at, 0, False) - segment * SEGL, 0, SEGL)
        for at in (core, 1 - core)
    ]
    pair = lax.dynamic_index_in_dim(mem_mask, core, 0, False)[1, 0]
    where = (dp, segment, core) if near else (0, 0, 0)
    info = jnp.stack([jnp.asarray(value, jnp.int32) for value in where + (used[0], pair, core)])

    their_tokens = swap(tokens)
    theirs = swap(cotangent)
    everything = jnp.where(
        core == 0,
        jnp.concatenate([cotangent, theirs], axis=1),
        jnp.concatenate([theirs, cotangent], axis=1),
    )
    seed = jnp.stack(
        [lax.dynamic_index_in_dim(everything, at, 0, False) for at in (core, 1 - core)]
    )
    seed = jnp.stack(
        [
            jnp.where(jnp.arange(SEGL)[:, None] < count, part, 0.0).astype(BF16)
            for count, part in zip(used, seed)
        ]
    )
    seed_t = seed.reshape(2 * SEGL, D).T

    projections = jnp.concatenate([w_qkv, w_out.T[None]])
    if near:
        mine = lax.dynamic_slice_in_dim(projections, core * 48, 48, axis=1)
        partner = swap(lax.dynamic_slice_in_dim(projections, (1 - core) * 48, 48, axis=1))
        projections = jnp.where(
            core == 0,
            jnp.concatenate([mine, partner], axis=2),
            jnp.concatenate([partner, mine], axis=2),
        )
        small = jnp.concatenate(
            [w_gauss.reshape(-1)] + exact_triple(jnp.concatenate([ln_gain, ln_bias]))
        )
        small_rows = jnp.pad(small[None], ((0, 15), (0, 384 - small.size)))
        packed = jnp.concatenate([projections.reshape(192, 384), small_rows])
        along_z = spread(after(packed, their_tokens, theirs), "z")
        along_z[1] = after(along_z[1], seed, seed_t, info)
        qk_near = jnp.stack(spread(jnp.stack([part[:96] for part in along_z]), "y"))
        v_near = jnp.stack(spread(jnp.stack([part[96:] for part in along_z]), "x"))
        qk_far, v_far = xor_permute(qk_near, "x", 1), xor_permute(v_near, "y", 1)
        qk_swap, v_swap = swap(qk_near), swap(v_near)
        up_z = spread(after(w_up, qk_swap, v_swap), "z")
        qk_parts = [qk_near, qk_far, qk_swap, swap(after(qk_far, *up_z[1:]))]
        v_parts = [v_near, v_far, v_swap, swap(after(v_far, *up_z[1:]))]
        up_z = after(jnp.stack(up_z), qk_parts[3], v_parts[3])
        up_x, up_y = xor_permute(up_z, "x", 1), xor_permute(up_z, "y", 1)
        down_z = spread(after(w_down.T, qk_parts[3], v_parts[3]), "z")
    else:
        every = lambda value: lax.all_gather(value, AXES, axis=0)
        cut = lambda value: value.reshape((8, dp_count // 8) + value.shape[1:])
        both = cut(every(projections).reshape(dp_count, 4, 4, -1, 192))
        both = both.transpose(0, 3, 1, 4, 2, 5).reshape(8, 4, 2, 48, 2, 384)
        both = both.transpose(0, 4, 2, 1, 3, 5)
        qk_parts = as_gathered(both[:, :, :, :2].reshape(8, 2, 2, 96, 384), ORDER_QK)
        v_parts = as_gathered(
            jnp.pad(both[:, :, :, 2:].reshape(8, 2, 2, 96, 384), ((0, 0),) * 3 + ((0, 16), (0, 0))),
            ORDER_V,
        )

        def wide(value):
            value = cut(every(value).reshape(dp_count, 4, -1, D)).transpose(0, 2, 1, 3, 4)
            value = value.reshape(8, 2, 2, 96, D)
            return lax.dynamic_slice_in_dim(value, core, 1, axis=2)

        def in_parts(whole):
            whole = whole.reshape((4, 2, 2) + whole.shape[3:])
            return [whole[:, ky, kx] for ky in range(2) for kx in range(2)]

        up_parts, down_parts = in_parts(wide(w_up)), in_parts(wide(w_down.T))
    table_qk, table_v = piece_table(ORDER_QK), piece_table(ORDER_V)
    table_wide = wide_table()

    tall = shape((SEGL, D))
    row = shape((1, D), F32)
    small_in, small_out = [], []
    if near:
        small_in = [jnp.asarray(small_layout())]
        small_out = [shape((PAIRS, 16, 128)), row, row]
    x, q, k, v, coef, *small_params = run(
        functools.partial(qkv_kernel, table_qk, table_v, near),
        "qkv",
        [info, tokens, their_tokens, jnp.asarray(ridge)] + qk_parts + v_parts + small_in,
        [SCALARS, FULL, FULL, FULL] + [ANY] * 8 + [FULL] * len(small_in),
        [tall] * 4 + [shape((NB, D))] + small_out,
        [FULL] * (5 + len(small_out)),
        [VMEM(MATRIX, BF16)] * 3 + [VMEM((512, 384), BF16), DMA((3,))],
        cost=6.0,
        vmem=24,
    )
    coef = lax.ppermute(coef, "tensor", [(0, 2), (1, 3)])

    q_late = q
    if near:
        q_late = after(q, up_x, up_y)
        up_parts = [up_z, up_x, up_y, xor_permute(after(up_x, q), "y", 1)]
        gauss_rows, norm_gain, norm_bias = small_params
    else:
        scales = every(jnp.stack([ln_gain, ln_bias]))
        gauss_parts = every(w_gauss.reshape(-1))
        norm_gain, norm_bias = scales[:, 0].reshape(1, D), scales[:, 1].reshape(1, D)
        gauss = gauss_parts.reshape(dp_count, 4, 2, 3, -1).transpose(2, 1, 3, 0, 4)
        gauss = gauss.reshape(2, PAIRS, 2, DH)
        spread_rows = jnp.eye(2, dtype=BF16)[None, None, :, :, None] * gauss[:, :, :, None, :]
        gauss_rows = spread_rows.transpose(1, 0, 2, 3, 4).reshape(PAIRS, 4, 128)
        gauss_rows = jnp.pad(gauss_rows, ((0, 0), (0, 12), (0, 0)))

    attn_t, local_t, dens_t = run(
        attend_kernel,
        "attend",
        [info, q_late, k, v, gauss_rows],
        [SCALARS] + [PAIR_COLUMNS] * 3 + [pair_block(16, 128)],
        [shape((H, SEGL, SEGL)), shape((D, SEGL), F32), shape((H, NB, SEGL))],
        [PAIR_ATTN, PAIR_ROWS, PAIR_DENS],
        [VMEM((SEGL, SEGL), F32)],
        grid=(PAIRS,),
        cost=12.0,
        vmem=14,
    )
    if near:
        down_z[1:] = lax.optimization_barrier((attn_t, coef, up_parts[3], *down_z[1:]))[3:]
        down_z = jnp.stack(down_z)
        down_x, down_y = xor_permute(down_z, "x", 1), xor_permute(down_z, "y", 1)
    whole = lambda *dims: pl.BlockSpec(dims, lambda p: (0,) * len(dims))
    heads_out, residual, normed = run(
        functools.partial(recall_kernel, table_v),
        "recall",
        [info, dens_t, coef, local_t, x, norm_gain, norm_bias] + v_parts,
        [SCALARS, PAIR_DENS, PAIR_COEF, PAIR_ROWS, whole(SEGL, D), whole(1, D), whole(1, D)]
        + [ANY] * 4,
        [tall, shape((SEGL, D), F32), tall],
        [whole(SEGL, D)] * 3,
        [VMEM(MATRIX, BF16), DMA(())],
        grid=(PAIRS,),
        cost=7.0,
        vmem=18,
    )
    if near:
        down_parts = [down_z, down_x, down_y, xor_permute(after(down_x, down_y, normed), "y", 1)]
    normed_other = swap(normed)
    piece_dims = lambda order: tuple(SIZES[letter] for letter in order)
    hidden, slope, *keep_down = run(
        functools.partial(up_kernel, table_wide, BACK_DOWN),
        "up",
        [info, normed, normed_other, seed_t] + up_parts,
        [SCALARS, FULL, FREE, ANY] + [ANY] * 4,
        [shape((2, SEGL, HALF))] * 2 + [shape(piece_dims(BACK_DOWN)[1:] + (96, D))] * 2,
        [ANY] * 4,
        [VMEM(WIDE, BF16)] * 2
        + [VMEM((2, SEGL, HALF), BF16)] * 2
        + [VMEM((D, 2 * SEGL), BF16)]
        + [DMA((2,))] * 2
        + [DMA((3,))],
        cost=12.0,
        vmem=22,
    )
    if near:
        down_1 = stage(lambda k: keep_down[k], BACK_DOWN[0])
    *keep_up, own_grad, other_grad = run(
        functools.partial(down_kernel, (table_wide, table_wide), BACK_UP),
        "down",
        [info, seed, normed, normed_other, slope] + down_parts + up_parts,
        [SCALARS] + [FULL] * 2 + [FREE] + [ANY] * 9,
        [shape(piece_dims(BACK_UP)[1:] + (96, D))] * 2 + [shape((SEGL, D), F32), tall],
        [ANY] * 2 + [FULL] * 2,
        [VMEM(WIDE, BF16)] * 3
        + [VMEM((2, SEGL, HALF), BF16)] * 2
        + [VMEM((D, 2 * SEGL), BF16)]
        + [DMA((2,))] * 4,
        cost=15.0,
        vmem=30,
    )
    if near:
        up_1 = stage(lambda k: keep_up[k], BACK_UP[0])
    other_grad = swap(other_grad)
    narrow_grad = [shape(piece_dims(BACK_V) + (48, 384))] * 2
    resid_grad, head_grad, coef_grad, gain_part, bias_part, keep_out, send_out = run(
        functools.partial(mix_back_kernel, table_v, BACK_V),
        "mix_back",
        [info, own_grad, other_grad, seed, residual, norm_gain, heads_out, dens_t] + v_parts,
        [SCALARS]
        + [whole(SEGL, D), FREE_ROWS, pl.BlockSpec((1, SEGL, D), lambda p: (0, 0, 0))]
        + [whole(SEGL, D), whole(1, D), whole(SEGL, D), PAIR_DENS]
        + [ANY] * 4,
        [shape((SEGL, D), F32), tall, shape((NB, D)), row, row] + narrow_grad,
        [whole(SEGL, D), whole(SEGL, D), PAIR_COEF, whole(1, D), whole(1, D)] + [ANY] * 2,
        [VMEM(MATRIX, BF16)] * 2
        + [VMEM((SEGL, D), BF16), VMEM((D, SEGL), BF16)]
        + [DMA(())] * 2,
        grid=(PAIRS,),
        cost=6.0,
        vmem=26,
    )
    coef_grad = lax.ppermute(coef_grad if not near else after(coef_grad, *down_1[1]), "tensor", [(2, 0), (3, 1)])
    if near:
        got_out = swap(send_out)
    dq, dk, dv, gauss_grad = run(
        attend_back_kernel,
        "attend_back",
        [attn_t, q, k, v, head_grad, local_t, dens_t, coef, gauss_rows],
        [PAIR_ATTN]
        + [PAIR_COLUMNS] * 4
        + [PAIR_ROWS, PAIR_DENS, PAIR_COEF, pair_block(16, 128)],
        [tall, tall, shape((SEGL, D), F32), shape((2, D), F32)],
        [PAIR_COLUMNS] * 3 + [pl.BlockSpec((2, 128), lambda p: (0, p))],
        [
            VMEM((128, SEGL), F32),
            VMEM((SEGL, 128), F32),
            VMEM((SEGL, 128), F32),
            VMEM((16, SEGL), F32),
        ],
        grid=(PAIRS,),
        cost=16.0,
        vmem=16,
    )
    if near:
        up_1 = (up_1[0], [after(a, dk, coef_grad, got_out) for a in up_1[1]])
        dq = after(dq, *up_1[1])
        down_1 = (down_1[0], [after(a, *up_1[1]) for a in down_1[1]])
        down_2 = stage(combined(*down_1), BACK_DOWN[1])
        up_2 = stage(combined(*up_1), BACK_UP[1])
    keep_qk, send_qk, keep_v, send_v, dv = run(
        functools.partial(qkv_grad_kernel, (BACK_QK, BACK_V), near),
        "qkv_grad",
        [info, x, dq, dk, dv, coef_grad, jnp.asarray(ridge.T)]
        + ([gauss_grad, gain_part, bias_part] + small_in if near else []),
        [SCALARS] + [FULL] * (10 if near else 6),
        [shape(piece_dims(BACK_QK) + (96, 384))] * 2
        + [shape(piece_dims(BACK_V) + (64, 384))] * 2
        + [tall],
        [ANY] * 4 + [FULL],
        [VMEM((D, SEGL), BF16)] + [VMEM(MATRIX, BF16)] * 3 + [VMEM((512, 384), BF16), DMA((3,))],
        cost=6.0,
        vmem=26,
    )

    if near:
        send_qk = after(send_qk, *down_2[1], *up_2[1])
        send_v = after(send_v, *down_2[1], *up_2[1])
        got_qk, got_v = swap(send_qk), swap(send_v)
        first_qk = [keep_qk[k].astype(F32) + got_qk[k].astype(F32) for k in range(2)]
        rest = ((keep_out, got_out), (keep_v, got_v))
        first_v = [
            jnp.concatenate([a[k].astype(F32) + b[k].astype(F32) for a, b in rest], axis=2)
            for k in range(2)
        ]
        first_qk[1], first_v[1] = first_qk[1].astype(BF16), first_v[1].astype(BF16)
        qk_1 = stage(lambda k: first_qk[k], BACK_QK[0])
        v_1 = stage(lambda k: first_v[k], BACK_V[0])
        down_2 = (down_2[0], [after(a, first_qk[1], first_v[1]) for a in down_2[1]])
        to_down, to_up = combined(*down_2), combined(*up_2)
        wide = [jnp.concatenate([to_down(k), to_up(k)]) for k in range(4)]
        wide[1:] = [value.astype(BF16) for value in wide[1:]]
        wide_3 = stage(lambda k: wide[k], "z")
        dq_late = after(dq, first_qk[1], first_v[1], *wide[1:])
    else:
        dq_late = dq

    token_keep, token_send, fed_keep, fed_send = run(
        functools.partial(finish_kernel, (table_qk, table_v, table_wide)),
        "finish",
        [info, dq_late, dk, dv, resid_grad, hidden, residual] + qk_parts + v_parts + down_parts,
        [SCALARS] + [FULL] * 6 + [ANY] * 12,
        [shape((HALF_SEG, D), F32), shape((HALF_SEG, D))]
        + [shape((2, HALF_SEG, D), F32), shape((2, HALF_SEG, D))],
        [FULL] * 4,
        [VMEM(MATRIX, BF16)] * 3 + [VMEM(WIDE, BF16)] + [DMA((2,))] * 2,
        cost=14.0,
        vmem=32,
    )
    if near:
        qk_1 = (qk_1[0], [after(value, token_send) for value in qk_1[1]])
        v_1 = (v_1[0], [after(value, token_send) for value in v_1[1]])
        qk_2 = stage(combined(*qk_1), BACK_QK[1])
        v_2 = stage(combined(*v_1), BACK_V[1])
        token_send = after(token_send, v_1[1][0], qk_1[1][0])
        fed_send = after(fed_send, v_1[1][0], qk_1[1][0])
    token_got, fed_got = swap(token_send).astype(F32), swap(fed_send).astype(F32)
    own_rows, their_rows = fed_keep[0] + fed_got[1], fed_keep[1] + fed_got[0]
    by_sequence = lambda mine, theirs: jnp.where(
        core == 0, jnp.stack([mine, theirs]), jnp.stack([theirs, mine])
    )
    output = by_sequence(own_rows, their_rows)
    grad_tokens = by_sequence(token_keep, token_got)

    if near:
        wide_3 = (wide_3[0], [after(a, *qk_1[1], *v_1[1]) for a in wide_3[1]])
        to_qk, to_v = combined(*qk_2), combined(*v_2)
        last = [jnp.concatenate([to_qk(k), to_v(k)]) for k in range(4)]
        last[1:] = [value.astype(BF16) for value in last[1:]]
        joined, arrived = stage(lambda k: last[k], "z")
        arrived[0] = after(arrived[0], output, grad_tokens)
        joined = final_sum(joined, arrived)
        own_small = joined[192]
        narrow = joined[:192].reshape(4, 48, 384)
        mine = lax.dynamic_slice_in_dim(narrow, core * 192, 192, axis=2)
        partner = swap(lax.dynamic_slice_in_dim(narrow, (1 - core) * 192, 192, axis=2))
        narrow = jnp.where(
            core == 0,
            jnp.concatenate([mine, partner], axis=1),
            jnp.concatenate([partner, mine], axis=1),
        )
        own_wide = final_sum(*wide_3)
        own_up, own_down = own_wide[96:], own_wide[:96].T
    else:
        gauss_grad = gauss_grad.reshape(2, 4, 3, dp_count, -1).transpose(3, 1, 0, 2, 4)
        small_grads = jnp.concatenate(
            [value.reshape(dp_count * 4, -1) for value in (gauss_grad, gain_part, bias_part)],
            axis=1,
        )
        own_small = lax.psum_scatter(small_grads, AXES, scatter_dimension=0)
        pieces = [
            whole_from([keep_qk, send_qk], BACK_QK).reshape(8, 2, 2, 2, 48, 384),
            whole_from([keep_out, send_out], BACK_V)[:, :, :, None],
            whole_from([keep_v, send_v], BACK_V)[:, :, :, None, :48],
        ]
        pieces = jnp.concatenate(pieces, axis=3).transpose(0, 2, 4, 3, 1, 5)
        pieces = pieces.reshape(dp_count, D // dp_count, 4, 4, 192).transpose(0, 3, 2, 1, 4)
        total = lambda value: lax.psum_scatter(value.astype(F32), AXES, scatter_dimension=0)
        narrow = total(pieces.reshape((-1,) + pieces.shape[2:]))

        def owned(keep, order):
            mine = whole_from([jnp.stack(keep)], order)
            both = jnp.concatenate(
                [jnp.where(core == at, mine, jnp.zeros_like(mine)) for at in range(2)], axis=2
            )
            both = both.transpose(0, 3, 1, 2, 4).reshape(dp_count, D // dp_count, 4, D)
            both = both.transpose(0, 2, 1, 3)
            return total(both.reshape((-1,) + both.shape[2:]))

        own_up, own_down = owned(keep_up, BACK_UP), owned(keep_down, BACK_DOWN).T
    own_qkv, own_out = jnp.concatenate([narrow[:2], narrow[3:]]), narrow[2].T
    return (
        output,
        grad_tokens,
        own_qkv,
        own_small[:gauss_size].reshape(w_gauss.shape),
        own_out,
        own_small[gauss_size : gauss_size + gain_size],
        own_small[gauss_size + gain_size : gauss_size + 2 * gain_size],
        own_up,
        own_down,
    )


def solution(mesh):
    return jax.shard_map(
        local,
        mesh=mesh,
        in_specs=(
            P("dp", "tensor", None),
            P("dp"),
            P("dp", None, None),
            P("dp", "tensor", None),
            P(None, "dp", "tensor"),
            P(None, "tensor", "dp"),
            P("tensor", "dp"),
            P(("dp", "tensor")),
            P(("dp", "tensor")),
            P("dp", "tensor"),
            P("tensor", "dp"),
        ),
        out_specs=(
            P("dp", "tensor", None),
            P("dp", "tensor", None),
            P(None, "dp", "tensor"),
            P(None, "tensor", "dp"),
            P("tensor", "dp"),
            P(("dp", "tensor")),
            P(("dp", "tensor")),
            P("dp", "tensor"),
            P("tensor", "dp"),
        ),
        check_vma=False,
    )
```
